32 devices in a mesh: region: 16 (over z, x, core), event: 2 (over y).
Axes of the slice: x: 2, y: 2, z: 4, core: 2. Of those that a mesh axis runs over, the one named last changes fastest.
Arguments:
- forward_field: float32 [2, 3, 128, 9, 128], P('event', None, 'region'), may hold values from -6 to 6
- forward_speed: float32 [2, 3, 128, 9, 128], P('event', None, 'region'), may hold values from -6 to 6
- adjoint_field: float32 [2, 3, 128, 9, 128], P('event', None, 'region'), may hold values from -6 to 6
- adjoint_speed: float32 [2, 3, 128, 9, 128], P('event', None, 'region'), may hold values from -6 to 6
- adjoint_source: float32 [2, 3, 128, 9, 128], P('event', None, 'region'), may hold values from -6 to 6
- lame_lambda: float32 [128, 9, 128], P('region'), may hold values from 0.5 to 2
- lame_mu: float32 [128, 9, 128], P('region'), may hold values from 0.3 to 1.2
- density: float32 [128, 9, 128], P('region'), may hold values from 0.8 to 2.4
Outputs:
- forward_out: float32 [2, 3, 128, 9, 128], P('event', None, 'region')
- forward_speed_out: float32 [2, 3, 128, 9, 128], P('event', None, 'region')
- adjoint_out: float32 [2, 3, 128, 9, 128], P('event', None, 'region')
- adjoint_speed_out: float32 [2, 3, 128, 9, 128], P('event', None, 'region')
- kernels: float32 [2, 128, 9, 128], P(None, ('region', 'event'))
The draws below stay inside these ranges and needn't reach their ends.
All inputs are finite; a program needn't handle non-finite values.
Results may differ from the reference program's by a relative error of at most 0.0003.
Values sent between devices are 32-bit elements; how exact they have to be, the bound alone decides.
A program may use at most 64 MiB of HBM per device.

```python
import math
import jax
import jax.numpy as jnp
import numpy as np
from jax import lax

STEPS = 2
EVENTS = 2
NXG = 128
NY = 128
NZ = 9


def steps_of(key, extent, pieces, least, high):
    loudness, own = 1.0, jax.random.fold_in(key, 6)
    for dim, shards_of in pieces:
        draws = jnp.exp(jax.random.uniform(jax.random.fold_in(own, dim), (shards_of,), jnp.float32, least / len(pieces), high / len(pieces)))
        loudness = loudness * jnp.repeat(draws, extent[dim] // shards_of).reshape([-1 if axis == dim else 1 for axis in range(len(extent))])
    return loudness


def centred(own_key, shape, deviation, limit, cuts=(), kind=jnp.bfloat16):
    level = steps_of(own_key, shape, cuts, -0.22, 0.18) if cuts else 1.0
    drawn = jax.random.normal(own_key, shape, jnp.float32) * deviation * level
    return jnp.minimum(jnp.maximum(drawn, -limit), limit).astype(kind)


def setup_inputs(seed: int = 0) -> dict:
    splits = jax.random.split(jax.random.key(seed), 9)
    forward_field = centred(splits[0], (EVENTS, 3, NXG, NZ, NY), 1.0, 6.0, ((0, 2), (2, 16)), jnp.float32)
    forward_speed = centred(splits[1], (EVENTS, 3, NXG, NZ, NY), 1.0, 6.0, ((0, 2), (2, 16)), jnp.float32)
    adjoint_field = centred(splits[2], (EVENTS, 3, NXG, NZ, NY), 1.0, 6.0, ((0, 2), (2, 16)), jnp.float32)
    adjoint_speed = centred(splits[3], (EVENTS, 3, NXG, NZ, NY), 1.0, 6.0, ((0, 2), (2, 16)), jnp.float32)
    adjoint_source = centred(splits[4], (EVENTS, 3, NXG, NZ, NY), 1.0, 6.0, ((0, 2), (2, 16)), jnp.float32)
    lame_lambda = jnp.clip(jnp.exp(math.log(2.0) - 1.3862944 * jax.random.uniform(splits[5], (NXG, NZ, NY), jnp.float32) ** steps_of(splits[5], (NXG, NZ, NY), ((0, 16),), -0.2, 0.2)), 0.5, 2.0)
    lame_mu = jnp.clip(jnp.exp(math.log(1.2) - 1.3862944 * jax.random.uniform(splits[6], (NXG, NZ, NY), jnp.float32) ** steps_of(splits[6], (NXG, NZ, NY), ((0, 16),), -0.2, 0.2)), 0.3, 1.2)
    density = jnp.clip(jnp.exp(math.log(2.4) - 1.0986123 * jax.random.uniform(splits[7], (NXG, NZ, NY), jnp.float32) ** steps_of(splits[7], (NXG, NZ, NY), ((0, 16),), -0.2, 0.2)), 0.8, 2.4)
    return {"forward_field": forward_field, "forward_speed": forward_speed, "adjoint_field": adjoint_field, "adjoint_speed": adjoint_speed, "adjoint_source": adjoint_source, "lame_lambda": lame_lambda, "lame_mu": lame_mu, "density": density}


time_step = 0.02

def gll_tables():
    points = np.array([-1.0, -math.sqrt(3.0 / 7.0), 0.0, math.sqrt(3.0 / 7.0), 1.0])
    weights = np.array([0.1, 49.0 / 90.0, 32.0 / 45.0, 49.0 / 90.0, 0.1])
    legendre = (35.0 * points ** 4 - 30.0 * points ** 2 + 3.0) / 8.0
    derivative = np.zeros((5, 5))
    for target in range(5):
        for column in range(5):
            if target != column:
                derivative[target, column] = legendre[target] / (legendre[column] * (points[target] - points[column]))
    derivative[0, 0] = -5.0
    derivative[4, 4] = 5.0
    return (jnp.asarray(derivative, jnp.float32), jnp.asarray(weights, jnp.float32))

def expand_axis(nodes, axis):
    moved = jnp.moveaxis(nodes, axis, 0)
    planes = (moved.shape[0] - 1) // 4
    trailing = moved.shape[1:]
    leading = moved[:4 * planes].reshape((planes, 4) + trailing)
    closing = moved[4:4 * planes + 1:4].reshape((planes, 1) + trailing)
    joined = jnp.concatenate([leading, closing], axis=1)
    return jnp.moveaxis(joined, (0, 1), (axis, axis + 1))

def collapse_axis(values, axis):
    moved = jnp.moveaxis(values, (axis, axis + 1), (0, 1))
    planes = moved.shape[0]
    trailing = moved.shape[2:]
    leading = moved[:, :4].reshape((4 * planes,) + trailing)
    padding = jnp.zeros((planes, 3) + trailing, moved.dtype)
    shifted = jnp.concatenate([moved[:, 4:5], padding], axis=1).reshape((4 * planes,) + trailing)
    upper = jnp.concatenate([leading, jnp.zeros((1,) + trailing, moved.dtype)], axis=0)
    lower = jnp.concatenate([jnp.zeros((4,) + trailing, moved.dtype), shifted[:4 * planes - 3]], axis=0)
    return jnp.moveaxis(upper + lower, 0, axis)

def to_elements(nodes, first):
    for offset in (0, 2, 4):
        nodes = expand_axis(nodes, first + offset)
    return nodes

def to_nodes(values, first):
    for offset in (4, 2, 0):
        values = collapse_axis(values, first + offset)
    return values

def element_work(forward_nodes, adjoint_nodes, lambda_nodes, mu_nodes):
    derivative, weights = gll_tables()
    quadrature = weights[None, :, None, None, None, None] * weights[None, None, None, :, None, None] * weights[None, None, None, None, None, :]
    lambda_values = to_elements(lambda_nodes, 0)
    mu_values = to_elements(mu_nodes, 0)
    highest = lax.Precision.HIGHEST
    forms = ('pi,xpyjzk->xiyjzk', 'pj,xiypzk->xiyjzk', 'pk,xiyjzp->xiyjzk')

    def strains(nodes):
        values = to_elements(nodes, 1)
        grads = (jnp.einsum('pi,cxiyjzk->cxpyjzk', derivative, values, precision=highest), jnp.einsum('pj,cxiyjzk->cxiypzk', derivative, values, precision=highest), jnp.einsum('pk,cxiyjzk->cxiyjzp', derivative, values, precision=highest))
        table = [[0.5 * (grads[source][target] + grads[target][source]) for target in range(3)] for source in range(3)]
        dilation = table[0][0] + table[1][1] + table[2][2]
        return (dilation, table)

    def forces(dilation, table):
        components = []
        for target in range(3):
            total = 0.0
            for source in range(3):
                stress = 2.0 * mu_values * table[source][target]
                if source == target:
                    stress = stress + lambda_values * dilation
                total = total + jnp.einsum(forms[source], derivative, quadrature * stress, precision=highest)
            components.append(total)
        return to_nodes(jnp.stack(components), 1)
    dilation_fwd, table_fwd = strains(forward_nodes)
    dilation_adj, table_adj = strains(adjoint_nodes)
    shear_sum = 0.0
    for source in range(3):
        for target in range(3):
            shear_sum = shear_sum + table_fwd[source][target] * table_adj[source][target]
    increments = jnp.stack([quadrature * dilation_fwd * dilation_adj, 2.0 * quadrature * shear_sum])
    return (forces(dilation_fwd, table_fwd), forces(dilation_adj, table_adj), to_nodes(increments, 1))

def line_weights(count, closed):
    positions = jnp.arange(count) % 4
    values = jnp.where(positions == 0, 0.2, jnp.where(positions == 2, 32.0 / 45.0, 49.0 / 90.0)).astype(jnp.float32)
    if closed:
        values = values.at[0].set(0.1).at[count - 1].set(0.1)
    return values

def mass_of(density):
    return density * line_weights(density.shape[0], False)[:, None, None] * line_weights(density.shape[1], True)[None, :, None] * line_weights(density.shape[2], False)[None, None, :]

def extend_both(nodes):
    with_first = jnp.concatenate([nodes, nodes[:, :1]], axis=1)
    return jnp.concatenate([with_first, with_first[..., :1]], axis=-1)

def extend_model(nodes):
    with_first = jnp.concatenate([nodes, nodes[:1]], axis=0)
    return jnp.concatenate([with_first, with_first[..., :1]], axis=-1)

def wrap_planes(values):
    lateral = values[..., :-1].at[..., 0].add(values[..., -1])
    return lateral[:, :-1].at[:, 0].add(lateral[:, -1])

def reference(forward_field, forward_speed, adjoint_field, adjoint_speed, adjoint_source, lame_lambda, lame_mu, density):
    node_mass = mass_of(density)
    lambda_nodes = extend_model(lame_lambda)
    mu_nodes = extend_model(lame_mu)

    def one_event(items):
        forward_now, forward_rate, adjoint_now, adjoint_rate, source = items
        kernel_total = jnp.zeros((2,) + forward_now.shape[1:], jnp.float32)
        for step_index in range(STEPS):
            forward_force, adjoint_force, increments = element_work(extend_both(forward_now), extend_both(adjoint_now), lambda_nodes, mu_nodes)
            forward_rate = forward_rate - time_step * wrap_planes(forward_force) / node_mass
            forward_now = forward_now + time_step * forward_rate
            adjoint_rate = adjoint_rate + time_step * (source - wrap_planes(adjoint_force)) / node_mass
            adjoint_now = adjoint_now + time_step * adjoint_rate
            kernel_total = kernel_total + wrap_planes(increments)
        return (forward_now, forward_rate, adjoint_now, adjoint_rate, kernel_total)
    results = lax.map(one_event, (forward_field, forward_speed, adjoint_field, adjoint_speed, adjoint_source))
    return (results[0], results[1], results[2], results[3], lax.optimization_barrier(jnp.sum(results[4], axis=0)))
```

```python
import functools
import math

import jax
import jax.numpy as jnp
import numpy as np
from jax import lax
from jax.experimental import pallas as pl
from jax.experimental.pallas import tpu as pltpu
from jax.sharding import PartitionSpec as P

STEPS = 2
time_step = 0.02
MESH = pl.DeviceIdType.MESH


def gll_numbers():
    points = np.array([-1.0, -math.sqrt(3.0 / 7.0), 0.0, math.sqrt(3.0 / 7.0), 1.0])
    weights = np.array([0.1, 49.0 / 90.0, 32.0 / 45.0, 49.0 / 90.0, 0.1])
    legendre = (35.0 * points**4 - 30.0 * points**2 + 3.0) / 8.0
    derivative = np.zeros((5, 5))
    for target in range(5):
        for column in range(5):
            if target != column:
                derivative[target, column] = legendre[target] / (
                    legendre[column] * (points[target] - points[column])
                )
    derivative[0, 0] = -5.0
    derivative[4, 4] = 5.0
    return (derivative, weights)


def lane_tables(lanes):
    numbers, _ = gll_numbers()
    table = np.zeros((lanes, 2 * lanes))
    for lane in range(lanes):
        start, local = lane - lane % 4, lane % 4
        for source in range(5):
            if local:
                table[(start + source) % lanes, lane] += numbers[local, source]
            else:
                right, left = (start + source) % lanes, (start - 4 + source) % lanes
                table[right, lane] += 0.5 * numbers[0, source]
                table[left, lane] += 0.5 * numbers[4, source]
                table[right, lanes + lane] += 0.5 * numbers[0, source]
                table[left, lanes + lane] -= 0.5 * numbers[4, source]
    high = table.astype(np.float32).astype(jnp.bfloat16)
    low = (table - high.astype(np.float64)).astype(np.float32).astype(jnp.bfloat16)
    return (
        np.concatenate([high, high], axis=0),
        low,
        np.concatenate([high.T, low.T], axis=1),
        np.ascontiguousarray(high.T),
    )


def combine(coefficients, pieces):
    total = None
    for number, piece in zip(coefficients, pieces):
        if number != 0.0:
            term = float(number) * piece
            total = term if total is None else total + term
    return total


def turn(value, shift):
    return pltpu.roll(value, shift % 8, value.ndim - 2)


def row_bit(shape, bit):
    return (lax.broadcasted_iota(jnp.int32, shape, len(shape) - 2) & bit) == 0


def swap_rows(four):
    shape = four[0].shape
    low_two, low_one = row_bit(shape, 2), row_bit(shape, 1)
    a0, a1, a2, a3 = four
    b0 = jnp.where(low_two, a0, turn(a2, 2))
    b2 = jnp.where(low_two, turn(a0, -2), a2)
    b1 = jnp.where(low_two, a1, turn(a3, 2))
    b3 = jnp.where(low_two, turn(a1, -2), a3)
    return (
        jnp.where(low_one, b0, turn(b1, 1)),
        jnp.where(low_one, turn(b0, -1), b1),
        jnp.where(low_one, b2, turn(b3, 1)),
        jnp.where(low_one, turn(b2, -1), b3),
    )


def middle_sum(blocks):
    first, last = blocks[..., 0, :, :], blocks[..., 4, :, :]
    low = row_bit(first.shape, 1)
    new_last = last + jnp.where(low, turn(first, -1), 0.0)
    new_first = first + jnp.where(low, 0.0, turn(last, 1))
    return jnp.concatenate(
        [new_first[..., None, :, :], blocks[..., 1:4, :, :], new_last[..., None, :, :]], axis=-3
    )


def pack_half(blocks, low):
    half = (blocks.shape[0] + 1) // 2
    first, second = blocks[:half], blocks[half:]
    if second.shape[0] < half:
        second = jnp.concatenate([second, first[-1:]], axis=0)
    keep = row_bit(first.shape, 4)
    other = turn(second, 4)
    return jnp.where(keep, first, other) if low else jnp.where(keep, other, first)


def unpack_half(packed, count):
    return jnp.concatenate([packed, turn(packed, 4)], axis=0)[:count]


def kernel(
    regions,
    events,
    uf_in,
    vf_in,
    ua_in,
    va_in,
    source_in,
    lam_in,
    mu_in,
    rho_in,
    slope_two_in,
    slope_low_in,
    back_two_in,
    back_high_in,
    uf_out,
    vf_out,
    ua_out,
    va_out,
    k_out,
    u,
    un,
    g,
    b,
    sm,
    im,
    muw,
    lamw,
    gy,
    sx,
    sy,
    f,
    fc,
    h,
    kacc,
    imc,
    muc,
    lamc,
    px,
    mx,
    send_a,
    recv_a,
    send_b,
    recv_b,
    send_m,
    recv_m,
    send_p,
    recv_p,
    send_q,
    recv_q,
    send_k,
    recv_k,
    sems,
    sems_k,
    uf,
    vf,
    ua,
    va,
    source,
    lam,
    mu,
    rho,
    slope_two,
    slope_low,
    back_two,
    back_high,
    load_sems,
):
    numbers, weights = gll_numbers()
    lanes = u.shape[-1]
    region, event = lax.axis_index("region"), lax.axis_index("event")
    left, right = lax.rem(region + regions - 1, regions), lax.rem(region + 1, regions)
    planes = 8 // events
    corner = float(numbers[4, 4])

    barrier = pltpu.get_barrier_semaphore()
    for side in (left, right):
        pl.semaphore_signal(barrier, inc=1, device_id=(side, event), device_id_type=MESH)
    for offset in range(1, events):
        partner = lax.rem(event + offset, events)
        pl.semaphore_signal(barrier, inc=1, device_id=(region, partner), device_id_type=MESH)

    loads = {}
    for number, (name, src, dst) in enumerate(
        (
            ("uf", uf_in, uf),
            ("ua", ua_in, ua),
            ("lam", lam_in, lam),
            ("mu", mu_in, mu),
            ("slope_two", slope_two_in, slope_two),
            ("slope_low", slope_low_in, slope_low),
            ("rho", rho_in, rho),
            ("vf", vf_in, vf),
            ("va", va_in, va),
            ("source", source_in, source),
            ("back_two", back_two_in, back_two),
            ("back_high", back_high_in, back_high),
        )
    ):
        loads[name] = pltpu.make_async_copy(src, dst, load_sems.at[number])
        loads[name].start()

    def ready(*names):
        for name in names:
            loads[name].wait()

    def remote(src, dst, number, target):
        return pltpu.make_async_remote_copy(
            src_ref=src,
            dst_ref=dst,
            send_sem=sems.at[0, number],
            recv_sem=sems.at[1, number],
            device_id=target,
            device_id_type=MESH,
        )

    copy_a = remote(send_a, recv_a, 0, (left, event))
    copy_b = remote(send_b, recv_b, 1, (left, event))
    copy_m = remote(send_m, recv_m, 2, (right, event))
    copy_p = remote(send_p, recv_p, 3, (right, event))
    copy_q = remote(send_q, recv_q, 4, (right, event))

    one = (5, 8, lanes)
    low4, low2, low1 = row_bit(one, 4), row_bit(one, 2), row_bit(one, 1)
    low4_all = row_bit((3,) + one, 4)
    lane_place = lax.broadcasted_iota(jnp.int32, one, 2) & 3
    lane_weight = jnp.where(
        lane_place == 0, 0.2, jnp.where(lane_place == 2, 32.0 / 45.0, 49.0 / 90.0)
    ).astype(jnp.float32)
    level = lax.broadcasted_iota(jnp.int32, one, 0)
    edge = (level == 0) | (level == 4)
    inner = jnp.where(level == 2, 32.0 / 45.0, 49.0 / 90.0)
    level_weight = jnp.where(edge, 0.1, inner).astype(jnp.float32)
    closed = ((level == 0) & low1) | ((level == 4) & jnp.logical_not(low1))
    node_weight = jnp.where(edge, jnp.where(closed, 0.1, 0.2), inner).astype(jnp.float32)
    element_weight = level_weight * lane_weight

    def take(first, second):
        return swap_rows((first[0:5], first[4:9], second[0:5], second[4:9]))

    def join(low, high):
        return jnp.where(low4_all, low, high)

    def rows_of(value):
        return value.reshape(-1, lanes)

    def split(values):
        high = values.astype(jnp.bfloat16)
        low = (values - high.astype(jnp.float32)).astype(jnp.bfloat16)
        return high, low

    def slope_rows(values, columns):
        high, low = split(values)
        return jnp.dot(
            jnp.concatenate([high, low], axis=1),
            slope_two[:, :columns],
            preferred_element_type=jnp.float32,
        ) + jnp.dot(high, slope_low[:, :columns], preferred_element_type=jnp.float32)

    def back_rows(values):
        deep = values.shape[1]
        high, low = split(values)
        first = jnp.dot(high, back_two[:deep], preferred_element_type=jnp.float32)
        total = first[:, :lanes] + first[:, lanes:]
        return total + jnp.dot(low, back_high[:deep], preferred_element_type=jnp.float32)

    def level_slopes(levels):
        return jnp.stack([combine(numbers[k], levels) for k in range(5)])

    def level_back(stress):
        levels = [stress[q] for q in range(5)]
        return jnp.stack([combine(numbers[:, k], levels) for k in range(5)])

    def slopes(src, begin, end):
        found = slope_rows(rows_of(src[begin:end]), 2 * lanes)
        gy[begin:end] = found.reshape(end - begin, 3, 5, 8, 2 * lanes)

    def product(value):
        return value * turn(value, -2)

    def kinds_of(weight, gx, gz, gm, gd):
        xz, xy, zy = gx[1] + gz[0], gx[2] + gm[0], gz[2] + gm[1]
        jump = product(gd[2])
        k1 = weight * (product(gx[0] + gz[1] + gm[2]) + jump)
        shear = product(gx[0]) + product(gz[1]) + product(gm[2]) + jump
        cross = product(xz) + product(xy) + product(zy) + product(gd[0]) + product(gd[1])
        k2 = weight * (2.0 * shear + cross)
        return jnp.where(low2, k1, turn(k2, 2))

    def store_stress(i, m, l, gx, gz, gm, gd):
        xz, xy, zy = gx[1] + gz[0], gx[2] + gm[0], gz[2] + gm[1]
        both = m + m
        press = l * (gx[0] + gz[1] + gm[2])
        s_xz, s_xy, s_zy = m * xz, m * xy, m * zy
        sx[i, 0] = both * gx[0] + press
        sx[i, 1] = s_xz
        sx[i, 2] = s_xy
        sy[i, 0, :, :, :lanes] = s_xy
        sy[i, 1, :, :, :lanes] = s_zy
        sy[i, 2, :, :, :lanes] = both * gm[2] + press
        sy[i, 0, :, :, lanes:] = m * gd[0]
        sy[i, 1, :, :, lanes:] = m * gd[1]
        sy[i, 2, :, :, lanes:] = (both + l) * gd[2]
        for c, stress in enumerate((s_xz, both * gz[1] + press, s_zy)):
            f[i, c] = level_back(stress)

    def grads(src, i):
        gx = [combine(numbers[i], [src[q, c] for q in range(5)]) for c in range(3)]
        gz = [level_slopes([src[i, c, q] for q in range(5)]) for c in range(3)]
        gm = [gy[i, c, :, :, :lanes] for c in range(3)]
        gd = [gy[i, c, :, :, lanes:] for c in range(3)]
        return gx, gz, gm, gd

    def stresses(src):
        for i in range(5):
            store_stress(i, muw[i], lamw[i], *grads(src, i))

    def kinds(src, step):
        for i in range(5):
            found = kinds_of(float(weights[i]) * element_weight, *grads(src, i))
            kacc[i] = found if step == 0 else kacc[i] + found

    def gather_forces(*places):
        for i in places:
            total = back_rows(sy[i].reshape(120, 2 * lanes)).reshape(3, 5, 8, lanes)
            for c in range(3):
                value = f[i, c] + total[c] + combine(numbers[:, i], [sx[p, c] for p in range(5)])
                f[i, c] = middle_sum(value)

    def open_face(src, m, l):
        rows = jnp.concatenate([rows_of(src[0:4, 0]), rows_of(src[0:4, 2])], axis=0)
        means = slope_rows(rows, lanes).reshape(2, 4, 5, 8, lanes)
        faces = []
        for p in range(4):
            gx = [combine(numbers[p, :4], [src[q, c] for q in range(4)]) for c in range(3)]
            gz = [level_slopes([src[p, c, q] for q in range(5)]) for c in range(2)]
            press = l[p] * (gx[0] + gz[1] + means[1, p])
            faces.append(
                (
                    (m[p] + m[p]) * gx[0] + press,
                    m[p] * (gx[1] + gz[0]),
                    m[p] * (gx[2] + means[0, p]),
                )
            )
        force = [
            middle_sum(combine(numbers[:4, 4], [faces[p][c] for p in range(4)])) for c in range(3)
        ]
        slope = [combine(numbers[4, :4], [src[q, c] for q in range(4)]) for c in range(3)]
        return jnp.stack(force), jnp.stack(slope)

    def face_terms(l, q, stress):
        radial = px[l] * q[0] + float(numbers[4, l]) * stress[0]
        return [
            radial,
            mx[l] * q[1] + float(numbers[4, l]) * stress[1],
            mx[l] * q[2] + float(numbers[4, l]) * stress[2],
        ]

    def last_plane(q, found, slope, force):
        gx = [slope[c] + corner * q[c] for c in range(3)]
        gz = [level_slopes([q[c, k] for k in range(5)]) for c in range(3)]
        gm = [found[c, :, :, :lanes] for c in range(3)]
        gd = [found[c, :, :, lanes:] for c in range(3)]
        kept = kinds_of(0.1 * element_weight, gx, gz, gm, gd)
        m, l = muc[4], lamc[4]
        xz, xy, zy = gx[1] + gz[0], gx[2] + gm[0], gz[2] + gm[1]
        both = m + m
        press = l * (gx[0] + gz[1] + gm[2])
        s_xz, s_xy, s_zy = m * xz, m * xy, m * zy
        face = (both * gx[0] + press, s_xz, s_xy)
        mean = jnp.stack([s_xy, s_zy, both * gm[2] + press])
        half = jnp.stack([m * gd[0], m * gd[1], (both + l) * gd[2]])
        total = back_rows(
            jnp.concatenate([rows_of(mean), rows_of(half)], axis=1)
        ).reshape(3, 5, 8, lanes)
        across = face_terms(4, q, face)
        up = (s_xz, both * gz[1] + press, s_zy)
        result = [
            force[c] + middle_sum(total[c] + across[c] + level_back(up[c])) for c in range(3)
        ]
        return kept, jnp.stack(result), face

    ready("uf", "ua")
    for comp in range(3):
        for place, value in enumerate(take(uf[comp], ua[comp])):
            u[place, comp] = value
    ready("slope_two", "slope_low")
    slopes(u, 0, 4)
    u[4] = join(turn(u[0], 4), 0.0)
    wide_low = row_bit((3, 5, 8, 2 * lanes), 4)
    gy[4] = jnp.where(wide_low, turn(gy[0], 4), 0.0)
    ready("lam", "mu")
    lam_here, mu_here = take(lam[...], lam[...]), take(mu[...], mu[...])
    for place in range(4):
        weight = float(weights[place]) * element_weight
        muw[place] = mu_here[place] * weight
        lamw[place] = lam_here[place] * weight
    muw[4] = jnp.where(low4, turn(mu_here[0], 4) * (0.1 * element_weight), 0.0)
    lamw[4] = jnp.where(low4, turn(lam_here[0], 4) * (0.1 * element_weight), 0.0)
    edge_pair = jnp.where(low2, mu_here[0], lam_here[0])
    send_a[...] = pack_half(
        jnp.concatenate([u[0].reshape(15, 8, lanes), edge_pair], axis=0), True
    )
    first_rows = row_bit((9, 8, lanes), 4)
    send_m[0:9] = jnp.where(first_rows, turn(lam[...], 4), mu[...])
    ready("rho")
    five = jnp.concatenate([rho[5:9], rho[8:9]], axis=0)
    send_m[9:14] = jnp.where(low4, turn(rho[0:5], 4), five)

    stresses(u)
    pl.semaphore_wait(barrier, 2 + events - 1)
    copy_a.start()
    copy_m.start()
    for c in range(3):
        h[c] = combine(numbers[4], [u[q, c] for q in range(5)])
    ready("back_two", "back_high")
    gather_forces(4)
    send_p[...] = pack_half(
        jnp.concatenate([f[4].reshape(15, 8, lanes), h[...].reshape(15, 8, lanes)], axis=0), False
    )
    copy_p.start()
    gather_forces(0)

    rho_here = take(rho[...], rho[...])
    for place in range(4):
        weight = 0.2 if place == 0 else float(weights[place])
        im[place] = time_step / (rho_here[place] * (weight * (node_weight * lane_weight)))
    ready("vf", "va", "source")
    for comp in range(3):
        rates = take(vf[comp], va[comp])
        sources = take(jnp.zeros_like(source[comp]), source[comp])
        for place in range(4):
            pushed = sources[place] * im[place]
            sm[place, comp] = pushed
            b[place, comp] = rates[place] + pushed

    def advance(src, dst, place, force):
        for c in range(3):
            rate = b[place, c] - im[place] * force[c]
            b[place, c] = rate
            dst[place, c] = src[place, c] + time_step * rate

    advance(u, un, 0, f[0] + join(0.0, turn(f[4], 4)))
    send_b[...] = pack_half(
        jnp.concatenate([un[0].reshape(15, 8, lanes), time_step * im[0]], axis=0), True
    )
    copy_b.start()
    gather_forces(1, 2, 3)
    for place in (1, 2, 3):
        advance(u, un, place, f[place])
    force, slope = open_face(un, muw, lamw)
    send_q[...] = pack_half(
        jnp.concatenate([force.reshape(15, 8, lanes), slope.reshape(15, 8, lanes)], axis=0), False
    )
    copy_q.start()

    copy_a.wait_recv()
    arrived = unpack_half(recv_a[...], 20)
    u[4] = join(u[4], turn(arrived[:15].reshape(3, 5, 8, lanes), 4))
    slopes(u, 4, 5)
    kinds(u, 0)

    copy_m.wait_recv()
    pair = arrived[15:]
    mu_next, lam_next = jnp.where(low2, pair, turn(pair, 2)), jnp.where(low2, turn(pair, -2), pair)
    both_models = recv_m[0:9]
    lam_mix = jnp.where(first_rows, both_models, lam[...])
    mu_mix = jnp.where(first_rows, turn(both_models, 4), mu[...])
    masses = recv_m[9:14]
    rho_mix = jnp.where(
        first_rows, jnp.concatenate([masses, turn(masses, 4)[0:4]], axis=0), rho[...]
    )
    lam_two, mu_two, rho_two = take(lam_mix, lam_mix), take(mu_mix, mu_mix), take(rho_mix, rho_mix)
    for place in range(4):
        weight = float(weights[place]) * element_weight
        muc[place] = mu_two[place] * weight
        lamc[place] = lam_two[place] * weight
        weight = 0.2 if place == 0 else float(weights[place])
        imc[place] = time_step / (rho_two[place] * (weight * (node_weight * lane_weight)))
    weight = 0.1 * element_weight
    muc[4] = jnp.where(low4, mu_here[0], turn(mu_next, 4)) * weight
    lamc[4] = jnp.where(low4, lam_here[0], turn(lam_next, 4)) * weight
    for l in range(5):
        factors = numbers[:4, l] * numbers[:4, 4]
        mx[l] = combine(factors, [muc[p] for p in range(4)])
        px[l] = 2.0 * mx[l] + combine(factors, [lamc[p] for p in range(4)])

    q = join(u[0], u[4])
    found = jnp.where(wide_low, gy[0], gy[4])
    shears = []
    for l in range(4):
        number = float(numbers[l, 4])
        shears.append(jnp.stack([muc[l] * q[2], lamc[l] * q[0]]) * number)
    around = back_rows(rows_of(jnp.stack(shears))).reshape(4, 2, 5, 8, lanes)
    copy_p.wait_recv()
    packed = recv_p[...].reshape(3, 5, 8, lanes)
    kept, last, face = last_plane(
        q, found, join(packed, h[...]), join(turn(packed, 4), f[4])
    )
    edges = [jnp.where(low4, kept, 0.0)]
    fc[4] = last
    for l in range(4):
        number = float(numbers[l, 4])
        across = face_terms(l, q, face)
        fc[l, 0] = middle_sum(across[0] + around[l, 0] + level_back((number * muc[l]) * q[1]))
        fc[l, 1] = middle_sum(across[1] + level_back((number * lamc[l]) * q[0]))
        fc[l, 2] = middle_sum(across[2] + around[l, 1])
    for place in range(4):
        for c in range(3):
            change = imc[place] * fc[place, c]
            g[place, c] = -time_step * change
            if place == 0:
                change = jnp.where(low4, im[0] * fc[4, c], change)
            else:
                change = jnp.where(low4, 0.0, change)
            rate = b[place, c] - change
            b[place, c] = rate + sm[place, c]
            un[place, c] = un[place, c] - time_step * change
    slopes(un, 0, 4)
    copy_b.wait_recv()
    later = unpack_half(recv_b[...], 20)
    for c in range(3):
        ahead = turn(later[5 * c : 5 * c + 5], 4) - turn(later[15:], 4) * fc[4, c]
        un[4, c] = jnp.where(low4, turn(un[0, c], 4), ahead)
    slopes(un, 4, 5)
    kinds(un, 1)
    force, slope = open_face(g, muc, lamc)
    copy_q.wait_recv()
    packed = recv_q[...].reshape(3, 5, 8, lanes)
    kept, last, _ = last_plane(un[0], gy[0], slope + packed, force + turn(packed, 4))
    fc[0] = last
    edges.append(jnp.where(low4, kept, turn(kacc[4], 4)))

    first_plane = middle_sum(kacc[0] + edges[0] + edges[1])
    nodes = swap_rows((first_plane, *[middle_sum(kacc[i]) for i in (1, 2, 3)]))
    for kind in range(2):
        whole = jnp.concatenate([nodes[2 * kind][0:4], nodes[2 * kind + 1]], axis=0)
        for owner in range(events):
            send_k[owner, kind] = whole[:, planes * owner : planes * owner + planes]
    copies = []
    for offset in range(1, events):
        partner = lax.rem(event + offset, events)
        copy = pltpu.make_async_remote_copy(
            src_ref=send_k.at[partner],
            dst_ref=recv_k.at[offset - 1],
            send_sem=sems_k.at[0, offset - 1],
            recv_sem=sems_k.at[1, offset - 1],
            device_id=(region, partner),
            device_id_type=MESH,
        )
        copy.start()
        copies.append(copy)

    muw[4] = jnp.where(low4, muw[4], muc[4])
    lamw[4] = jnp.where(low4, lamw[4], lamc[4])
    stresses(un)
    gather_forces(4, 0, 1, 2, 3)
    advance(un, un, 0, f[0] + join(fc[0], turn(f[4], 4)))
    for place in (1, 2, 3):
        advance(un, un, place, f[place])

    def give(state, forward_out, adjoint_out):
        for c in range(3):
            four = swap_rows((state[0, c], state[1, c], state[2, c], state[3, c]))
            forward_out[c] = jnp.concatenate([four[0][0:4], four[1]], axis=0)
            adjoint_out[c] = jnp.concatenate([four[2][0:4], four[3]], axis=0)

    give(un, uf_out, ua_out)
    give(b, vf_out, va_out)

    total = send_k[event]
    for offset in range(1, events):
        copies[offset - 1].wait_recv()
        total = total + recv_k[offset - 1]
    k_out[...] = total

    for copy in [copy_a, copy_b, copy_m, copy_p, copy_q] + copies:
        copy.wait_send()


def flush(*refs):
    sources, outs, sems = refs[:5], refs[5:10], refs[10]
    stores = [pltpu.make_async_copy(sources[n], outs[n], sems.at[n]) for n in range(5)]
    for store in stores:
        store.start()
    for store in stores:
        store.wait()


def run(regions, events, interpret, *arrays):
    lanes = arrays[0].shape[-1]
    fields = [jnp.transpose(array[0], (0, 2, 1, 3)) for array in arrays[:5]]
    models = [jnp.transpose(array, (1, 0, 2)) for array in arrays[5:]]
    tables = [jnp.asarray(table) for table in lane_tables(lanes)]
    operands = [*fields, *models, *tables]
    operands = [pltpu.with_memory_space_constraint(array, pltpu.HBM) for array in operands]
    planes = 8 // events
    state = jax.ShapeDtypeStruct((3, 9, 8, lanes), jnp.float32)
    f32 = jnp.float32
    vector = pltpu.VMEM((5, 3, 5, 8, lanes), f32)
    wide = pltpu.VMEM((5, 3, 5, 8, 2 * lanes), f32)
    scalar = pltpu.VMEM((5, 5, 8, lanes), f32)

    def packed(*lead):
        return pltpu.VMEM(lead + (8, lanes), f32)

    outs = pl.pallas_call(
        functools.partial(kernel, regions, events),
        out_shape=[state] * 4 + [jax.ShapeDtypeStruct((2, 9, planes, lanes), f32)],
        in_specs=[pl.BlockSpec(memory_space=pltpu.HBM)] * 12,
        out_specs=[pl.BlockSpec(memory_space=pltpu.VMEM)] * 5,
        scratch_shapes=[
            vector,
            vector,
            vector,
            vector,
            vector,
            scalar,
            scalar,
            scalar,
            wide,
            vector,
            wide,
            vector,
            vector,
            packed(3, 5),
            scalar,
            scalar,
            scalar,
            scalar,
            scalar,
            scalar,
            packed(10),
            packed(10),
            packed(10),
            packed(10),
            packed(14),
            packed(14),
            packed(15),
            packed(15),
            packed(15),
            packed(15),
            pltpu.VMEM((events, 2, 9, planes, lanes), f32),
            pltpu.VMEM((max(events - 1, 1), 2, 9, planes, lanes), f32),
            pltpu.SemaphoreType.DMA((2, 5)),
            pltpu.SemaphoreType.DMA((2, max(events - 1, 1))),
            *[pltpu.VMEM(array.shape, array.dtype) for array in operands],
            pltpu.SemaphoreType.DMA((len(operands),)),
        ],
        compiler_params=pltpu.CompilerParams(
            collective_id=0, has_side_effects=True, vmem_limit_bytes=40 * 1024 * 1024
        ),
        name="adjoint_steps",
    )(*operands)
    shapes = [jax.ShapeDtypeStruct(out.shape, out.dtype) for out in outs]
    outs = pl.pallas_call(
        flush,
        out_shape=shapes,
        in_specs=[pl.BlockSpec(memory_space=pltpu.VMEM)] * 5,
        out_specs=[pl.BlockSpec(memory_space=pltpu.HBM)] * 5,
        scratch_shapes=[pltpu.SemaphoreType.DMA((5,))],
        compiler_params=pltpu.CompilerParams(vmem_limit_bytes=16 * 1024 * 1024),
        name="write_out",
    )(*outs)
    forward, forward_rate, adjoint, adjoint_rate = [
        jnp.transpose(out, (0, 2, 1, 3))[None] for out in outs[:4]
    ]
    return (forward, forward_rate, adjoint, adjoint_rate, jnp.transpose(outs[4], (0, 2, 1, 3)))


def solution(mesh):
    field = P("event", None, "region", None, None)
    model = P("region", None, None)
    regions, events = mesh.shape["region"], mesh.shape["event"]
    return jax.shard_map(
        functools.partial(run, regions, events, False),
        mesh=mesh,
        in_specs=(field,) * 5 + (model,) * 3,
        out_specs=(field,) * 4 + (P(None, ("region", "event"), None, None),),
        check_vma=False,
    )
```

```python
import functools
import math

import jax
import jax.numpy as jnp
import numpy as np
from jax import lax
from jax.experimental import pallas as pl
from jax.experimental.pallas import tpu as pltpu
from jax.sharding import PartitionSpec as P

STEPS = 2
time_step = 0.02
MESH = pl.DeviceIdType.MESH


def gll_numbers():
    points = np.array([-1.0, -math.sqrt(3.0 / 7.0), 0.0, math.sqrt(3.0 / 7.0), 1.0])
    weights = np.array([0.1, 49.0 / 90.0, 32.0 / 45.0, 49.0 / 90.0, 0.1])
    legendre = (35.0 * points**4 - 30.0 * points**2 + 3.0) / 8.0
    derivative = np.zeros((5, 5))
    for target in range(5):
        for column in range(5):
            if target != column:
                derivative[target, column] = legendre[target] / (
                    legendre[column] * (points[target] - points[column])
                )
    derivative[0, 0] = -5.0
    derivative[4, 4] = 5.0
    return (derivative, weights)


def lane_tables(lanes):
    numbers, _ = gll_numbers()
    table = np.zeros((lanes, 2 * lanes))
    for lane in range(lanes):
        start, local = lane - lane % 4, lane % 4
        for source in range(5):
            if local:
                table[(start + source) % lanes, lane] += numbers[local, source]
            else:
                right, left = (start + source) % lanes, (start - 4 + source) % lanes
                table[right, lane] += 0.5 * numbers[0, source]
                table[left, lane] += 0.5 * numbers[4, source]
                table[right, lanes + lane] += 0.5 * numbers[0, source]
                table[left, lanes + lane] -= 0.5 * numbers[4, source]
    high = table.astype(np.float32).astype(jnp.bfloat16)
    low = (table - high.astype(np.float64)).astype(np.float32).astype(jnp.bfloat16)
    return (
        np.concatenate([high, high], axis=0),
        low,
        np.concatenate([high.T, low.T], axis=1),
        np.ascontiguousarray(high.T),
    )


def combine(coefficients, pieces):
    total = None
    for number, piece in zip(coefficients, pieces):
        if number != 0.0:
            term = float(number) * piece
            total = term if total is None else total + term
    return total


def turn(value, shift):
    return pltpu.roll(value, shift % 8, value.ndim - 2)


def row_bit(shape, bit):
    return (lax.broadcasted_iota(jnp.int32, shape, len(shape) - 2) & bit) == 0


def swap_rows(four):
    shape = four[0].shape
    low_two, low_one = row_bit(shape, 2), row_bit(shape, 1)
    a0, a1, a2, a3 = four
    b0 = jnp.where(low_two, a0, turn(a2, 2))
    b2 = jnp.where(low_two, turn(a0, -2), a2)
    b1 = jnp.where(low_two, a1, turn(a3, 2))
    b3 = jnp.where(low_two, turn(a1, -2), a3)
    return (
        jnp.where(low_one, b0, turn(b1, 1)),
        jnp.where(low_one, turn(b0, -1), b1),
        jnp.where(low_one, b2, turn(b3, 1)),
        jnp.where(low_one, turn(b2, -1), b3),
    )


def middle_sum(blocks):
    first, last = blocks[..., 0, :, :], blocks[..., 4, :, :]
    low = row_bit(first.shape, 1)
    new_last = last + jnp.where(low, turn(first, -1), 0.0)
    new_first = first + jnp.where(low, 0.0, turn(last, 1))
    return jnp.concatenate(
        [new_first[..., None, :, :], blocks[..., 1:4, :, :], new_last[..., None, :, :]], axis=-3
    )


def pack_half(blocks, low):
    half = (blocks.shape[0] + 1) // 2
    first, second = blocks[:half], blocks[half:]
    if second.shape[0] < half:
        second = jnp.concatenate([second, first[-1:]], axis=0)
    keep = row_bit(first.shape, 4)
    other = turn(second, 4)
    return jnp.where(keep, first, other) if low else jnp.where(keep, other, first)


def unpack_half(packed, count):
    return jnp.concatenate([packed, turn(packed, 4)], axis=0)[:count]


def kernel(
    regions,
    events,
    uf_in,
    vf_in,
    ua_in,
    va_in,
    source_in,
    lam_in,
    mu_in,
    rho_in,
    slope_two_in,
    slope_low_in,
    back_two_in,
    back_high_in,
    uf_out,
    vf_out,
    ua_out,
    va_out,
    k_out,
    u,
    un,
    g,
    b,
    sm,
    im,
    muw,
    lamw,
    gy,
    sx,
    sy,
    f,
    fc,
    h,
    pre,
    kacc,
    imc,
    muc,
    lamc,
    px,
    mx,
    send_a,
    recv_a,
    send_b,
    recv_b,
    send_m,
    recv_m,
    send_p,
    recv_p,
    send_d,
    recv_d,
    send_q,
    recv_q,
    send_k,
    recv_k,
    sems,
    sems_k,
    uf,
    vf,
    ua,
    va,
    source,
    lam,
    mu,
    rho,
    slope_two,
    slope_low,
    back_two,
    back_high,
    load_sems,
):
    numbers, weights = gll_numbers()
    lanes = u.shape[-1]
    region, event = lax.axis_index("region"), lax.axis_index("event")
    left, right = lax.rem(region + regions - 1, regions), lax.rem(region + 1, regions)
    planes = 8 // events
    corner = float(numbers[4, 4])

    barrier = pltpu.get_barrier_semaphore()
    for side in (left, right):
        pl.semaphore_signal(barrier, inc=1, device_id=(side, event), device_id_type=MESH)
    for offset in range(1, events):
        partner = lax.rem(event + offset, events)
        pl.semaphore_signal(barrier, inc=1, device_id=(region, partner), device_id_type=MESH)

    loads = {}
    for number, (name, src, dst) in enumerate(
        (
            ("uf", uf_in, uf),
            ("ua", ua_in, ua),
            ("lam", lam_in, lam),
            ("mu", mu_in, mu),
            ("slope_two", slope_two_in, slope_two),
            ("slope_low", slope_low_in, slope_low),
            ("rho", rho_in, rho),
            ("vf", vf_in, vf),
            ("va", va_in, va),
            ("source", source_in, source),
            ("back_two", back_two_in, back_two),
            ("back_high", back_high_in, back_high),
        )
    ):
        loads[name] = pltpu.make_async_copy(src, dst, load_sems.at[number])
        loads[name].start()

    def ready(*names):
        for name in names:
            loads[name].wait()

    def remote(src, dst, number, target):
        return pltpu.make_async_remote_copy(
            src_ref=src,
            dst_ref=dst,
            send_sem=sems.at[0, number],
            recv_sem=sems.at[1, number],
            device_id=target,
            device_id_type=MESH,
        )

    copy_a = remote(send_a, recv_a, 0, (left, event))
    copy_b = remote(send_b, recv_b, 1, (left, event))
    copy_m = remote(send_m, recv_m, 2, (right, event))
    copy_p = remote(send_p, recv_p, 3, (right, event))
    copy_d = remote(send_d, recv_d, 4, (right, event))
    copy_q = remote(send_q, recv_q, 5, (right, event))

    one = (5, 8, lanes)
    low4, low2, low1 = row_bit(one, 4), row_bit(one, 2), row_bit(one, 1)
    low4_all = row_bit((3,) + one, 4)
    lane_place = lax.broadcasted_iota(jnp.int32, one, 2) & 3
    lane_weight = jnp.where(
        lane_place == 0, 0.2, jnp.where(lane_place == 2, 32.0 / 45.0, 49.0 / 90.0)
    ).astype(jnp.float32)
    level = lax.broadcasted_iota(jnp.int32, one, 0)
    edge = (level == 0) | (level == 4)
    inner = jnp.where(level == 2, 32.0 / 45.0, 49.0 / 90.0)
    level_weight = jnp.where(edge, 0.1, inner).astype(jnp.float32)
    closed = ((level == 0) & low1) | ((level == 4) & jnp.logical_not(low1))
    node_weight = jnp.where(edge, jnp.where(closed, 0.1, 0.2), inner).astype(jnp.float32)
    element_weight = level_weight * lane_weight

    def take(first, second):
        return swap_rows((first[0:5], first[4:9], second[0:5], second[4:9]))

    def join(low, high):
        return jnp.where(low4_all, low, high)

    def rows_of(value):
        return value.reshape(-1, lanes)

    def split(values):
        high = values.astype(jnp.bfloat16)
        low = (values - high.astype(jnp.float32)).astype(jnp.bfloat16)
        return high, low

    def slope_rows(values, columns):
        high, low = split(values)
        return jnp.dot(
            jnp.concatenate([high, low], axis=1),
            slope_two[:, :columns],
            preferred_element_type=jnp.float32,
        ) + jnp.dot(high, slope_low[:, :columns], preferred_element_type=jnp.float32)

    def back_rows(values):
        deep = values.shape[1]
        high, low = split(values)
        first = jnp.dot(high, back_two[:deep], preferred_element_type=jnp.float32)
        total = first[:, :lanes] + first[:, lanes:]
        return total + jnp.dot(low, back_high[:deep], preferred_element_type=jnp.float32)

    def level_slopes(levels):
        return jnp.stack([combine(numbers[k], levels) for k in range(5)])

    def level_back(stress):
        levels = [stress[q] for q in range(5)]
        return jnp.stack([combine(numbers[:, k], levels) for k in range(5)])

    def slopes(src, begin, end):
        found = slope_rows(rows_of(src[begin:end]), 2 * lanes)
        gy[begin:end] = found.reshape(end - begin, 3, 5, 8, 2 * lanes)

    def product(value):
        return value * turn(value, -2)

    def kinds_of(weight, gx, gz, gm, gd):
        xz, xy, zy = gx[1] + gz[0], gx[2] + gm[0], gz[2] + gm[1]
        jump = product(gd[2])
        k1 = weight * (product(gx[0] + gz[1] + gm[2]) + jump)
        shear = product(gx[0]) + product(gz[1]) + product(gm[2]) + jump
        cross = product(xz) + product(xy) + product(zy) + product(gd[0]) + product(gd[1])
        k2 = weight * (2.0 * shear + cross)
        return jnp.where(low2, k1, turn(k2, 2))

    def store_stress(i, m, l, gx, gz, gm, gd):
        xz, xy, zy = gx[1] + gz[0], gx[2] + gm[0], gz[2] + gm[1]
        both = m + m
        press = l * (gx[0] + gz[1] + gm[2])
        s_xz, s_xy, s_zy = m * xz, m * xy, m * zy
        sx[i, 0] = both * gx[0] + press
        sx[i, 1] = s_xz
        sx[i, 2] = s_xy
        sy[i, 0, :, :, :lanes] = s_xy
        sy[i, 1, :, :, :lanes] = s_zy
        sy[i, 2, :, :, :lanes] = both * gm[2] + press
        sy[i, 0, :, :, lanes:] = m * gd[0]
        sy[i, 1, :, :, lanes:] = m * gd[1]
        sy[i, 2, :, :, lanes:] = (both + l) * gd[2]
        for c, stress in enumerate((s_xz, both * gz[1] + press, s_zy)):
            f[i, c] = level_back(stress)

    def grads(src, i):
        gx = [combine(numbers[i], [src[q, c] for q in range(5)]) for c in range(3)]
        gz = [level_slopes([src[i, c, q] for q in range(5)]) for c in range(3)]
        gm = [gy[i, c, :, :, :lanes] for c in range(3)]
        gd = [gy[i, c, :, :, lanes:] for c in range(3)]
        return gx, gz, gm, gd

    def stresses(src):
        for i in range(5):
            store_stress(i, muw[i], lamw[i], *grads(src, i))

    def kinds(src, step):
        for i in range(5):
            found = kinds_of(float(weights[i]) * element_weight, *grads(src, i))
            kacc[i] = found if step == 0 else kacc[i] + found

    def gather_forces(*places):
        for i in places:
            total = back_rows(sy[i].reshape(120, 2 * lanes)).reshape(3, 5, 8, lanes)
            for c in range(3):
                value = f[i, c] + total[c] + combine(numbers[:, i], [sx[p, c] for p in range(5)])
                f[i, c] = middle_sum(value)

    def open_slope(src):
        return jnp.stack([combine(numbers[4, :4], [src[q, c] for q in range(4)]) for c in range(3)])

    def open_face(src, m, l, means):
        faces = []
        for p in range(4):
            gx = [combine(numbers[p, :4], [src[q, c] for q in range(4)]) for c in range(3)]
            gz = [level_slopes([src[p, c, q] for q in range(5)]) for c in range(2)]
            press = l[p] * (gx[0] + gz[1] + means(p, 2))
            faces.append(
                (
                    (m[p] + m[p]) * gx[0] + press,
                    m[p] * (gx[1] + gz[0]),
                    m[p] * (gx[2] + means(p, 0)),
                )
            )
        return jnp.stack(
            [middle_sum(combine(numbers[:4, 4], [faces[p][c] for p in range(4)])) for c in range(3)]
        )

    def face_means(src):
        rows = jnp.concatenate([rows_of(src[0:4, 0]), rows_of(src[0:4, 2])], axis=0)
        means = slope_rows(rows, lanes).reshape(2, 4, 5, 8, lanes)
        return lambda p, c: means[c // 2, p]

    def held_means(p, c):
        return gy[p, c, :, :, :lanes]

    def plane_grads(q, found, slope):
        gx = [slope[c] + corner * q[c] for c in range(3)]
        gz = [level_slopes([q[c, k] for k in range(5)]) for c in range(3)]
        gm = [found[c, :, :, :lanes] for c in range(3)]
        gd = [found[c, :, :, lanes:] for c in range(3)]
        return gx, gz, gm, gd

    def last_plane(q, gx, gz, gm, gd):
        m, l = muc[4], lamc[4]
        xz, xy, zy = gx[1] + gz[0], gx[2] + gm[0], gz[2] + gm[1]
        both = m + m
        press = l * (gx[0] + gz[1] + gm[2])
        s_xz, s_xy, s_zy = m * xz, m * xy, m * zy
        face = (both * gx[0] + press, s_xz, s_xy)
        mean = jnp.stack([s_xy, s_zy, both * gm[2] + press])
        half = jnp.stack([m * gd[0], m * gd[1], (both + l) * gd[2]])
        total = back_rows(
            jnp.concatenate([rows_of(mean), rows_of(half)], axis=1)
        ).reshape(3, 5, 8, lanes)
        inner_face = (px[4] * q[0], mx[4] * q[1], mx[4] * q[2])
        up = (s_xz, both * gz[1] + press, s_zy)
        result = [
            middle_sum(total[c] + inner_face[c] + corner * face[c] + level_back(up[c]))
            for c in range(3)
        ]
        return jnp.stack(result), face

    ready("uf", "ua")
    for comp in range(3):
        for place, value in enumerate(take(uf[comp], ua[comp])):
            u[place, comp] = value
    ready("slope_two", "slope_low")
    slopes(u, 0, 4)
    ready("lam", "mu")
    lam_here, mu_here = take(lam[...], lam[...]), take(mu[...], mu[...])
    for place in range(4):
        weight = float(weights[place]) * element_weight
        muw[place] = mu_here[place] * weight
        lamw[place] = lam_here[place] * weight
    first_rows = row_bit((9, 8, lanes), 4)
    send_m[0:9] = jnp.where(first_rows, turn(lam[...], 4), mu[...])
    ready("rho")
    five = jnp.concatenate([rho[5:9], rho[8:9]], axis=0)
    send_m[9:14] = jnp.where(low4, turn(rho[0:5], 4), five)
    h[...] = open_slope(u)
    opened = open_face(u, muw, lamw, held_means)
    send_p[...] = pack_half(
        jnp.concatenate([opened.reshape(15, 8, lanes), h[...].reshape(15, 8, lanes)], axis=0), False
    )
    edge_pair = jnp.where(low2, mu_here[0], lam_here[0])
    send_a[...] = pack_half(
        jnp.concatenate([u[0].reshape(15, 8, lanes), edge_pair], axis=0), True
    )
    pl.semaphore_wait(barrier, 2 + events - 1)
    copy_m.start()
    copy_p.start()
    copy_a.start()

    u[4] = join(turn(u[0], 4), 0.0)
    wide_low = row_bit((3, 5, 8, 2 * lanes), 4)
    gy[4] = jnp.where(wide_low, turn(gy[0], 4), 0.0)
    muw[4] = jnp.where(low4, turn(mu_here[0], 4) * (0.1 * element_weight), 0.0)
    lamw[4] = jnp.where(low4, turn(lam_here[0], 4) * (0.1 * element_weight), 0.0)
    stresses(u)
    ready("back_two", "back_high")
    gather_forces(4, 0)

    rho_here = take(rho[...], rho[...])
    for place in range(4):
        weight = 0.2 if place == 0 else float(weights[place])
        im[place] = time_step / (rho_here[place] * (weight * (node_weight * lane_weight)))
    ready("vf", "va", "source")
    for comp in range(3):
        rates = take(vf[comp], va[comp])
        sources = take(jnp.zeros_like(source[comp]), source[comp])
        for place in range(4):
            pushed = sources[place] * im[place]
            sm[place, comp] = pushed
            b[place, comp] = rates[place] + pushed

    def advance(src, dst, place, force):
        for c in range(3):
            rate = b[place, c] - im[place] * force[c]
            b[place, c] = rate
            dst[place, c] = src[place, c] + time_step * rate

    advance(u, un, 0, f[0] + join(0.0, turn(f[4], 4)))
    send_b[...] = pack_half(
        jnp.concatenate([un[0].reshape(15, 8, lanes), time_step * im[0]], axis=0), True
    )
    copy_b.start()
    gather_forces(1, 2, 3)
    for place in (1, 2, 3):
        advance(u, un, place, f[place])
    send_d[...] = pack_half(open_slope(un).reshape(15, 8, lanes), False)
    copy_d.start()
    send_q[...] = pack_half(
        open_face(un, muw, lamw, face_means(un)).reshape(15, 8, lanes), False
    )
    copy_q.start()

    copy_a.wait_recv()
    arrived = unpack_half(recv_a[...], 20)
    u[4] = join(u[4], turn(arrived[:15].reshape(3, 5, 8, lanes), 4))
    slopes(u, 4, 5)
    kinds(u, 0)

    copy_m.wait_recv()
    pair = arrived[15:]
    mu_next, lam_next = jnp.where(low2, pair, turn(pair, 2)), jnp.where(low2, turn(pair, -2), pair)
    both_models = recv_m[0:9]
    lam_mix = jnp.where(first_rows, both_models, lam[...])
    mu_mix = jnp.where(first_rows, turn(both_models, 4), mu[...])
    masses = recv_m[9:14]
    rho_mix = jnp.where(
        first_rows, jnp.concatenate([masses, turn(masses, 4)[0:4]], axis=0), rho[...]
    )
    lam_two, mu_two, rho_two = take(lam_mix, lam_mix), take(mu_mix, mu_mix), take(rho_mix, rho_mix)
    for place in range(4):
        weight = float(weights[place]) * element_weight
        muc[place] = mu_two[place] * weight
        lamc[place] = lam_two[place] * weight
        weight = 0.2 if place == 0 else float(weights[place])
        imc[place] = time_step / (rho_two[place] * (weight * (node_weight * lane_weight)))
    weight = 0.1 * element_weight
    muc[4] = jnp.where(low4, mu_here[0], turn(mu_next, 4)) * weight
    lamc[4] = jnp.where(low4, lam_here[0], turn(lam_next, 4)) * weight
    muw[4] = jnp.where(low4, muw[4], muc[4])
    lamw[4] = jnp.where(low4, lamw[4], lamc[4])
    for l in range(5):
        factors = numbers[:4, l] * numbers[:4, 4]
        mx[l] = combine(factors, [muc[p] for p in range(4)])
        px[l] = 2.0 * mx[l] + combine(factors, [lamc[p] for p in range(4)])
    ends = -time_step * combine(numbers[4, :4] ** 2, [imc[p] for p in range(4)])

    q = join(u[0], u[4])
    found = jnp.where(wide_low, gy[0], gy[4])
    shears = []
    for l in range(4):
        number = float(numbers[l, 4])
        shears.append(jnp.stack([muc[l] * q[2], lamc[l] * q[0]]) * number)
    around = back_rows(rows_of(jnp.stack(shears))).reshape(4, 2, 5, 8, lanes)
    for l in range(4):
        number = float(numbers[l, 4])
        up = level_back((number * muc[l]) * q[1])
        pre[l, 0] = middle_sum(px[l] * q[0] + around[l, 0] + up)
        pre[l, 1] = middle_sum(mx[l] * q[1] + level_back((number * lamc[l]) * q[0]))
        pre[l, 2] = middle_sum(mx[l] * q[2] + around[l, 1])
    for c in range(3):
        terms = [imc[l] * pre[l, c] for l in range(4)]
        fc[4, c] = -time_step * combine(numbers[4, :4], terms)

    last, face = last_plane(q, *plane_grads(q, found, h[...]))
    for c in range(3):
        beyond = middle_sum(face[c])
        for place in range(4):
            change = imc[place] * (pre[place, c] + float(numbers[4, place]) * beyond)
            change = jnp.where(low4, 0.0, change)
            rate = b[place, c] - change
            b[place, c] = rate if place == 0 else rate + sm[place, c]
            un[place, c] = un[place, c] - time_step * change
    slopes(un, 1, 4)
    copy_b.wait_recv()
    later = unpack_half(recv_b[...], 20)
    for c in range(3):
        ahead = turn(later[5 * c : 5 * c + 5], 4) - turn(later[15:], 4) * (
            last[c] + f[4, c]
        )
        un[4, c] = jnp.where(low4, turn(un[0, c], 4), ahead)
    slopes(un, 4, 5)

    copy_p.wait_recv()
    packed = recv_p[...].reshape(3, 5, 8, lanes)
    first_grads = plane_grads(q, found, packed)
    last, face = last_plane(q, *first_grads)
    for c in range(3):
        force = last[c] + turn(packed[c], 4)
        change = jnp.where(low4, im[0] * force, 0.0)
        rate = b[0, c] - change
        b[0, c] = rate + sm[0, c]
        un[0, c] = un[0, c] - time_step * change
    slopes(un, 0, 1)
    edge_kinds = kinds_of(0.1 * element_weight, *first_grads)
    kinds(un, 1)
    copy_d.wait_recv()
    coming = unpack_half(recv_d[...], 15).reshape(3, 5, 8, lanes)
    beyond = [middle_sum(face[c]) for c in range(3)]
    slope = [fc[4, c] + ends * beyond[c] + turn(coming[c], 4) for c in range(3)]
    second_grads = plane_grads(un[0], gy[0], slope)
    edge_kinds = edge_kinds + kinds_of(0.1 * element_weight, *second_grads)
    edge_kinds = jnp.where(low4, edge_kinds, turn(kacc[4], 4))

    first_plane = middle_sum(kacc[0] + edge_kinds)
    nodes = swap_rows((first_plane, *[middle_sum(kacc[i]) for i in (1, 2, 3)]))
    for kind in range(2):
        whole = jnp.concatenate([nodes[2 * kind][0:4], nodes[2 * kind + 1]], axis=0)
        for owner in range(events):
            send_k[owner, kind] = whole[:, planes * owner : planes * owner + planes]
    copies = []
    for offset in range(1, events):
        partner = lax.rem(event + offset, events)
        copy = pltpu.make_async_remote_copy(
            src_ref=send_k.at[partner],
            dst_ref=recv_k.at[offset - 1],
            send_sem=sems_k.at[0, offset - 1],
            recv_sem=sems_k.at[1, offset - 1],
            device_id=(region, partner),
            device_id_type=MESH,
        )
        copy.start()
        copies.append(copy)

    for c in range(3):
        for l in range(4):
            change = pre[l, c] + float(numbers[4, l]) * beyond[c]
            g[l, c] = -time_step * (imc[l] * change)
    force = open_face(g, muc, lamc, face_means(g))
    last, _ = last_plane(un[0], *second_grads)
    copy_q.wait_recv()
    coming = unpack_half(recv_q[...], 15).reshape(3, 5, 8, lanes)
    fc[0] = last + force + turn(coming, 4)
    stresses(un)
    gather_forces(4, 0, 1, 2, 3)
    advance(un, un, 0, f[0] + join(fc[0], turn(f[4], 4)))
    for place in (1, 2, 3):
        advance(un, un, place, f[place])

    def give(state, forward_out, adjoint_out):
        for c in range(3):
            four = swap_rows((state[0, c], state[1, c], state[2, c], state[3, c]))
            forward_out[c] = jnp.concatenate([four[0][0:4], four[1]], axis=0)
            adjoint_out[c] = jnp.concatenate([four[2][0:4], four[3]], axis=0)

    give(un, uf_out, ua_out)
    give(b, vf_out, va_out)

    total = send_k[event]
    for offset in range(1, events):
        copies[offset - 1].wait_recv()
        total = total + recv_k[offset - 1]
    k_out[...] = total

    for copy in [copy_a, copy_b, copy_m, copy_p, copy_d, copy_q] + copies:
        copy.wait_send()


def flush(*refs):
    sources, outs, sems = refs[:5], refs[5:10], refs[10]
    stores = [pltpu.make_async_copy(sources[n], outs[n], sems.at[n]) for n in range(5)]
    for store in stores:
        store.start()
    for store in stores:
        store.wait()


def run(regions, events, interpret, *arrays):
    lanes = arrays[0].shape[-1]
    fields = [jnp.transpose(array[0], (0, 2, 1, 3)) for array in arrays[:5]]
    models = [jnp.transpose(array, (1, 0, 2)) for array in arrays[5:]]
    tables = [jnp.asarray(table) for table in lane_tables(lanes)]
    operands = [*fields, *models, *tables]
    operands = [pltpu.with_memory_space_constraint(array, pltpu.HBM) for array in operands]
    planes = 8 // events
    state = jax.ShapeDtypeStruct((3, 9, 8, lanes), jnp.float32)
    f32 = jnp.float32
    vector = pltpu.VMEM((5, 3, 5, 8, lanes), f32)
    wide = pltpu.VMEM((5, 3, 5, 8, 2 * lanes), f32)
    scalar = pltpu.VMEM((5, 5, 8, lanes), f32)

    def packed(*lead):
        return pltpu.VMEM(lead + (8, lanes), f32)

    outs = pl.pallas_call(
        functools.partial(kernel, regions, events),
        out_shape=[state] * 4 + [jax.ShapeDtypeStruct((2, 9, planes, lanes), f32)],
        in_specs=[pl.BlockSpec(memory_space=pltpu.HBM)] * 12,
        out_specs=[pl.BlockSpec(memory_space=pltpu.VMEM)] * 5,
        scratch_shapes=[
            vector,
            vector,
            vector,
            vector,
            vector,
            scalar,
            scalar,
            scalar,
            wide,
            vector,
            wide,
            vector,
            vector,
            packed(3, 5),
            vector,
            scalar,
            scalar,
            scalar,
            scalar,
            scalar,
            scalar,
            packed(10),
            packed(10),
            packed(10),
            packed(10),
            packed(14),
            packed(14),
            packed(15),
            packed(15),
            packed(8),
            packed(8),
            packed(8),
            packed(8),
            pltpu.VMEM((events, 2, 9, planes, lanes), f32),
            pltpu.VMEM((max(events - 1, 1), 2, 9, planes, lanes), f32),
            pltpu.SemaphoreType.DMA((2, 6)),
            pltpu.SemaphoreType.DMA((2, max(events - 1, 1))),
            *[pltpu.VMEM(array.shape, array.dtype) for array in operands],
            pltpu.SemaphoreType.DMA((len(operands),)),
        ],
        compiler_params=pltpu.CompilerParams(
            collective_id=0, has_side_effects=True, vmem_limit_bytes=40 * 1024 * 1024
        ),
        name="adjoint_steps",
    )(*operands)
    shapes = [jax.ShapeDtypeStruct(out.shape, out.dtype) for out in outs]
    outs = pl.pallas_call(
        flush,
        out_shape=shapes,
        in_specs=[pl.BlockSpec(memory_space=pltpu.VMEM)] * 5,
        out_specs=[pl.BlockSpec(memory_space=pltpu.HBM)] * 5,
        scratch_shapes=[pltpu.SemaphoreType.DMA((5,))],
        compiler_params=pltpu.CompilerParams(vmem_limit_bytes=16 * 1024 * 1024),
        name="write_out",
    )(*outs)
    forward, forward_rate, adjoint, adjoint_rate = [
        jnp.transpose(out, (0, 2, 1, 3))[None] for out in outs[:4]
    ]
    return (forward, forward_rate, adjoint, adjoint_rate, jnp.transpose(outs[4], (0, 2, 1, 3)))


def solution(mesh):
    field = P("event", None, "region", None, None)
    model = P("region", None, None)
    regions, events = mesh.shape["region"], mesh.shape["event"]
    return jax.shard_map(
        functools.partial(run, regions, events, False),
        mesh=mesh,
        in_specs=(field,) * 5 + (model,) * 3,
        out_specs=(field,) * 4 + (P(None, ("region", "event"), None, None),),
        check_vma=False,
    )
```

```python
import functools
import math

import jax
import jax.numpy as jnp
import numpy as np
from jax import lax
from jax.experimental import pallas as pl
from jax.experimental.pallas import tpu as pltpu
from jax.sharding import PartitionSpec as P

STEPS = 2
time_step = 0.02
MESH = pl.DeviceIdType.MESH


def gll_numbers():
    points = np.array([-1.0, -math.sqrt(3.0 / 7.0), 0.0, math.sqrt(3.0 / 7.0), 1.0])
    weights = np.array([0.1, 49.0 / 90.0, 32.0 / 45.0, 49.0 / 90.0, 0.1])
    legendre = (35.0 * points**4 - 30.0 * points**2 + 3.0) / 8.0
    derivative = np.zeros((5, 5))
    for target in range(5):
        for column in range(5):
            if target != column:
                derivative[target, column] = legendre[target] / (
                    legendre[column] * (points[target] - points[column])
                )
    derivative[0, 0] = -5.0
    derivative[4, 4] = 5.0
    return (derivative, weights)


def lane_tables(lanes):
    numbers, _ = gll_numbers()
    table = np.zeros((lanes, 2 * lanes))
    for lane in range(lanes):
        start, local = lane - lane % 4, lane % 4
        for source in range(5):
            if local:
                table[(start + source) % lanes, lane] += numbers[local, source]
            else:
                right, left = (start + source) % lanes, (start - 4 + source) % lanes
                table[right, lane] += 0.5 * numbers[0, source]
                table[left, lane] += 0.5 * numbers[4, source]
                table[right, lanes + lane] += 0.5 * numbers[0, source]
                table[left, lanes + lane] -= 0.5 * numbers[4, source]
    high = table.astype(np.float32).astype(jnp.bfloat16)
    low = (table - high.astype(np.float64)).astype(np.float32).astype(jnp.bfloat16)
    return (
        np.concatenate([high, high], axis=0),
        low,
        np.concatenate([high.T, low.T], axis=1),
        np.ascontiguousarray(high.T),
    )


def combine(coefficients, pieces):
    total = None
    for number, piece in zip(coefficients, pieces):
        if number != 0.0:
            term = float(number) * piece
            total = term if total is None else total + term
    return total


def turn(value, shift):
    return pltpu.roll(value, shift % 8, value.ndim - 2)


def row_bit(shape, bit):
    return (lax.broadcasted_iota(jnp.int32, shape, len(shape) - 2) & bit) == 0


def swap_rows(four):
    shape = four[0].shape
    low_two, low_one = row_bit(shape, 2), row_bit(shape, 1)
    a0, a1, a2, a3 = four
    b0 = jnp.where(low_two, a0, turn(a2, 2))
    b2 = jnp.where(low_two, turn(a0, -2), a2)
    b1 = jnp.where(low_two, a1, turn(a3, 2))
    b3 = jnp.where(low_two, turn(a1, -2), a3)
    return (
        jnp.where(low_one, b0, turn(b1, 1)),
        jnp.where(low_one, turn(b0, -1), b1),
        jnp.where(low_one, b2, turn(b3, 1)),
        jnp.where(low_one, turn(b2, -1), b3),
    )


def middle_sum(blocks):
    first, last = blocks[..., 0, :, :], blocks[..., 4, :, :]
    low = row_bit(first.shape, 1)
    new_last = last + jnp.where(low, turn(first, -1), 0.0)
    new_first = first + jnp.where(low, 0.0, turn(last, 1))
    return jnp.concatenate(
        [new_first[..., None, :, :], blocks[..., 1:4, :, :], new_last[..., None, :, :]], axis=-3
    )


def pack_half(blocks, low):
    half = (blocks.shape[0] + 1) // 2
    first, second = blocks[:half], blocks[half:]
    if second.shape[0] < half:
        second = jnp.concatenate([second, first[-1:]], axis=0)
    keep = row_bit(first.shape, 4)
    other = turn(second, 4)
    return jnp.where(keep, first, other) if low else jnp.where(keep, other, first)


def unpack_half(packed, count):
    return jnp.concatenate([packed, turn(packed, 4)], axis=0)[:count]


def kernel(
    regions,
    events,
    uf_in,
    vf_in,
    ua_in,
    va_in,
    source_in,
    lam_in,
    mu_in,
    rho_in,
    slope_two_in,
    slope_low_in,
    back_two_in,
    back_high_in,
    uf_out,
    vf_out,
    ua_out,
    va_out,
    k_out,
    u,
    un,
    g,
    b,
    sm,
    im,
    muw,
    lamw,
    gy,
    sx,
    sy,
    f,
    fc,
    h,
    pre,
    kacc,
    imc,
    muc,
    lamc,
    px,
    mx,
    send_a,
    recv_a,
    send_b,
    recv_b,
    send_m,
    recv_m,
    send_p,
    recv_p,
    send_d,
    recv_d,
    send_q,
    recv_q,
    send_e,
    recv_e,
    send_k,
    recv_k,
    sems,
    sems_k,
    sems_e,
    uf,
    vf,
    ua,
    va,
    source,
    lam,
    mu,
    rho,
    slope_two,
    slope_low,
    back_two,
    back_high,
    load_sems,
):
    numbers, weights = gll_numbers()
    lanes = u.shape[-1]
    region, event = lax.axis_index("region"), lax.axis_index("event")
    left, right = lax.rem(region + regions - 1, regions), lax.rem(region + 1, regions)
    planes = 8 // events
    corner = float(numbers[4, 4])

    barrier = pltpu.get_barrier_semaphore()
    for side in (left, right):
        pl.semaphore_signal(barrier, inc=1, device_id=(side, event), device_id_type=MESH)
    for offset in range(1, events):
        partner = lax.rem(event + offset, events)
        pl.semaphore_signal(barrier, inc=1, device_id=(region, partner), device_id_type=MESH)

    loads = {}
    for number, (name, src, dst) in enumerate(
        (
            ("uf", uf_in, uf),
            ("ua", ua_in, ua),
            ("lam", lam_in, lam),
            ("mu", mu_in, mu),
            ("slope_two", slope_two_in, slope_two),
            ("slope_low", slope_low_in, slope_low),
            ("rho", rho_in, rho),
            ("back_two", back_two_in, back_two),
            ("back_high", back_high_in, back_high),
            ("vf", vf_in, vf),
            ("va", va_in, va),
            ("source", source_in, source),
        )
    ):
        loads[name] = pltpu.make_async_copy(src, dst, load_sems.at[number])
        if number < 7:
            loads[name].start()

    def ready(*names):
        for name in names:
            loads[name].wait()

    def remote(src, dst, number, target):
        return pltpu.make_async_remote_copy(
            src_ref=src,
            dst_ref=dst,
            send_sem=sems.at[0, number],
            recv_sem=sems.at[1, number],
            device_id=target,
            device_id_type=MESH,
        )

    copy_a = remote(send_a, recv_a, 0, (left, event))
    copy_b = remote(send_b, recv_b, 1, (left, event))
    copy_m = remote(send_m, recv_m, 2, (right, event))
    copy_p = remote(send_p, recv_p, 3, (right, event))
    copy_d = remote(send_d, recv_d, 4, (right, event))
    copy_q = remote(send_q, recv_q, 5, (right, event))

    one = (5, 8, lanes)
    low4, low2, low1 = row_bit(one, 4), row_bit(one, 2), row_bit(one, 1)
    low4_all = row_bit((3,) + one, 4)
    lane_place = lax.broadcasted_iota(jnp.int32, one, 2) & 3
    lane_weight = jnp.where(
        lane_place == 0, 0.2, jnp.where(lane_place == 2, 32.0 / 45.0, 49.0 / 90.0)
    ).astype(jnp.float32)
    level = lax.broadcasted_iota(jnp.int32, one, 0)
    edge = (level == 0) | (level == 4)
    inner = jnp.where(level == 2, 32.0 / 45.0, 49.0 / 90.0)
    level_weight = jnp.where(edge, 0.1, inner).astype(jnp.float32)
    closed = ((level == 0) & low1) | ((level == 4) & jnp.logical_not(low1))
    node_weight = jnp.where(edge, jnp.where(closed, 0.1, 0.2), inner).astype(jnp.float32)
    element_weight = level_weight * lane_weight

    def take(first, second):
        return swap_rows((first[0:5], first[4:9], second[0:5], second[4:9]))

    def join(low, high):
        return jnp.where(low4_all, low, high)

    def rows_of(value):
        return value.reshape(-1, lanes)

    def split(values):
        high = values.astype(jnp.bfloat16)
        low = (values - high.astype(jnp.float32)).astype(jnp.bfloat16)
        return high, low

    def slope_rows(values, columns):
        high, low = split(values)
        return jnp.dot(
            jnp.concatenate([high, low], axis=1),
            slope_two[:, :columns],
            preferred_element_type=jnp.float32,
        ) + jnp.dot(high, slope_low[:, :columns], preferred_element_type=jnp.float32)

    def back_rows(values):
        deep = values.shape[1]
        high, low = split(values)
        first = jnp.dot(high, back_two[:deep], preferred_element_type=jnp.float32)
        total = first[:, :lanes] + first[:, lanes:]
        return total + jnp.dot(low, back_high[:deep], preferred_element_type=jnp.float32)

    def level_slopes(levels):
        return jnp.stack([combine(numbers[k], levels) for k in range(5)])

    def level_back(stress):
        levels = [stress[q] for q in range(5)]
        return jnp.stack([combine(numbers[:, k], levels) for k in range(5)])

    def slopes(src, begin, end):
        found = slope_rows(rows_of(src[begin:end]), 2 * lanes)
        gy[begin:end] = found.reshape(end - begin, 3, 5, 8, 2 * lanes)

    def product(value):
        return value * turn(value, -2)

    def kinds_of(weight, gx, gz, gm, gd):
        xz, xy, zy = gx[1] + gz[0], gx[2] + gm[0], gz[2] + gm[1]
        jump = product(gd[2])
        k1 = weight * (product(gx[0] + gz[1] + gm[2]) + jump)
        shear = product(gx[0]) + product(gz[1]) + product(gm[2]) + jump
        cross = product(xz) + product(xy) + product(zy) + product(gd[0]) + product(gd[1])
        k2 = weight * (2.0 * shear + cross)
        return jnp.where(low2, k1, turn(k2, 2))

    def store_stress(i, m, l, gx, gz, gm, gd):
        xz, xy, zy = gx[1] + gz[0], gx[2] + gm[0], gz[2] + gm[1]
        both = m + m
        press = l * (gx[0] + gz[1] + gm[2])
        s_xz, s_xy, s_zy = m * xz, m * xy, m * zy
        sx[i, 0] = both * gx[0] + press
        sx[i, 1] = s_xz
        sx[i, 2] = s_xy
        sy[i, 0, :, :, :lanes] = s_xy
        sy[i, 1, :, :, :lanes] = s_zy
        sy[i, 2, :, :, :lanes] = both * gm[2] + press
        sy[i, 0, :, :, lanes:] = m * gd[0]
        sy[i, 1, :, :, lanes:] = m * gd[1]
        sy[i, 2, :, :, lanes:] = (both + l) * gd[2]
        for c, stress in enumerate((s_xz, both * gz[1] + press, s_zy)):
            f[i, c] = level_back(stress)

    def grads(src, i):
        gx = [combine(numbers[i], [src[q, c] for q in range(5)]) for c in range(3)]
        gz = [level_slopes([src[i, c, q] for q in range(5)]) for c in range(3)]
        gm = [gy[i, c, :, :, :lanes] for c in range(3)]
        gd = [gy[i, c, :, :, lanes:] for c in range(3)]
        return gx, gz, gm, gd

    def stresses(src):
        for i in range(5):
            store_stress(i, muw[i], lamw[i], *grads(src, i))

    def kinds(src, step):
        for i in range(5):
            found = kinds_of(float(weights[i]) * element_weight, *grads(src, i))
            kacc[i] = found if step == 0 else kacc[i] + found

    def gather_forces(*places):
        for i in places:
            total = back_rows(sy[i].reshape(120, 2 * lanes)).reshape(3, 5, 8, lanes)
            for c in range(3):
                value = f[i, c] + total[c] + combine(numbers[:, i], [sx[p, c] for p in range(5)])
                f[i, c] = middle_sum(value)

    def open_slope(src):
        return jnp.stack([combine(numbers[4, :4], [src[q, c] for q in range(4)]) for c in range(3)])

    def open_face(src, m, l, means):
        faces = []
        for p in range(4):
            gx = [combine(numbers[p, :4], [src[q, c] for q in range(4)]) for c in range(3)]
            gz = [level_slopes([src[p, c, q] for q in range(5)]) for c in range(2)]
            press = l[p] * (gx[0] + gz[1] + means(p, 2))
            faces.append(
                (
                    (m[p] + m[p]) * gx[0] + press,
                    m[p] * (gx[1] + gz[0]),
                    m[p] * (gx[2] + means(p, 0)),
                )
            )
        return jnp.stack(
            [middle_sum(combine(numbers[:4, 4], [faces[p][c] for p in range(4)])) for c in range(3)]
        )

    def face_means(src):
        rows = jnp.concatenate([rows_of(src[0:4, 0]), rows_of(src[0:4, 2])], axis=0)
        means = slope_rows(rows, lanes).reshape(2, 4, 5, 8, lanes)
        return lambda p, c: means[c // 2, p]

    def held_means(p, c):
        return gy[p, c, :, :, :lanes]

    def plane_grads(q, found, slope):
        gx = [slope[c] + corner * q[c] for c in range(3)]
        gz = [level_slopes([q[c, k] for k in range(5)]) for c in range(3)]
        gm = [found[c, :, :, :lanes] for c in range(3)]
        gd = [found[c, :, :, lanes:] for c in range(3)]
        return gx, gz, gm, gd

    def last_plane(q, gx, gz, gm, gd):
        m, l = muc[4], lamc[4]
        xz, xy, zy = gx[1] + gz[0], gx[2] + gm[0], gz[2] + gm[1]
        both = m + m
        press = l * (gx[0] + gz[1] + gm[2])
        s_xz, s_xy, s_zy = m * xz, m * xy, m * zy
        face = (both * gx[0] + press, s_xz, s_xy)
        mean = jnp.stack([s_xy, s_zy, both * gm[2] + press])
        half = jnp.stack([m * gd[0], m * gd[1], (both + l) * gd[2]])
        total = back_rows(
            jnp.concatenate([rows_of(mean), rows_of(half)], axis=1)
        ).reshape(3, 5, 8, lanes)
        inner_face = (px[4] * q[0], mx[4] * q[1], mx[4] * q[2])
        up = (s_xz, both * gz[1] + press, s_zy)
        result = [
            middle_sum(total[c] + inner_face[c] + corner * face[c] + level_back(up[c]))
            for c in range(3)
        ]
        return jnp.stack(result), face

    ready("uf", "ua")
    for comp in range(3):
        for place, value in enumerate(take(uf[comp], ua[comp])):
            u[place, comp] = value
    ready("lam", "mu", "rho")
    first_rows = row_bit((9, 8, lanes), 4)
    send_m[0:9] = jnp.where(first_rows, turn(lam[...], 4), mu[...])
    five = jnp.concatenate([rho[5:9], rho[8:9]], axis=0)
    send_m[9:14] = jnp.where(low4, turn(rho[0:5], 4), five)
    ready("slope_two", "slope_low")
    for name in ("back_two", "back_high", "vf", "va", "source"):
        loads[name].start()
    pl.semaphore_wait(barrier, 2 + events - 1)
    copy_m.start()
    slopes(u, 0, 4)
    lam_here, mu_here = take(lam[...], lam[...]), take(mu[...], mu[...])
    for place in range(4):
        weight = float(weights[place]) * element_weight
        muw[place] = mu_here[place] * weight
        lamw[place] = lam_here[place] * weight
    h[...] = open_slope(u)
    opened = open_face(u, muw, lamw, held_means)
    send_p[...] = pack_half(
        jnp.concatenate([opened.reshape(15, 8, lanes), h[...].reshape(15, 8, lanes)], axis=0), False
    )
    copy_p.start()
    edge_pair = jnp.where(low2, mu_here[0], lam_here[0])
    send_a[...] = pack_half(
        jnp.concatenate([u[0].reshape(15, 8, lanes), edge_pair], axis=0), True
    )
    copy_a.start()

    u[4] = join(turn(u[0], 4), 0.0)
    wide_low = row_bit((3, 5, 8, 2 * lanes), 4)
    gy[4] = jnp.where(wide_low, turn(gy[0], 4), 0.0)
    muw[4] = jnp.where(low4, turn(mu_here[0], 4) * (0.1 * element_weight), 0.0)
    lamw[4] = jnp.where(low4, turn(lam_here[0], 4) * (0.1 * element_weight), 0.0)
    stresses(u)
    ready("back_two", "back_high")
    gather_forces(4, 0)

    rho_here = take(rho[...], rho[...])
    for place in range(4):
        weight = 0.2 if place == 0 else float(weights[place])
        im[place] = time_step / (rho_here[place] * (weight * (node_weight * lane_weight)))
    ready("vf", "va", "source")
    for comp in range(3):
        rates = take(vf[comp], va[comp])
        sources = take(jnp.zeros_like(source[comp]), source[comp])
        for place in range(4):
            pushed = sources[place] * im[place]
            sm[place, comp] = pushed
            b[place, comp] = rates[place] + pushed

    def advance(src, dst, place, force):
        for c in range(3):
            rate = b[place, c] - im[place] * force[c]
            b[place, c] = rate
            dst[place, c] = src[place, c] + time_step * rate

    advance(u, un, 0, f[0] + join(0.0, turn(f[4], 4)))
    send_b[...] = pack_half(
        jnp.concatenate([un[0].reshape(15, 8, lanes), time_step * im[0]], axis=0), True
    )
    copy_b.start()
    gather_forces(1, 2, 3)
    for place in (1, 2, 3):
        advance(u, un, place, f[place])
    send_d[...] = pack_half(open_slope(un).reshape(15, 8, lanes), False)
    copy_d.start()
    send_q[...] = pack_half(
        open_face(un, muw, lamw, face_means(un)).reshape(15, 8, lanes), False
    )
    copy_q.start()

    copy_a.wait_recv()
    arrived = unpack_half(recv_a[...], 20)
    u[4] = join(u[4], turn(arrived[:15].reshape(3, 5, 8, lanes), 4))
    slopes(u, 4, 5)
    kinds(u, 0)

    copy_m.wait_recv()
    pair = arrived[15:]
    mu_next, lam_next = jnp.where(low2, pair, turn(pair, 2)), jnp.where(low2, turn(pair, -2), pair)
    both_models = recv_m[0:9]
    lam_mix = jnp.where(first_rows, both_models, lam[...])
    mu_mix = jnp.where(first_rows, turn(both_models, 4), mu[...])
    masses = recv_m[9:14]
    rho_mix = jnp.where(
        first_rows, jnp.concatenate([masses, turn(masses, 4)[0:4]], axis=0), rho[...]
    )
    lam_two, mu_two, rho_two = take(lam_mix, lam_mix), take(mu_mix, mu_mix), take(rho_mix, rho_mix)
    for place in range(4):
        weight = float(weights[place]) * element_weight
        muc[place] = mu_two[place] * weight
        lamc[place] = lam_two[place] * weight
        weight = 0.2 if place == 0 else float(weights[place])
        imc[place] = time_step / (rho_two[place] * (weight * (node_weight * lane_weight)))
    weight = 0.1 * element_weight
    muc[4] = jnp.where(low4, mu_here[0], turn(mu_next, 4)) * weight
    lamc[4] = jnp.where(low4, lam_here[0], turn(lam_next, 4)) * weight
    muw[4] = jnp.where(low4, muw[4], muc[4])
    lamw[4] = jnp.where(low4, lamw[4], lamc[4])
    for l in range(5):
        factors = numbers[:4, l] * numbers[:4, 4]
        mx[l] = combine(factors, [muc[p] for p in range(4)])
        px[l] = 2.0 * mx[l] + combine(factors, [lamc[p] for p in range(4)])
    ends = -time_step * combine(numbers[4, :4] ** 2, [imc[p] for p in range(4)])

    q = join(u[0], u[4])
    found = jnp.where(wide_low, gy[0], gy[4])
    shears = []
    for l in range(4):
        number = float(numbers[l, 4])
        shears.append(jnp.stack([muc[l] * q[2], lamc[l] * q[0]]) * number)
    around = back_rows(rows_of(jnp.stack(shears))).reshape(4, 2, 5, 8, lanes)
    for l in range(4):
        number = float(numbers[l, 4])
        up = level_back((number * muc[l]) * q[1])
        pre[l, 0] = middle_sum(px[l] * q[0] + around[l, 0] + up)
        pre[l, 1] = middle_sum(mx[l] * q[1] + level_back((number * lamc[l]) * q[0]))
        pre[l, 2] = middle_sum(mx[l] * q[2] + around[l, 1])
    for c in range(3):
        terms = [imc[l] * pre[l, c] for l in range(4)]
        fc[4, c] = -time_step * combine(numbers[4, :4], terms)

    last, face = last_plane(q, *plane_grads(q, found, h[...]))
    for c in range(3):
        beyond = middle_sum(face[c])
        for place in range(4):
            change = imc[place] * (pre[place, c] + float(numbers[4, place]) * beyond)
            change = jnp.where(low4, 0.0, change)
            rate = b[place, c] - change
            b[place, c] = rate if place == 0 else rate + sm[place, c]
            un[place, c] = un[place, c] - time_step * change
    slopes(un, 1, 4)
    copy_b.wait_recv()
    later = unpack_half(recv_b[...], 20)
    for c in range(3):
        ahead = turn(later[5 * c : 5 * c + 5], 4) - turn(later[15:], 4) * (
            last[c] + f[4, c]
        )
        un[4, c] = jnp.where(low4, turn(un[0, c], 4), ahead)
    slopes(un, 4, 5)

    copy_p.wait_recv()
    packed = recv_p[...].reshape(3, 5, 8, lanes)
    first_grads = plane_grads(q, found, packed)
    last, face = last_plane(q, *first_grads)
    for c in range(3):
        force = last[c] + turn(packed[c], 4)
        change = jnp.where(low4, im[0] * force, 0.0)
        rate = b[0, c] - change
        b[0, c] = rate + sm[0, c]
        un[0, c] = un[0, c] - time_step * change
    slopes(un, 0, 1)
    kinds(un, 1)
    first_plane = middle_sum(kacc[0] + jnp.where(low4, 0.0, turn(kacc[4], 4)))
    nodes = swap_rows((first_plane, *[middle_sum(kacc[i]) for i in (1, 2, 3)]))
    for kind in range(2):
        whole = jnp.concatenate([nodes[2 * kind][0:4], nodes[2 * kind + 1]], axis=0)
        for owner in range(events):
            send_k[owner, kind] = whole[:, planes * owner : planes * owner + planes]
    copies = []
    for offset in range(1, events):
        partner = lax.rem(event + offset, events)
        copy = pltpu.make_async_remote_copy(
            src_ref=send_k.at[partner],
            dst_ref=recv_k.at[offset - 1],
            send_sem=sems_k.at[0, offset - 1],
            recv_sem=sems_k.at[1, offset - 1],
            device_id=(region, partner),
            device_id_type=MESH,
        )
        copy.start()
        copies.append(copy)

    edge_kinds = kinds_of(0.1 * element_weight, *first_grads)
    copy_d.wait_recv()
    coming = unpack_half(recv_d[...], 15).reshape(3, 5, 8, lanes)
    beyond = [middle_sum(face[c]) for c in range(3)]
    slope = [fc[4, c] + ends * beyond[c] + turn(coming[c], 4) for c in range(3)]
    second_grads = plane_grads(un[0], gy[0], slope)
    edge_kinds = middle_sum(edge_kinds + kinds_of(0.1 * element_weight, *second_grads))
    send_e[...] = pack_half(edge_kinds, True)
    slot = lax.max(event - 1, 0)
    copy_e = pltpu.make_async_remote_copy(
        src_ref=send_e,
        dst_ref=recv_e.at[slot],
        send_sem=sems_e.at[events - 1],
        recv_sem=sems_e.at[slot],
        device_id=(region, 0),
        device_id_type=MESH,
    )

    @pl.when(event > 0)
    def _():
        copy_e.start()

    for c in range(3):
        for l in range(4):
            change = pre[l, c] + float(numbers[4, l]) * beyond[c]
            g[l, c] = -time_step * (imc[l] * change)
    force = open_face(g, muc, lamc, face_means(g))
    last, _ = last_plane(un[0], *second_grads)
    copy_q.wait_recv()
    coming = unpack_half(recv_q[...], 15).reshape(3, 5, 8, lanes)
    fc[0] = last + force + turn(coming, 4)
    stresses(un)
    gather_forces(4, 0, 1, 2, 3)
    advance(un, un, 0, f[0] + join(fc[0], turn(f[4], 4)))
    for place in (1, 2, 3):
        advance(un, un, place, f[place])

    def give(state, forward_out, adjoint_out):
        for c in range(3):
            four = swap_rows((state[0, c], state[1, c], state[2, c], state[3, c]))
            forward_out[c] = jnp.concatenate([four[0][0:4], four[1]], axis=0)
            adjoint_out[c] = jnp.concatenate([four[2][0:4], four[3]], axis=0)

    give(un, uf_out, ua_out)
    give(b, vf_out, va_out)

    def first_share(value):
        nothing = jnp.zeros_like(value)
        parts = swap_rows((jnp.where(low4, value, 0.0), nothing, nothing, nothing))
        return [
            jnp.concatenate([parts[2 * kind][0:4], parts[2 * kind + 1]], axis=0)[:, 0:planes]
            for kind in range(2)
        ]

    own = first_share(unpack_half(send_e[...], 5))
    total = send_k[event]
    for kind in range(2):
        k_out[kind] = total[kind] + jnp.where(event == 0, own[kind], 0.0)
    for offset in range(1, events):
        copies[offset - 1].wait_recv()
        k_out[...] = k_out[...] + recv_k[offset - 1]

    @pl.when(event == 0)
    def _():
        extra = None
        for other in range(events - 1):
            pltpu.make_async_copy(recv_e.at[other], recv_e.at[other], sems_e.at[other]).wait()
            share = unpack_half(recv_e[other], 5)
            extra = share if extra is None else extra + share
        parts = first_share(extra)
        for kind in range(2):
            k_out[kind] = k_out[kind] + parts[kind]

    @pl.when(event > 0)
    def _():
        copy_e.wait_send()

    for copy in [copy_a, copy_b, copy_m, copy_p, copy_d, copy_q] + copies:
        copy.wait_send()


def flush(*refs):
    sources, outs, sems = refs[:5], refs[5:10], refs[10]
    stores = [pltpu.make_async_copy(sources[n], outs[n], sems.at[n]) for n in range(5)]
    for store in stores:
        store.start()
    for store in stores:
        store.wait()


def run(regions, events, interpret, *arrays):
    lanes = arrays[0].shape[-1]
    fields = [jnp.transpose(array[0], (0, 2, 1, 3)) for array in arrays[:5]]
    models = [jnp.transpose(array, (1, 0, 2)) for array in arrays[5:]]
    tables = [jnp.asarray(table) for table in lane_tables(lanes)]
    operands = [*fields, *models, *tables]
    operands = [pltpu.with_memory_space_constraint(array, pltpu.HBM) for array in operands]
    planes = 8 // events
    state = jax.ShapeDtypeStruct((3, 9, 8, lanes), jnp.float32)
    f32 = jnp.float32
    vector = pltpu.VMEM((5, 3, 5, 8, lanes), f32)
    wide = pltpu.VMEM((5, 3, 5, 8, 2 * lanes), f32)
    scalar = pltpu.VMEM((5, 5, 8, lanes), f32)

    def packed(*lead):
        return pltpu.VMEM(lead + (8, lanes), f32)

    outs = pl.pallas_call(
        functools.partial(kernel, regions, events),
        out_shape=[state] * 4 + [jax.ShapeDtypeStruct((2, 9, planes, lanes), f32)],
        in_specs=[pl.BlockSpec(memory_space=pltpu.HBM)] * 12,
        out_specs=[pl.BlockSpec(memory_space=pltpu.VMEM)] * 5,
        scratch_shapes=[
            vector,
            vector,
            vector,
            vector,
            vector,
            scalar,
            scalar,
            scalar,
            wide,
            vector,
            wide,
            vector,
            vector,
            packed(3, 5),
            vector,
            scalar,
            scalar,
            scalar,
            scalar,
            scalar,
            scalar,
            packed(10),
            packed(10),
            packed(10),
            packed(10),
            packed(14),
            packed(14),
            packed(15),
            packed(15),
            packed(8),
            packed(8),
            packed(8),
            packed(8),
            packed(3),
            packed(max(events - 1, 1), 3),
            pltpu.VMEM((events, 2, 9, planes, lanes), f32),
            pltpu.VMEM((max(events - 1, 1), 2, 9, planes, lanes), f32),
            pltpu.SemaphoreType.DMA((2, 6)),
            pltpu.SemaphoreType.DMA((2, max(events - 1, 1))),
            pltpu.SemaphoreType.DMA((events,)),
            *[pltpu.VMEM(array.shape, array.dtype) for array in operands],
            pltpu.SemaphoreType.DMA((len(operands),)),
        ],
        compiler_params=pltpu.CompilerParams(
            collective_id=0, has_side_effects=True, vmem_limit_bytes=40 * 1024 * 1024
        ),
        name="adjoint_steps",
    )(*operands)
    shapes = [jax.ShapeDtypeStruct(out.shape, out.dtype) for out in outs]
    outs = pl.pallas_call(
        flush,
        out_shape=shapes,
        in_specs=[pl.BlockSpec(memory_space=pltpu.VMEM)] * 5,
        out_specs=[pl.BlockSpec(memory_space=pltpu.HBM)] * 5,
        scratch_shapes=[pltpu.SemaphoreType.DMA((5,))],
        compiler_params=pltpu.CompilerParams(vmem_limit_bytes=16 * 1024 * 1024),
        name="write_out",
    )(*outs)
    forward, forward_rate, adjoint, adjoint_rate = [
        jnp.transpose(out, (0, 2, 1, 3))[None] for out in outs[:4]
    ]
    return (forward, forward_rate, adjoint, adjoint_rate, jnp.transpose(outs[4], (0, 2, 1, 3)))


def solution(mesh):
    field = P("event", None, "region", None, None)
    model = P("region", None, None)
    regions, events = mesh.shape["region"], mesh.shape["event"]
    return jax.shard_map(
        functools.partial(run, regions, events, False),
        mesh=mesh,
        in_specs=(field,) * 5 + (model,) * 3,
        out_specs=(field,) * 4 + (P(None, ("region", "event"), None, None),),
        check_vma=False,
    )
```

```python
import functools
import math

import jax
import jax.numpy as jnp
import numpy as np
from jax import lax
from jax.experimental import pallas as pl
from jax.experimental.pallas import tpu as pltpu
from jax.sharding import PartitionSpec as P

STEPS = 2
time_step = 0.02
MESH = pl.DeviceIdType.MESH


def gll_numbers():
    points = np.array([-1.0, -math.sqrt(3.0 / 7.0), 0.0, math.sqrt(3.0 / 7.0), 1.0])
    weights = np.array([0.1, 49.0 / 90.0, 32.0 / 45.0, 49.0 / 90.0, 0.1])
    legendre = (35.0 * points**4 - 30.0 * points**2 + 3.0) / 8.0
    derivative = np.zeros((5, 5))
    for target in range(5):
        for column in range(5):
            if target != column:
                derivative[target, column] = legendre[target] / (
                    legendre[column] * (points[target] - points[column])
                )
    derivative[0, 0] = -5.0
    derivative[4, 4] = 5.0
    return (derivative, weights)


def lane_tables(lanes):
    numbers, _ = gll_numbers()
    table = np.zeros((lanes, 2 * lanes))
    for lane in range(lanes):
        start, local = lane - lane % 4, lane % 4
        for source in range(5):
            if local:
                table[(start + source) % lanes, lane] += numbers[local, source]
            else:
                right, left = (start + source) % lanes, (start - 4 + source) % lanes
                table[right, lane] += 0.5 * numbers[0, source]
                table[left, lane] += 0.5 * numbers[4, source]
                table[right, lanes + lane] += 0.5 * numbers[0, source]
                table[left, lanes + lane] -= 0.5 * numbers[4, source]
    high = table.astype(np.float32).astype(jnp.bfloat16)
    low = (table - high.astype(np.float64)).astype(np.float32).astype(jnp.bfloat16)
    return (
        np.concatenate([high, high], axis=0),
        low,
        np.concatenate([high.T, low.T], axis=1),
        np.ascontiguousarray(high.T),
    )


def combine(coefficients, pieces):
    total = None
    for number, piece in zip(coefficients, pieces):
        if number != 0.0:
            term = float(number) * piece
            total = term if total is None else total + term
    return total


def turn(value, shift):
    return pltpu.roll(value, shift % 8, value.ndim - 2)


def row_bit(shape, bit):
    return (lax.broadcasted_iota(jnp.int32, shape, len(shape) - 2) & bit) == 0


def swap_rows(four):
    shape = four[0].shape
    low_two, low_one = row_bit(shape, 2), row_bit(shape, 1)
    a0, a1, a2, a3 = four
    b0 = jnp.where(low_two, a0, turn(a2, 2))
    b2 = jnp.where(low_two, turn(a0, -2), a2)
    b1 = jnp.where(low_two, a1, turn(a3, 2))
    b3 = jnp.where(low_two, turn(a1, -2), a3)
    return (
        jnp.where(low_one, b0, turn(b1, 1)),
        jnp.where(low_one, turn(b0, -1), b1),
        jnp.where(low_one, b2, turn(b3, 1)),
        jnp.where(low_one, turn(b2, -1), b3),
    )


def middle_sum(blocks):
    first, last = blocks[..., 0, :, :], blocks[..., 4, :, :]
    low = row_bit(first.shape, 1)
    new_last = last + jnp.where(low, turn(first, -1), 0.0)
    new_first = first + jnp.where(low, 0.0, turn(last, 1))
    return jnp.concatenate(
        [new_first[..., None, :, :], blocks[..., 1:4, :, :], new_last[..., None, :, :]], axis=-3
    )


def pack_half(blocks, low):
    half = (blocks.shape[0] + 1) // 2
    first, second = blocks[:half], blocks[half:]
    if second.shape[0] < half:
        second = jnp.concatenate([second, first[-1:]], axis=0)
    keep = row_bit(first.shape, 4)
    other = turn(second, 4)
    return jnp.where(keep, first, other) if low else jnp.where(keep, other, first)


def unpack_half(packed, count):
    return jnp.concatenate([packed, turn(packed, 4)], axis=0)[:count]


def kernel(
    regions,
    events,
    uf_in,
    vf_in,
    ua_in,
    va_in,
    source_in,
    lam_in,
    mu_in,
    rho_in,
    slope_two_in,
    slope_low_in,
    back_two_in,
    back_high_in,
    uf_out,
    vf_out,
    ua_out,
    va_out,
    k_out,
    u,
    un,
    g,
    b,
    sm,
    im,
    muw,
    lamw,
    gy,
    sx,
    sy,
    f,
    fc,
    h,
    pre,
    kacc,
    imc,
    muc,
    lamc,
    px,
    mx,
    send_a,
    recv_a,
    send_b,
    recv_b,
    send_m,
    recv_m,
    send_p,
    recv_p,
    send_d,
    recv_d,
    send_q,
    recv_q,
    send_e,
    recv_e,
    send_x,
    recv_x,
    send_y,
    recv_y,
    send_z,
    recv_z,
    recv_pd,
    recv_dd,
    u_two,
    gy_two,
    sems_y,
    open_sem,
    send_k,
    recv_k,
    sems,
    sems_k,
    sems_e,
    uf,
    vf,
    ua,
    va,
    source,
    lam,
    mu,
    rho,
    slope_two,
    slope_low,
    back_two,
    back_high,
    load_sems,
):
    numbers, weights = gll_numbers()
    lanes = u.shape[-1]
    region, event = lax.axis_index("region"), lax.axis_index("event")
    left, right = lax.rem(region + regions - 1, regions), lax.rem(region + 1, regions)
    planes = 8 // events
    corner = float(numbers[4, 4])
    pair_up = events == 2
    lead = jnp.logical_and(region == 0, event == 0)
    mate = jnp.logical_and(region == 0, event == 1)
    giver = jnp.logical_and(region == regions - 1, event == 1)

    def only(condition, action):
        if pair_up:
            pl.when(condition)(action)

    def unless(condition, action):
        if pair_up:
            pl.when(jnp.logical_not(condition))(action)
        else:
            action()

    barrier = pltpu.get_barrier_semaphore()
    def greet(side, other):
        pl.semaphore_signal(barrier, inc=1, device_id=(side, other), device_id_type=MESH)

    greet(left, event)
    unless(giver, lambda: greet(right, event))
    only(lead, lambda: greet(left, 1))
    for offset in range(1, events):
        partner = lax.rem(event + offset, events)
        pl.semaphore_signal(barrier, inc=1, device_id=(region, partner), device_id_type=MESH)

    loads = {}
    for number, (name, src, dst) in enumerate(
        (
            ("uf", uf_in, uf),
            ("ua", ua_in, ua),
            ("lam", lam_in, lam),
            ("mu", mu_in, mu),
            ("slope_two", slope_two_in, slope_two),
            ("slope_low", slope_low_in, slope_low),
            ("rho", rho_in, rho),
            ("back_two", back_two_in, back_two),
            ("back_high", back_high_in, back_high),
            ("vf", vf_in, vf),
            ("va", va_in, va),
            ("source", source_in, source),
        )
    ):
        loads[name] = pltpu.make_async_copy(src, dst, load_sems.at[number])
        if number < 7:
            loads[name].start()

    def ready(*names):
        for name in names:
            loads[name].wait()

    def remote(src, dst, number, target):
        return pltpu.make_async_remote_copy(
            src_ref=src,
            dst_ref=dst,
            send_sem=sems.at[0, number],
            recv_sem=sems.at[1, number],
            device_id=target,
            device_id_type=MESH,
        )

    def aside(src, dst, number, target):
        return pltpu.make_async_remote_copy(
            src_ref=src,
            dst_ref=dst,
            send_sem=sems_y.at[0, number],
            recv_sem=sems_y.at[1, number],
            device_id=target,
            device_id_type=MESH,
        )

    copy_x = aside(send_x, recv_x, 0, (region, 0))
    copy_y = aside(send_y, recv_y, 1, (region, 0))
    copy_z = aside(send_z, recv_z, 2, (region, 0))
    copy_pd = aside(send_p, recv_pd, 3, (right, 0))
    copy_dd = aside(send_d, recv_dd, 4, (right, 0))
    copy_a = remote(send_a, recv_a, 0, (left, event))
    copy_b = remote(send_b, recv_b, 1, (left, event))
    copy_m = remote(send_m, recv_m, 2, (right, event))
    copy_p = remote(send_p, recv_p, 3, (right, event))
    copy_d = remote(send_d, recv_d, 4, (right, event))
    copy_q = remote(send_q, recv_q, 5, (right, event))

    one = (5, 8, lanes)
    low4, low2, low1 = row_bit(one, 4), row_bit(one, 2), row_bit(one, 1)
    low4_all = row_bit((3,) + one, 4)
    lane_place = lax.broadcasted_iota(jnp.int32, one, 2) & 3
    lane_weight = jnp.where(
        lane_place == 0, 0.2, jnp.where(lane_place == 2, 32.0 / 45.0, 49.0 / 90.0)
    ).astype(jnp.float32)
    level = lax.broadcasted_iota(jnp.int32, one, 0)
    edge = (level == 0) | (level == 4)
    inner = jnp.where(level == 2, 32.0 / 45.0, 49.0 / 90.0)
    level_weight = jnp.where(edge, 0.1, inner).astype(jnp.float32)
    closed = ((level == 0) & low1) | ((level == 4) & jnp.logical_not(low1))
    node_weight = jnp.where(edge, jnp.where(closed, 0.1, 0.2), inner).astype(jnp.float32)
    element_weight = level_weight * lane_weight

    def take(first, second):
        return swap_rows((first[0:5], first[4:9], second[0:5], second[4:9]))

    def join(low, high):
        return jnp.where(low4_all, low, high)

    def rows_of(value):
        return value.reshape(-1, lanes)

    def split(values):
        high = values.astype(jnp.bfloat16)
        low = (values - high.astype(jnp.float32)).astype(jnp.bfloat16)
        return high, low

    def slope_rows(values, columns):
        high, low = split(values)
        return jnp.dot(
            jnp.concatenate([high, low], axis=1),
            slope_two[:, :columns],
            preferred_element_type=jnp.float32,
        ) + jnp.dot(high, slope_low[:, :columns], preferred_element_type=jnp.float32)

    def back_rows(values):
        deep = values.shape[1]
        high, low = split(values)
        first = jnp.dot(high, back_two[:deep], preferred_element_type=jnp.float32)
        total = first[:, :lanes] + first[:, lanes:]
        return total + jnp.dot(low, back_high[:deep], preferred_element_type=jnp.float32)

    def level_slopes(levels):
        return jnp.stack([combine(numbers[k], levels) for k in range(5)])

    def level_back(stress):
        levels = [stress[q] for q in range(5)]
        return jnp.stack([combine(numbers[:, k], levels) for k in range(5)])

    def slopes(src, begin, end):
        found = slope_rows(rows_of(src[begin:end]), 2 * lanes)
        gy[begin:end] = found.reshape(end - begin, 3, 5, 8, 2 * lanes)

    def product(value):
        return value * turn(value, -2)

    def kinds_of(weight, gx, gz, gm, gd):
        xz, xy, zy = gx[1] + gz[0], gx[2] + gm[0], gz[2] + gm[1]
        jump = product(gd[2])
        k1 = weight * (product(gx[0] + gz[1] + gm[2]) + jump)
        shear = product(gx[0]) + product(gz[1]) + product(gm[2]) + jump
        cross = product(xz) + product(xy) + product(zy) + product(gd[0]) + product(gd[1])
        k2 = weight * (2.0 * shear + cross)
        return jnp.where(low2, k1, turn(k2, 2))

    def store_stress(i, m, l, gx, gz, gm, gd):
        xz, xy, zy = gx[1] + gz[0], gx[2] + gm[0], gz[2] + gm[1]
        both = m + m
        press = l * (gx[0] + gz[1] + gm[2])
        s_xz, s_xy, s_zy = m * xz, m * xy, m * zy
        sx[i, 0] = both * gx[0] + press
        sx[i, 1] = s_xz
        sx[i, 2] = s_xy
        sy[i, 0, :, :, :lanes] = s_xy
        sy[i, 1, :, :, :lanes] = s_zy
        sy[i, 2, :, :, :lanes] = both * gm[2] + press
        sy[i, 0, :, :, lanes:] = m * gd[0]
        sy[i, 1, :, :, lanes:] = m * gd[1]
        sy[i, 2, :, :, lanes:] = (both + l) * gd[2]
        for c, stress in enumerate((s_xz, both * gz[1] + press, s_zy)):
            f[i, c] = level_back(stress)

    def grads(src, i, gy=gy):
        gx = [combine(numbers[i], [src[q, c] for q in range(5)]) for c in range(3)]
        gz = [level_slopes([src[i, c, q] for q in range(5)]) for c in range(3)]
        gm = [gy[i, c, :, :, :lanes] for c in range(3)]
        gd = [gy[i, c, :, :, lanes:] for c in range(3)]
        return gx, gz, gm, gd

    def stresses(src):
        for i in range(5):
            store_stress(i, muw[i], lamw[i], *grads(src, i))

    def kinds(src, step, gy=gy, last=5):
        for i in range(last):
            found = kinds_of(float(weights[i]) * element_weight, *grads(src, i, gy))
            kacc[i] = found if step == 0 else kacc[i] + found

    def gather_forces(*places):
        for i in places:
            total = back_rows(sy[i].reshape(120, 2 * lanes)).reshape(3, 5, 8, lanes)
            for c in range(3):
                value = f[i, c] + total[c] + combine(numbers[:, i], [sx[p, c] for p in range(5)])
                f[i, c] = middle_sum(value)

    def open_slope(src):
        return jnp.stack([combine(numbers[4, :4], [src[q, c] for q in range(4)]) for c in range(3)])

    def open_face(src, m, l, means):
        faces = []
        for p in range(4):
            gx = [combine(numbers[p, :4], [src[q, c] for q in range(4)]) for c in range(3)]
            gz = [level_slopes([src[p, c, q] for q in range(5)]) for c in range(2)]
            press = l[p] * (gx[0] + gz[1] + means(p, 2))
            faces.append(
                (
                    (m[p] + m[p]) * gx[0] + press,
                    m[p] * (gx[1] + gz[0]),
                    m[p] * (gx[2] + means(p, 0)),
                )
            )
        return jnp.stack(
            [middle_sum(combine(numbers[:4, 4], [faces[p][c] for p in range(4)])) for c in range(3)]
        )

    def face_means(src):
        rows = jnp.concatenate([rows_of(src[0:4, 0]), rows_of(src[0:4, 2])], axis=0)
        means = slope_rows(rows, lanes).reshape(2, 4, 5, 8, lanes)
        return lambda p, c: means[c // 2, p]

    def held_means(p, c):
        return gy[p, c, :, :, :lanes]

    def plane_grads(q, found, slope):
        gx = [slope[c] + corner * q[c] for c in range(3)]
        gz = [level_slopes([q[c, k] for k in range(5)]) for c in range(3)]
        gm = [found[c, :, :, :lanes] for c in range(3)]
        gd = [found[c, :, :, lanes:] for c in range(3)]
        return gx, gz, gm, gd

    def last_plane(q, gx, gz, gm, gd):
        m, l = muc[4], lamc[4]
        xz, xy, zy = gx[1] + gz[0], gx[2] + gm[0], gz[2] + gm[1]
        both = m + m
        press = l * (gx[0] + gz[1] + gm[2])
        s_xz, s_xy, s_zy = m * xz, m * xy, m * zy
        face = (both * gx[0] + press, s_xz, s_xy)
        mean = jnp.stack([s_xy, s_zy, both * gm[2] + press])
        half = jnp.stack([m * gd[0], m * gd[1], (both + l) * gd[2]])
        total = back_rows(
            jnp.concatenate([rows_of(mean), rows_of(half)], axis=1)
        ).reshape(3, 5, 8, lanes)
        inner_face = (px[4] * q[0], mx[4] * q[1], mx[4] * q[2])
        up = (s_xz, both * gz[1] + press, s_zy)
        result = [
            middle_sum(total[c] + inner_face[c] + corner * face[c] + level_back(up[c]))
            for c in range(3)
        ]
        return jnp.stack(result), face

    ready("uf", "ua")
    for comp in range(3):
        for place, value in enumerate(take(uf[comp], ua[comp])):
            u[place, comp] = value
    ready("lam", "mu", "rho")
    first_rows = row_bit((9, 8, lanes), 4)
    send_m[0:9] = jnp.where(first_rows, turn(lam[...], 4), mu[...])
    five = jnp.concatenate([rho[5:9], rho[8:9]], axis=0)
    send_m[9:14] = jnp.where(low4, turn(rho[0:5], 4), five)
    ready("slope_two", "slope_low")
    for name in ("back_two", "back_high", "vf", "va", "source"):
        loads[name].start()
    peers = jnp.where(mate, events, jnp.where(giver, events + 2, events + 1))
    pl.semaphore_wait(barrier, peers if pair_up else events + 1)

    def open_left():
        pl.semaphore_signal(open_sem, inc=1, device_id=(right, event), device_id_type=MESH)

    only(giver, open_left)
    unless(giver, copy_m.start)
    slopes(u, 0, 4)
    lam_here, mu_here = take(lam[...], lam[...]), take(mu[...], mu[...])
    for place in range(4):
        weight = float(weights[place]) * element_weight
        muw[place] = mu_here[place] * weight
        lamw[place] = lam_here[place] * weight
    h[...] = open_slope(u)
    opened = open_face(u, muw, lamw, held_means)
    send_p[...] = pack_half(
        jnp.concatenate([opened.reshape(15, 8, lanes), h[...].reshape(15, 8, lanes)], axis=0), False
    )

    def give_twice():
        copy_pd.start()
        copy_m.start()

    only(giver, give_twice)
    copy_p.start()
    edge_pair = jnp.where(low2, mu_here[0], lam_here[0])
    send_a[...] = pack_half(
        jnp.concatenate([u[0].reshape(15, 8, lanes), edge_pair], axis=0), True
    )

    def share_first_plane():
        send_x[...] = pack_half(u[0].reshape(15, 8, lanes), True)
        copy_x.start()

    unless(mate, copy_a.start)
    only(mate, share_first_plane)

    u[4] = join(turn(u[0], 4), 0.0)
    wide_low = row_bit((3, 5, 8, 2 * lanes), 4)
    gy[4] = jnp.where(wide_low, turn(gy[0], 4), 0.0)
    muw[4] = jnp.where(low4, turn(mu_here[0], 4) * (0.1 * element_weight), 0.0)
    lamw[4] = jnp.where(low4, turn(lam_here[0], 4) * (0.1 * element_weight), 0.0)
    stresses(u)
    ready("back_two", "back_high")
    gather_forces(4, 0)

    rho_here = take(rho[...], rho[...])
    for place in range(4):
        weight = 0.2 if place == 0 else float(weights[place])
        im[place] = time_step / (rho_here[place] * (weight * (node_weight * lane_weight)))
    ready("vf", "va", "source")
    for comp in range(3):
        rates = take(vf[comp], va[comp])
        sources = take(jnp.zeros_like(source[comp]), source[comp])
        for place in range(4):
            pushed = sources[place] * im[place]
            sm[place, comp] = pushed
            b[place, comp] = rates[place] + pushed

    def advance(src, dst, place, force):
        for c in range(3):
            rate = b[place, c] - im[place] * force[c]
            b[place, c] = rate
            dst[place, c] = src[place, c] + time_step * rate

    advance(u, un, 0, f[0] + join(0.0, turn(f[4], 4)))
    send_b[...] = pack_half(
        jnp.concatenate([un[0].reshape(15, 8, lanes), time_step * im[0]], axis=0), True
    )
    unless(mate, copy_b.start)
    gather_forces(1, 2, 3)
    for place in (1, 2, 3):
        advance(u, un, place, f[place])
    send_d[...] = pack_half(open_slope(un).reshape(15, 8, lanes), False)
    only(giver, copy_dd.start)
    copy_d.start()
    send_q[...] = pack_half(
        open_face(un, muw, lamw, face_means(un)).reshape(15, 8, lanes), False
    )
    copy_q.start()

    copy_a.wait_recv()
    arrived = unpack_half(recv_a[...], 20)
    u[4] = join(u[4], turn(arrived[:15].reshape(3, 5, 8, lanes), 4))
    slopes(u, 4, 5)
    kinds(u, 0)
    pair = arrived[15:]
    mu_next, lam_next = jnp.where(low2, pair, turn(pair, 2)), jnp.where(low2, turn(pair, -2), pair)
    weight = 0.1 * element_weight
    muc[4] = jnp.where(low4, mu_here[0], turn(mu_next, 4)) * weight
    lamc[4] = jnp.where(low4, lam_here[0], turn(lam_next, 4)) * weight

    def share_first_element():
        send_z[...] = pack_half(kacc[0:4].reshape(20, 8, lanes), True)
        copy_z.start()
        far, m, l = u[4], muw, lamw
        factors = numbers[:4, 0] * numbers[:4, 4]
        m_face = combine(factors, [m[p] for p in range(4)])
        l_face = 2.0 * m_face + combine(factors, [l[p] for p in range(4)])
        number = float(numbers[0, 4])
        m_one, l_one = m[0] * number, l[0] * number
        rows = rows_of(jnp.stack([m_one * far[2], l_one * far[0]]))
        across = back_rows(rows).reshape(2, 5, 8, lanes)
        gx, gz, gm, _ = plane_grads(far, gy[4], h[...])
        m_last, l_last = muc[4], lamc[4]
        face = (
            (m_last + m_last) * gx[0] + l_last * (gx[0] + gz[1] + gm[2]),
            m_last * (gx[1] + gz[0]),
            m_last * (gx[2] + gm[0]),
        )
        inside = (
            l_face * far[0] + across[0] + level_back(m_one * far[1]),
            m_face * far[1] + level_back(l_one * far[0]),
            m_face * far[2] + across[1],
        )
        ends_here = []
        for c in range(3):
            force = middle_sum(inside[c] + float(numbers[4, 0]) * face[c])
            ends_here.append(turn(un[0, c] - time_step * (im[0] * force), 4))
        firsts = un[0:4].reshape(60, 8, lanes)
        send_y[...] = pack_half(jnp.concatenate([firsts, *ends_here], axis=0), True)

        copy_y.start()
        pl.semaphore_wait(open_sem, 1)
        copy_a.start()
        copy_b.start()

    only(mate, share_first_element)

    copy_m.wait_recv()
    both_models = recv_m[0:9]
    lam_mix = jnp.where(first_rows, both_models, lam[...])
    mu_mix = jnp.where(first_rows, turn(both_models, 4), mu[...])
    masses = recv_m[9:14]
    rho_mix = jnp.where(
        first_rows, jnp.concatenate([masses, turn(masses, 4)[0:4]], axis=0), rho[...]
    )
    lam_two, mu_two, rho_two = take(lam_mix, lam_mix), take(mu_mix, mu_mix), take(rho_mix, rho_mix)
    for place in range(4):
        weight = float(weights[place]) * element_weight
        muc[place] = mu_two[place] * weight
        lamc[place] = lam_two[place] * weight
        weight = 0.2 if place == 0 else float(weights[place])
        imc[place] = time_step / (rho_two[place] * (weight * (node_weight * lane_weight)))
    muw[4] = jnp.where(low4, muw[4], muc[4])
    lamw[4] = jnp.where(low4, lamw[4], lamc[4])
    for l in range(5):
        factors = numbers[:4, l] * numbers[:4, 4]
        mx[l] = combine(factors, [muc[p] for p in range(4)])
        px[l] = 2.0 * mx[l] + combine(factors, [lamc[p] for p in range(4)])
    ends = -time_step * combine(numbers[4, :4] ** 2, [imc[p] for p in range(4)])

    q = join(u[0], u[4])
    found = jnp.where(wide_low, gy[0], gy[4])

    def add_plane(q):
        shears = []
        for l in range(4):
            number = float(numbers[l, 4])
            shears.append(jnp.stack([muc[l] * q[2], lamc[l] * q[0]]) * number)
        around = back_rows(rows_of(jnp.stack(shears))).reshape(4, 2, 5, 8, lanes)
        for l in range(4):
            number = float(numbers[l, 4])
            up = level_back((number * muc[l]) * q[1])
            pre[l, 0] = middle_sum(px[l] * q[0] + around[l, 0] + up)
            pre[l, 1] = middle_sum(mx[l] * q[1] + level_back((number * lamc[l]) * q[0]))
            pre[l, 2] = middle_sum(mx[l] * q[2] + around[l, 1])
        for c in range(3):
            terms = [imc[l] * pre[l, c] for l in range(4)]
            fc[4, c] = -time_step * combine(numbers[4, :4], terms)

    add_plane(q)

    last, face = last_plane(q, *plane_grads(q, found, h[...]))
    for c in range(3):
        beyond = middle_sum(face[c])
        for place in range(4):
            change = imc[place] * (pre[place, c] + float(numbers[4, place]) * beyond)
            change = jnp.where(low4, 0.0, change)
            rate = b[place, c] - change
            b[place, c] = rate if place == 0 else rate + sm[place, c]
            un[place, c] = un[place, c] - time_step * change
    slopes(un, 1, 4)
    copy_b.wait_recv()
    later = unpack_half(recv_b[...], 20)
    for c in range(3):
        ahead = turn(later[5 * c : 5 * c + 5], 4) - turn(later[15:], 4) * (
            last[c] + f[4, c]
        )
        un[4, c] = jnp.where(low4, turn(un[0, c], 4), ahead)
    slopes(un, 4, 5)

    copy_p.wait_recv()
    packed = recv_p[...].reshape(3, 5, 8, lanes)
    first_grads = plane_grads(q, found, packed)
    last, face = last_plane(q, *first_grads)
    for c in range(3):
        force = last[c] + turn(packed[c], 4)
        change = jnp.where(low4, im[0] * force, 0.0)
        rate = b[0, c] - change
        b[0, c] = rate + sm[0, c]
        un[0, c] = un[0, c] - time_step * change
    slopes(un, 0, 1)
    kinds(un, 1)
    first_plane = middle_sum(kacc[0] + jnp.where(low4, 0.0, turn(kacc[4], 4)))
    nodes = swap_rows((first_plane, *[middle_sum(kacc[i]) for i in (1, 2, 3)]))
    for kind in range(2):
        whole = jnp.concatenate([nodes[2 * kind][0:4], nodes[2 * kind + 1]], axis=0)
        for owner in range(events):
            send_k[owner, kind] = whole[:, planes * owner : planes * owner + planes]
    copies = []
    for offset in range(1, events):
        partner = lax.rem(event + offset, events)
        copy = pltpu.make_async_remote_copy(
            src_ref=send_k.at[partner],
            dst_ref=recv_k.at[offset - 1],
            send_sem=sems_k.at[0, offset - 1],
            recv_sem=sems_k.at[1, offset - 1],
            device_id=(region, partner),
            device_id_type=MESH,
        )
        unless(mate, copy.start)
        copies.append(copy)

    edge_kinds = kinds_of(0.1 * element_weight, *first_grads)
    copy_d.wait_recv()
    coming = unpack_half(recv_d[...], 15).reshape(3, 5, 8, lanes)
    beyond = [middle_sum(face[c]) for c in range(3)]
    slope = [fc[4, c] + ends * beyond[c] + turn(coming[c], 4) for c in range(3)]
    second_grads = plane_grads(un[0], gy[0], slope)
    edge_kinds = middle_sum(edge_kinds + kinds_of(0.1 * element_weight, *second_grads))
    send_e[...] = pack_half(edge_kinds, True)
    slot = lax.max(event - 1, 0)
    copy_e = pltpu.make_async_remote_copy(
        src_ref=send_e,
        dst_ref=recv_e.at[slot],
        send_sem=sems_e.at[events - 1],
        recv_sem=sems_e.at[slot],
        device_id=(region, 0),
        device_id_type=MESH,
    )

    sends_share = jnp.logical_and(event > 0, jnp.logical_not(mate)) if pair_up else event > 0

    @pl.when(sends_share)
    def _():
        copy_e.start()

    for c in range(3):
        for l in range(4):
            change = pre[l, c] + float(numbers[4, l]) * beyond[c]
            g[l, c] = -time_step * (imc[l] * change)
    force = open_face(g, muc, lamc, face_means(g))
    last, _ = last_plane(un[0], *second_grads)
    copy_q.wait_recv()
    coming = unpack_half(recv_q[...], 15).reshape(3, 5, 8, lanes)
    fc[0] = last + force + turn(coming, 4)
    stresses(un)
    gather_forces(4, 0, 1, 2, 3)
    advance(un, un, 0, f[0] + join(fc[0], turn(f[4], 4)))
    for place in (1, 2, 3):
        advance(un, un, place, f[place])

    def give(state, forward_out, adjoint_out):
        for c in range(3):
            four = swap_rows((state[0, c], state[1, c], state[2, c], state[3, c]))
            forward_out[c] = jnp.concatenate([four[0][0:4], four[1]], axis=0)
            adjoint_out[c] = jnp.concatenate([four[2][0:4], four[3]], axis=0)

    give(un, uf_out, ua_out)
    give(b, vf_out, va_out)

    def first_share(value):
        nothing = jnp.zeros_like(value)
        parts = swap_rows((jnp.where(low4, value, 0.0), nothing, nothing, nothing))
        return [
            jnp.concatenate([parts[2 * kind][0:4], parts[2 * kind + 1]], axis=0)[:, 0:planes]
            for kind in range(2)
        ]

    own = first_share(unpack_half(send_e[...], 5))
    total = send_k[event]
    for kind in range(2):
        k_out[kind] = total[kind] + jnp.where(event == 0, own[kind], 0.0)

    def take_kernels():
        for offset in range(1, events):
            copies[offset - 1].wait_recv()
            k_out[...] = k_out[...] + recv_k[offset - 1]

    unless(lead, take_kernels)

    def meet_partner():
        copy_x.wait_recv()
        other = unpack_half(recv_x[...], 15).reshape(3, 5, 8, lanes)
        gy_two[0] = slope_rows(rows_of(other), 2 * lanes).reshape(3, 5, 8, 2 * lanes)
        copy_y.wait_recv()
        u_two[...] = unpack_half(recv_y[...], 75).reshape(5, 3, 5, 8, lanes)
        rows = slope_rows(rows_of(u_two[1:4]), 2 * lanes)
        gy_two[1:4] = rows.reshape(3, 3, 5, 8, 2 * lanes)

    def partner_kernels():
        meet_partner()
        other = unpack_half(recv_x[...], 15).reshape(3, 5, 8, lanes)
        add_plane(other)
        copy_pd.wait_recv()
        packed = recv_pd[...].reshape(3, 5, 8, lanes)
        grads_one = plane_grads(other, gy_two[0], packed)
        last, face = last_plane(other, *grads_one)
        for c in range(3):
            force = last[c] + turn(packed[c], 4)
            u_two[0, c] = u_two[0, c] - time_step * (im[0] * force)
        rows = slope_rows(rows_of(u_two[0]), 2 * lanes)
        gy_two[0] = rows.reshape(3, 5, 8, 2 * lanes)
        copy_z.wait_recv()
        kacc[0:4] = unpack_half(recv_z[...], 20).reshape(4, 5, 8, lanes)
        kinds(u_two, 1, gy_two, 4)
        copy_dd.wait_recv()
        coming = unpack_half(recv_dd[...], 15).reshape(3, 5, 8, lanes)
        slope = [fc[4, c] + ends * middle_sum(face[c]) + turn(coming[c], 4) for c in range(3)]
        grads_two = plane_grads(u_two[0], gy_two[0], slope)
        weight = 0.1 * element_weight
        share = kinds_of(weight, *grads_one) + kinds_of(weight, *grads_two)
        first = middle_sum(kacc[0] + share)
        nodes = swap_rows((first, *[middle_sum(kacc[i]) for i in (1, 2, 3)]))
        for kind in range(2):
            whole = jnp.concatenate([nodes[2 * kind][0:4], nodes[2 * kind + 1]], axis=0)
            k_out[kind] = k_out[kind] + whole[:, 0:planes]

    only(lead, partner_kernels)

    takes_share = jnp.logical_and(event == 0, jnp.logical_not(lead)) if pair_up else event == 0

    @pl.when(takes_share)
    def _():
        extra = None
        for other in range(events - 1):
            pltpu.make_async_copy(recv_e.at[other], recv_e.at[other], sems_e.at[other]).wait()
            share = unpack_half(recv_e[other], 5)
            extra = share if extra is None else extra + share
        parts = first_share(extra)
        for kind in range(2):
            k_out[kind] = k_out[kind] + parts[kind]

    @pl.when(sends_share)
    def _():
        copy_e.wait_send()

    for copy in [copy_a, copy_b, copy_m, copy_p, copy_d, copy_q]:
        copy.wait_send()

    def close_copies():
        for copy in copies:
            copy.wait_send()

    def close_mate():
        for copy in (copy_x, copy_y, copy_z):
            copy.wait_send()

    def close_giver():
        for copy in (copy_pd, copy_dd):
            copy.wait_send()

    unless(mate, close_copies)
    only(mate, close_mate)
    only(giver, close_giver)


def flush(*refs):
    sources, outs, sems = refs[:5], refs[5:10], refs[10]
    stores = [pltpu.make_async_copy(sources[n], outs[n], sems.at[n]) for n in range(5)]
    for store in stores:
        store.start()
    for store in stores:
        store.wait()


def run(regions, events, interpret, *arrays):
    lanes = arrays[0].shape[-1]
    fields = [jnp.transpose(array[0], (0, 2, 1, 3)) for array in arrays[:5]]
    models = [jnp.transpose(array, (1, 0, 2)) for array in arrays[5:]]
    tables = [jnp.asarray(table) for table in lane_tables(lanes)]
    operands = [*fields, *models, *tables]
    operands = [pltpu.with_memory_space_constraint(array, pltpu.HBM) for array in operands]
    planes = 8 // events
    state = jax.ShapeDtypeStruct((3, 9, 8, lanes), jnp.float32)
    f32 = jnp.float32
    vector = pltpu.VMEM((5, 3, 5, 8, lanes), f32)
    wide = pltpu.VMEM((5, 3, 5, 8, 2 * lanes), f32)
    scalar = pltpu.VMEM((5, 5, 8, lanes), f32)

    def packed(*lead):
        return pltpu.VMEM(lead + (8, lanes), f32)

    outs = pl.pallas_call(
        functools.partial(kernel, regions, events),
        out_shape=[state] * 4 + [jax.ShapeDtypeStruct((2, 9, planes, lanes), f32)],
        in_specs=[pl.BlockSpec(memory_space=pltpu.HBM)] * 12,
        out_specs=[pl.BlockSpec(memory_space=pltpu.VMEM)] * 5,
        scratch_shapes=[
            vector,
            vector,
            vector,
            vector,
            vector,
            scalar,
            scalar,
            scalar,
            wide,
            vector,
            wide,
            vector,
            vector,
            packed(3, 5),
            vector,
            scalar,
            scalar,
            scalar,
            scalar,
            scalar,
            scalar,
            packed(10),
            packed(10),
            packed(10),
            packed(10),
            packed(14),
            packed(14),
            packed(15),
            packed(15),
            packed(8),
            packed(8),
            packed(8),
            packed(8),
            packed(3),
            packed(max(events - 1, 1), 3),
            packed(8),
            packed(8),
            packed(38),
            packed(38),
            packed(10),
            packed(10),
            packed(15),
            packed(8),
            vector,
            wide,
            pltpu.SemaphoreType.DMA((2, 5)),
            pltpu.SemaphoreType.REGULAR,
            pltpu.VMEM((events, 2, 9, planes, lanes), f32),
            pltpu.VMEM((max(events - 1, 1), 2, 9, planes, lanes), f32),
            pltpu.SemaphoreType.DMA((2, 6)),
            pltpu.SemaphoreType.DMA((2, max(events - 1, 1))),
            pltpu.SemaphoreType.DMA((events,)),
            *[pltpu.VMEM(array.shape, array.dtype) for array in operands],
            pltpu.SemaphoreType.DMA((len(operands),)),
        ],
        compiler_params=pltpu.CompilerParams(
            collective_id=0, has_side_effects=True, vmem_limit_bytes=40 * 1024 * 1024
        ),
        name="adjoint_steps",
    )(*operands)
    shapes = [jax.ShapeDtypeStruct(out.shape, out.dtype) for out in outs]
    outs = pl.pallas_call(
        flush,
        out_shape=shapes,
        in_specs=[pl.BlockSpec(memory_space=pltpu.VMEM)] * 5,
        out_specs=[pl.BlockSpec(memory_space=pltpu.HBM)] * 5,
        scratch_shapes=[pltpu.SemaphoreType.DMA((5,))],
        compiler_params=pltpu.CompilerParams(vmem_limit_bytes=16 * 1024 * 1024),
        name="write_out",
    )(*outs)
    forward, forward_rate, adjoint, adjoint_rate = [
        jnp.transpose(out, (0, 2, 1, 3))[None] for out in outs[:4]
    ]
    return (forward, forward_rate, adjoint, adjoint_rate, jnp.transpose(outs[4], (0, 2, 1, 3)))


def solution(mesh):
    field = P("event", None, "region", None, None)
    model = P("region", None, None)
    regions, events = mesh.shape["region"], mesh.shape["event"]
    return jax.shard_map(
        functools.partial(run, regions, events, False),
        mesh=mesh,
        in_specs=(field,) * 5 + (model,) * 3,
        out_specs=(field,) * 4 + (P(None, ("region", "event"), None, None),),
        check_vma=False,
    )
```

```python
import functools
import math

import jax
import jax.numpy as jnp
import numpy as np
from jax import lax
from jax.experimental import pallas as pl
from jax.experimental.pallas import tpu as pltpu
from jax.sharding import PartitionSpec as P

STEPS = 2
time_step = 0.02
MESH = pl.DeviceIdType.MESH


def gll_numbers():
    points = np.array([-1.0, -math.sqrt(3.0 / 7.0), 0.0, math.sqrt(3.0 / 7.0), 1.0])
    weights = np.array([0.1, 49.0 / 90.0, 32.0 / 45.0, 49.0 / 90.0, 0.1])
    legendre = (35.0 * points**4 - 30.0 * points**2 + 3.0) / 8.0
    derivative = np.zeros((5, 5))
    for target in range(5):
        for column in range(5):
            if target != column:
                derivative[target, column] = legendre[target] / (
                    legendre[column] * (points[target] - points[column])
                )
    derivative[0, 0] = -5.0
    derivative[4, 4] = 5.0
    return (derivative, weights)


def lane_tables(lanes):
    numbers, _ = gll_numbers()
    table = np.zeros((lanes, 2 * lanes))
    for lane in range(lanes):
        start, local = lane - lane % 4, lane % 4
        for source in range(5):
            if local:
                table[(start + source) % lanes, lane] += numbers[local, source]
            else:
                right, left = (start + source) % lanes, (start - 4 + source) % lanes
                table[right, lane] += 0.5 * numbers[0, source]
                table[left, lane] += 0.5 * numbers[4, source]
                table[right, lanes + lane] += 0.5 * numbers[0, source]
                table[left, lanes + lane] -= 0.5 * numbers[4, source]
    high = table.astype(np.float32).astype(jnp.bfloat16)
    low = (table - high.astype(np.float64)).astype(np.float32).astype(jnp.bfloat16)
    return (
        np.concatenate([high, high], axis=0),
        low,
        np.concatenate([high.T, low.T], axis=1),
        np.ascontiguousarray(high.T),
    )


def combine(coefficients, pieces):
    total = None
    for number, piece in zip(coefficients, pieces):
        if number != 0.0:
            term = float(number) * piece
            total = term if total is None else total + term
    return total


def turn(value, shift):
    return pltpu.roll(value, shift % 8, value.ndim - 2)


def row_bit(shape, bit):
    return (lax.broadcasted_iota(jnp.int32, shape, len(shape) - 2) & bit) == 0


def swap_rows(four):
    shape = four[0].shape
    low_two, low_one = row_bit(shape, 2), row_bit(shape, 1)
    a0, a1, a2, a3 = four
    b0 = jnp.where(low_two, a0, turn(a2, 2))
    b2 = jnp.where(low_two, turn(a0, -2), a2)
    b1 = jnp.where(low_two, a1, turn(a3, 2))
    b3 = jnp.where(low_two, turn(a1, -2), a3)
    return (
        jnp.where(low_one, b0, turn(b1, 1)),
        jnp.where(low_one, turn(b0, -1), b1),
        jnp.where(low_one, b2, turn(b3, 1)),
        jnp.where(low_one, turn(b2, -1), b3),
    )


def middle_sum(blocks):
    first, last = blocks[..., 0, :, :], blocks[..., 4, :, :]
    low = row_bit(first.shape, 1)
    new_last = last + jnp.where(low, turn(first, -1), 0.0)
    new_first = first + jnp.where(low, 0.0, turn(last, 1))
    return jnp.concatenate(
        [new_first[..., None, :, :], blocks[..., 1:4, :, :], new_last[..., None, :, :]], axis=-3
    )


def pack_half(blocks, low):
    half = (blocks.shape[0] + 1) // 2
    first, second = blocks[:half], blocks[half:]
    if second.shape[0] < half:
        second = jnp.concatenate([second, first[-1:]], axis=0)
    keep = row_bit(first.shape, 4)
    other = turn(second, 4)
    return jnp.where(keep, first, other) if low else jnp.where(keep, other, first)


def unpack_half(packed, count):
    return jnp.concatenate([packed, turn(packed, 4)], axis=0)[:count]


def kernel(
    regions,
    events,
    uf_in,
    vf_in,
    ua_in,
    va_in,
    source_in,
    lam_in,
    mu_in,
    rho_in,
    slope_two_in,
    slope_low_in,
    back_two_in,
    back_high_in,
    uf_out,
    vf_out,
    ua_out,
    va_out,
    k_out,
    u,
    un,
    g,
    b,
    sm,
    im,
    muw,
    lamw,
    gy,
    sx,
    sy,
    f,
    fc,
    h,
    pre,
    kacc,
    imc,
    muc,
    lamc,
    px,
    mx,
    send_a,
    recv_a,
    send_b,
    recv_b,
    send_m,
    recv_m,
    send_p,
    recv_p,
    send_d,
    recv_d,
    send_q,
    recv_q,
    send_e,
    recv_e,
    send_x,
    recv_x,
    send_y,
    recv_y,
    send_w,
    recv_w,
    send_z,
    recv_z,
    recv_pd,
    recv_dd,
    u_two,
    gy_two,
    sems_y,
    open_sem,
    send_k,
    recv_k,
    sems,
    sems_k,
    sems_e,
    uf,
    vf,
    ua,
    va,
    source,
    lam,
    mu,
    rho,
    slope_two,
    slope_low,
    back_two,
    back_high,
    load_sems,
):
    numbers, weights = gll_numbers()
    lanes = u.shape[-1]
    region, event = lax.axis_index("region"), lax.axis_index("event")
    left, right = lax.rem(region + regions - 1, regions), lax.rem(region + 1, regions)
    planes = 8 // events
    corner = float(numbers[4, 4])
    pair_up = events == 2
    lead = jnp.logical_and(region == 0, event == 0)
    mate = jnp.logical_and(region == 0, event == 1)
    giver = jnp.logical_and(region == regions - 1, event == 1)
    keeper = jnp.logical_and(region == regions - 1, event == 0)

    def only(condition, action):
        if pair_up:
            pl.when(condition)(action)

    def unless(condition, action):
        if pair_up:
            pl.when(jnp.logical_not(condition))(action)
        else:
            action()

    barrier = pltpu.get_barrier_semaphore()
    def greet(side, other):
        pl.semaphore_signal(barrier, inc=1, device_id=(side, other), device_id_type=MESH)

    greet(left, event)
    unless(giver, lambda: greet(right, event))
    only(lead, lambda: greet(left, 1))
    for offset in range(1, events):
        partner = lax.rem(event + offset, events)
        unless(giver, functools.partial(greet, region, partner))

    loads = {}
    for number, (name, src, dst) in enumerate(
        (
            ("uf", uf_in, uf),
            ("ua", ua_in, ua),
            ("lam", lam_in, lam),
            ("mu", mu_in, mu),
            ("slope_two", slope_two_in, slope_two),
            ("slope_low", slope_low_in, slope_low),
            ("rho", rho_in, rho),
            ("back_two", back_two_in, back_two),
            ("back_high", back_high_in, back_high),
            ("vf", vf_in, vf),
            ("va", va_in, va),
            ("source", source_in, source),
        )
    ):
        loads[name] = pltpu.make_async_copy(src, dst, load_sems.at[number])
        if number < 7:
            loads[name].start()

    def ready(*names):
        for name in names:
            loads[name].wait()

    def remote(src, dst, number, target):
        return pltpu.make_async_remote_copy(
            src_ref=src,
            dst_ref=dst,
            send_sem=sems.at[0, number],
            recv_sem=sems.at[1, number],
            device_id=target,
            device_id_type=MESH,
        )

    def aside(src, dst, number, target):
        return pltpu.make_async_remote_copy(
            src_ref=src,
            dst_ref=dst,
            send_sem=sems_y.at[0, number],
            recv_sem=sems_y.at[1, number],
            device_id=target,
            device_id_type=MESH,
        )

    copy_x = aside(send_x, recv_x, 0, (region, 0))
    copy_y = aside(send_y, recv_y, 1, (region, 0))
    copy_z = aside(send_z, recv_z, 2, (region, 0))
    copy_w = aside(send_w, recv_w, 5, (region, 0))
    copy_pd = aside(send_p, recv_pd, 3, (right, 0))
    copy_dd = aside(send_d, recv_dd, 4, (right, 0))
    copy_a = remote(send_a, recv_a, 0, (left, event))
    copy_b = remote(send_b, recv_b, 1, (left, event))
    copy_m = remote(send_m, recv_m, 2, (right, event))
    copy_p = remote(send_p, recv_p, 3, (right, event))
    copy_d = remote(send_d, recv_d, 4, (right, event))
    copy_q = remote(send_q, recv_q, 5, (right, event))

    one = (5, 8, lanes)
    low4, low2, low1 = row_bit(one, 4), row_bit(one, 2), row_bit(one, 1)
    low4_all = row_bit((3,) + one, 4)
    lane_place = lax.broadcasted_iota(jnp.int32, one, 2) & 3
    lane_weight = jnp.where(
        lane_place == 0, 0.2, jnp.where(lane_place == 2, 32.0 / 45.0, 49.0 / 90.0)
    ).astype(jnp.float32)
    level = lax.broadcasted_iota(jnp.int32, one, 0)
    edge = (level == 0) | (level == 4)
    inner = jnp.where(level == 2, 32.0 / 45.0, 49.0 / 90.0)
    level_weight = jnp.where(edge, 0.1, inner).astype(jnp.float32)
    closed = ((level == 0) & low1) | ((level == 4) & jnp.logical_not(low1))
    node_weight = jnp.where(edge, jnp.where(closed, 0.1, 0.2), inner).astype(jnp.float32)
    element_weight = level_weight * lane_weight

    def take(first, second):
        return swap_rows((first[0:5], first[4:9], second[0:5], second[4:9]))

    def join(low, high):
        return jnp.where(low4_all, low, high)

    def rows_of(value):
        return value.reshape(-1, lanes)

    def split(values):
        high = values.astype(jnp.bfloat16)
        low = (values - high.astype(jnp.float32)).astype(jnp.bfloat16)
        return high, low

    def slope_rows(values, columns):
        high, low = split(values)
        return jnp.dot(
            jnp.concatenate([high, low], axis=1),
            slope_two[:, :columns],
            preferred_element_type=jnp.float32,
        ) + jnp.dot(high, slope_low[:, :columns], preferred_element_type=jnp.float32)

    def back_rows(values):
        deep = values.shape[1]
        high, low = split(values)
        first = jnp.dot(high, back_two[:deep], preferred_element_type=jnp.float32)
        total = first[:, :lanes] + first[:, lanes:]
        return total + jnp.dot(low, back_high[:deep], preferred_element_type=jnp.float32)

    def level_slopes(levels):
        return jnp.stack([combine(numbers[k], levels) for k in range(5)])

    def level_back(stress):
        levels = [stress[q] for q in range(5)]
        return jnp.stack([combine(numbers[:, k], levels) for k in range(5)])

    def slopes(src, begin, end):
        found = slope_rows(rows_of(src[begin:end]), 2 * lanes)
        gy[begin:end] = found.reshape(end - begin, 3, 5, 8, 2 * lanes)

    def product(value):
        return value * turn(value, -2)

    def kinds_of(weight, gx, gz, gm, gd):
        xz, xy, zy = gx[1] + gz[0], gx[2] + gm[0], gz[2] + gm[1]
        jump = product(gd[2])
        k1 = weight * (product(gx[0] + gz[1] + gm[2]) + jump)
        shear = product(gx[0]) + product(gz[1]) + product(gm[2]) + jump
        cross = product(xz) + product(xy) + product(zy) + product(gd[0]) + product(gd[1])
        k2 = weight * (2.0 * shear + cross)
        return jnp.where(low2, k1, turn(k2, 2))

    def store_stress(i, m, l, gx, gz, gm, gd):
        xz, xy, zy = gx[1] + gz[0], gx[2] + gm[0], gz[2] + gm[1]
        both = m + m
        press = l * (gx[0] + gz[1] + gm[2])
        s_xz, s_xy, s_zy = m * xz, m * xy, m * zy
        sx[i, 0] = both * gx[0] + press
        sx[i, 1] = s_xz
        sx[i, 2] = s_xy
        sy[i, 0, :, :, :lanes] = s_xy
        sy[i, 1, :, :, :lanes] = s_zy
        sy[i, 2, :, :, :lanes] = both * gm[2] + press
        sy[i, 0, :, :, lanes:] = m * gd[0]
        sy[i, 1, :, :, lanes:] = m * gd[1]
        sy[i, 2, :, :, lanes:] = (both + l) * gd[2]
        for c, stress in enumerate((s_xz, both * gz[1] + press, s_zy)):
            f[i, c] = level_back(stress)

    def grads(src, i, gy=gy):
        gx = [combine(numbers[i], [src[q, c] for q in range(5)]) for c in range(3)]
        gz = [level_slopes([src[i, c, q] for q in range(5)]) for c in range(3)]
        gm = [gy[i, c, :, :, :lanes] for c in range(3)]
        gd = [gy[i, c, :, :, lanes:] for c in range(3)]
        return gx, gz, gm, gd

    def stresses(src):
        for i in range(5):
            store_stress(i, muw[i], lamw[i], *grads(src, i))

    def kinds(src, step, gy=gy, last=5):
        for i in range(last):
            found = kinds_of(float(weights[i]) * element_weight, *grads(src, i, gy))
            kacc[i] = found if step == 0 else kacc[i] + found

    def gather_forces(*places):
        for i in places:
            total = back_rows(sy[i].reshape(120, 2 * lanes)).reshape(3, 5, 8, lanes)
            for c in range(3):
                value = f[i, c] + total[c] + combine(numbers[:, i], [sx[p, c] for p in range(5)])
                f[i, c] = middle_sum(value)

    def open_slope(src):
        return jnp.stack([combine(numbers[4, :4], [src[q, c] for q in range(4)]) for c in range(3)])

    def open_face(src, m, l, means):
        faces = []
        for p in range(4):
            gx = [combine(numbers[p, :4], [src[q, c] for q in range(4)]) for c in range(3)]
            gz = [level_slopes([src[p, c, q] for q in range(5)]) for c in range(2)]
            press = l[p] * (gx[0] + gz[1] + means(p, 2))
            faces.append(
                (
                    (m[p] + m[p]) * gx[0] + press,
                    m[p] * (gx[1] + gz[0]),
                    m[p] * (gx[2] + means(p, 0)),
                )
            )
        return jnp.stack(
            [middle_sum(combine(numbers[:4, 4], [faces[p][c] for p in range(4)])) for c in range(3)]
        )

    def face_means(src):
        rows = jnp.concatenate([rows_of(src[0:4, 0]), rows_of(src[0:4, 2])], axis=0)
        means = slope_rows(rows, lanes).reshape(2, 4, 5, 8, lanes)
        return lambda p, c: means[c // 2, p]

    def held_means(p, c):
        return gy[p, c, :, :, :lanes]

    def plane_grads(q, found, slope):
        gx = [slope[c] + corner * q[c] for c in range(3)]
        gz = [level_slopes([q[c, k] for k in range(5)]) for c in range(3)]
        gm = [found[c, :, :, :lanes] for c in range(3)]
        gd = [found[c, :, :, lanes:] for c in range(3)]
        return gx, gz, gm, gd

    def last_plane(q, gx, gz, gm, gd):
        m, l = muc[4], lamc[4]
        xz, xy, zy = gx[1] + gz[0], gx[2] + gm[0], gz[2] + gm[1]
        both = m + m
        press = l * (gx[0] + gz[1] + gm[2])
        s_xz, s_xy, s_zy = m * xz, m * xy, m * zy
        face = (both * gx[0] + press, s_xz, s_xy)
        mean = jnp.stack([s_xy, s_zy, both * gm[2] + press])
        half = jnp.stack([m * gd[0], m * gd[1], (both + l) * gd[2]])
        total = back_rows(
            jnp.concatenate([rows_of(mean), rows_of(half)], axis=1)
        ).reshape(3, 5, 8, lanes)
        inner_face = (px[4] * q[0], mx[4] * q[1], mx[4] * q[2])
        up = (s_xz, both * gz[1] + press, s_zy)
        result = [
            middle_sum(total[c] + inner_face[c] + corner * face[c] + level_back(up[c]))
            for c in range(3)
        ]
        return jnp.stack(result), face

    ready("uf", "ua")
    for comp in range(3):
        for place, value in enumerate(take(uf[comp], ua[comp])):
            u[place, comp] = value
    ready("lam", "mu", "rho")
    first_rows = row_bit((9, 8, lanes), 4)
    send_m[0:9] = jnp.where(first_rows, turn(lam[...], 4), mu[...])
    five = jnp.concatenate([rho[5:9], rho[8:9]], axis=0)
    send_m[9:14] = jnp.where(low4, turn(rho[0:5], 4), five)
    ready("slope_two", "slope_low")
    for name in ("back_two", "back_high", "vf", "va", "source"):
        loads[name].start()
    fewer = jnp.logical_or(mate, keeper)
    peers = jnp.where(fewer, events, jnp.where(giver, events + 2, events + 1))

    def enter():
        pl.semaphore_wait(barrier, peers if pair_up else events + 1)
        unless(giver, copy_m.start)

    def open_left():
        pl.semaphore_signal(open_sem, inc=1, device_id=(right, event), device_id_type=MESH)
        pl.semaphore_signal(open_sem, inc=1, device_id=(region, 0), device_id_type=MESH)

    unless(lead, enter)
    only(giver, open_left)
    slopes(u, 0, 4)
    lam_here, mu_here = take(lam[...], lam[...]), take(mu[...], mu[...])
    for place in range(4):
        weight = float(weights[place]) * element_weight
        muw[place] = mu_here[place] * weight
        lamw[place] = lam_here[place] * weight
    h[...] = open_slope(u)
    opened = open_face(u, muw, lamw, held_means)
    send_p[...] = pack_half(
        jnp.concatenate([opened.reshape(15, 8, lanes), h[...].reshape(15, 8, lanes)], axis=0), False
    )

    def give_twice():
        copy_pd.start()
        copy_m.start()

    only(giver, give_twice)
    unless(jnp.logical_or(lead, giver), copy_p.start)
    edge_pair = jnp.where(low2, mu_here[0], lam_here[0])
    send_a[...] = pack_half(
        jnp.concatenate([u[0].reshape(15, 8, lanes), edge_pair], axis=0), True
    )

    def share_first_plane():
        send_x[...] = pack_half(u[0].reshape(15, 8, lanes), True)
        copy_x.start()

    unless(region == 0, copy_a.start)
    only(mate, share_first_plane)

    u[4] = join(turn(u[0], 4), 0.0)
    wide_low = row_bit((3, 5, 8, 2 * lanes), 4)
    gy[4] = jnp.where(wide_low, turn(gy[0], 4), 0.0)
    muw[4] = jnp.where(low4, turn(mu_here[0], 4) * (0.1 * element_weight), 0.0)
    lamw[4] = jnp.where(low4, turn(lam_here[0], 4) * (0.1 * element_weight), 0.0)
    stresses(u)
    ready("back_two", "back_high")
    gather_forces(4, 0)

    rho_here = take(rho[...], rho[...])
    for place in range(4):
        weight = 0.2 if place == 0 else float(weights[place])
        im[place] = time_step / (rho_here[place] * (weight * (node_weight * lane_weight)))
    ready("vf", "va", "source")
    for comp in range(3):
        rates = take(vf[comp], va[comp])
        sources = take(jnp.zeros_like(source[comp]), source[comp])
        for place in range(4):
            pushed = sources[place] * im[place]
            sm[place, comp] = pushed
            b[place, comp] = rates[place] + pushed

    def advance(src, dst, place, force):
        for c in range(3):
            rate = b[place, c] - im[place] * force[c]
            b[place, c] = rate
            dst[place, c] = src[place, c] + time_step * rate

    advance(u, un, 0, f[0] + join(0.0, turn(f[4], 4)))
    send_b[...] = pack_half(
        jnp.concatenate([un[0].reshape(15, 8, lanes), time_step * im[0]], axis=0), True
    )
    unless(region == 0, copy_b.start)
    gather_forces(1, 2, 3)
    for place in (1, 2, 3):
        advance(u, un, place, f[place])

    def share_planes():
        send_y[...] = pack_half(un[0:4].reshape(60, 8, lanes), True)
        copy_y.start()

    only(mate, share_planes)
    send_d[...] = pack_half(open_slope(un).reshape(15, 8, lanes), False)

    def give_slope_twice():
        copy_dd.start()
        copy_p.start()

    only(giver, give_slope_twice)
    unless(lead, copy_d.start)
    send_q[...] = pack_half(
        open_face(un, muw, lamw, face_means(un)).reshape(15, 8, lanes), False
    )
    unless(lead, copy_q.start)

    def enter_late():
        pl.semaphore_wait(barrier, events + 1)
        for copy in (copy_a, copy_b, copy_m, copy_p, copy_d, copy_q):
            copy.start()

    copy_a.wait_recv()
    arrived = unpack_half(recv_a[...], 20)
    u[4] = join(u[4], turn(arrived[:15].reshape(3, 5, 8, lanes), 4))
    slopes(u, 4, 5)
    kinds(u, 0)
    pair = arrived[15:]
    mu_next, lam_next = jnp.where(low2, pair, turn(pair, 2)), jnp.where(low2, turn(pair, -2), pair)
    weight = 0.1 * element_weight
    muc[4] = jnp.where(low4, mu_here[0], turn(mu_next, 4)) * weight
    lamc[4] = jnp.where(low4, lam_here[0], turn(lam_next, 4)) * weight

    def share_first_element():
        far, m, l = u[4], muw, lamw
        factors = numbers[:4, 0] * numbers[:4, 4]
        m_face = combine(factors, [m[p] for p in range(4)])
        l_face = 2.0 * m_face + combine(factors, [l[p] for p in range(4)])
        number = float(numbers[0, 4])
        m_one, l_one = m[0] * number, l[0] * number
        rows = rows_of(jnp.stack([m_one * far[2], l_one * far[0]]))
        across = back_rows(rows).reshape(2, 5, 8, lanes)
        gx, gz, gm, _ = plane_grads(far, gy[4], h[...])
        m_last, l_last = muc[4], lamc[4]
        face = (
            (m_last + m_last) * gx[0] + l_last * (gx[0] + gz[1] + gm[2]),
            m_last * (gx[1] + gz[0]),
            m_last * (gx[2] + gm[0]),
        )
        inside = (
            l_face * far[0] + across[0] + level_back(m_one * far[1]),
            m_face * far[1] + level_back(l_one * far[0]),
            m_face * far[2] + across[1],
        )
        ends_here = []
        for c in range(3):
            force = middle_sum(inside[c] + float(numbers[4, 0]) * face[c])
            ends_here.append(turn(un[0, c] - time_step * (im[0] * force), 4))
        send_w[...] = pack_half(jnp.concatenate(ends_here, axis=0), True)
        copy_w.start()
        send_z[...] = pack_half(kacc[0:4].reshape(20, 8, lanes), True)
        copy_z.start()
        pl.semaphore_wait(open_sem, 1)
        copy_a.start()
        copy_b.start()

    only(mate, share_first_element)
    only(lead, enter_late)

    copy_m.wait_recv()
    both_models = recv_m[0:9]
    lam_mix = jnp.where(first_rows, both_models, lam[...])
    mu_mix = jnp.where(first_rows, turn(both_models, 4), mu[...])
    masses = recv_m[9:14]
    rho_mix = jnp.where(
        first_rows, jnp.concatenate([masses, turn(masses, 4)[0:4]], axis=0), rho[...]
    )
    lam_two, mu_two, rho_two = take(lam_mix, lam_mix), take(mu_mix, mu_mix), take(rho_mix, rho_mix)
    for place in range(4):
        weight = float(weights[place]) * element_weight
        muc[place] = mu_two[place] * weight
        lamc[place] = lam_two[place] * weight
        weight = 0.2 if place == 0 else float(weights[place])
        imc[place] = time_step / (rho_two[place] * (weight * (node_weight * lane_weight)))
    muw[4] = jnp.where(low4, muw[4], muc[4])
    lamw[4] = jnp.where(low4, lamw[4], lamc[4])
    for l in range(5):
        factors = numbers[:4, l] * numbers[:4, 4]
        mx[l] = combine(factors, [muc[p] for p in range(4)])
        px[l] = 2.0 * mx[l] + combine(factors, [lamc[p] for p in range(4)])
    ends = -time_step * combine(numbers[4, :4] ** 2, [imc[p] for p in range(4)])

    q = join(u[0], u[4])
    found = jnp.where(wide_low, gy[0], gy[4])

    def add_plane(q):
        shears = []
        for l in range(4):
            number = float(numbers[l, 4])
            shears.append(jnp.stack([muc[l] * q[2], lamc[l] * q[0]]) * number)
        around = back_rows(rows_of(jnp.stack(shears))).reshape(4, 2, 5, 8, lanes)
        for l in range(4):
            number = float(numbers[l, 4])
            up = level_back((number * muc[l]) * q[1])
            pre[l, 0] = middle_sum(px[l] * q[0] + around[l, 0] + up)
            pre[l, 1] = middle_sum(mx[l] * q[1] + level_back((number * lamc[l]) * q[0]))
            pre[l, 2] = middle_sum(mx[l] * q[2] + around[l, 1])
        for c in range(3):
            terms = [imc[l] * pre[l, c] for l in range(4)]
            fc[4, c] = -time_step * combine(numbers[4, :4], terms)

    add_plane(q)

    last, face = last_plane(q, *plane_grads(q, found, h[...]))
    for c in range(3):
        beyond = middle_sum(face[c])
        for place in range(4):
            change = imc[place] * (pre[place, c] + float(numbers[4, place]) * beyond)
            change = jnp.where(low4, 0.0, change)
            rate = b[place, c] - change
            b[place, c] = rate if place == 0 else rate + sm[place, c]
            un[place, c] = un[place, c] - time_step * change
    slopes(un, 1, 4)
    copy_b.wait_recv()
    later = unpack_half(recv_b[...], 20)
    for c in range(3):
        ahead = turn(later[5 * c : 5 * c + 5], 4) - turn(later[15:], 4) * (
            last[c] + f[4, c]
        )
        un[4, c] = jnp.where(low4, turn(un[0, c], 4), ahead)
    slopes(un, 4, 5)

    copy_p.wait_recv()
    packed = recv_p[...].reshape(3, 5, 8, lanes)
    first_grads = plane_grads(q, found, packed)
    last, face = last_plane(q, *first_grads)
    for c in range(3):
        force = last[c] + turn(packed[c], 4)
        change = jnp.where(low4, im[0] * force, 0.0)
        rate = b[0, c] - change
        b[0, c] = rate + sm[0, c]
        un[0, c] = un[0, c] - time_step * change
    slopes(un, 0, 1)
    kinds(un, 1)
    first_plane = middle_sum(kacc[0] + jnp.where(low4, 0.0, turn(kacc[4], 4)))
    nodes = swap_rows((first_plane, *[middle_sum(kacc[i]) for i in (1, 2, 3)]))
    for kind in range(2):
        whole = jnp.concatenate([nodes[2 * kind][0:4], nodes[2 * kind + 1]], axis=0)
        for owner in range(events):
            send_k[owner, kind] = whole[:, planes * owner : planes * owner + planes]
    copies = []
    for offset in range(1, events):
        partner = lax.rem(event + offset, events)
        copy = pltpu.make_async_remote_copy(
            src_ref=send_k.at[partner],
            dst_ref=recv_k.at[offset - 1],
            send_sem=sems_k.at[0, offset - 1],
            recv_sem=sems_k.at[1, offset - 1],
            device_id=(region, partner),
            device_id_type=MESH,
        )
        only(keeper, lambda: pl.semaphore_wait(open_sem, 1))
        unless(mate, copy.start)
        copies.append(copy)

    edge_kinds = kinds_of(0.1 * element_weight, *first_grads)
    copy_d.wait_recv()
    coming = unpack_half(recv_d[...], 15).reshape(3, 5, 8, lanes)
    beyond = [middle_sum(face[c]) for c in range(3)]
    slope = [fc[4, c] + ends * beyond[c] + turn(coming[c], 4) for c in range(3)]
    second_grads = plane_grads(un[0], gy[0], slope)
    edge_kinds = middle_sum(edge_kinds + kinds_of(0.1 * element_weight, *second_grads))
    send_e[...] = pack_half(edge_kinds, True)
    slot = lax.max(event - 1, 0)
    copy_e = pltpu.make_async_remote_copy(
        src_ref=send_e,
        dst_ref=recv_e.at[slot],
        send_sem=sems_e.at[events - 1],
        recv_sem=sems_e.at[slot],
        device_id=(region, 0),
        device_id_type=MESH,
    )

    sends_share = jnp.logical_and(event > 0, jnp.logical_not(mate)) if pair_up else event > 0

    @pl.when(sends_share)
    def _():
        copy_e.start()

    for c in range(3):
        for l in range(4):
            change = pre[l, c] + float(numbers[4, l]) * beyond[c]
            g[l, c] = -time_step * (imc[l] * change)
    force = open_face(g, muc, lamc, face_means(g))
    last, _ = last_plane(un[0], *second_grads)
    copy_q.wait_recv()
    coming = unpack_half(recv_q[...], 15).reshape(3, 5, 8, lanes)
    fc[0] = last + force + turn(coming, 4)
    stresses(un)
    gather_forces(4, 0, 1, 2, 3)
    advance(un, un, 0, f[0] + join(fc[0], turn(f[4], 4)))
    for place in (1, 2, 3):
        advance(un, un, place, f[place])

    def give(state, forward_out, adjoint_out):
        for c in range(3):
            four = swap_rows((state[0, c], state[1, c], state[2, c], state[3, c]))
            forward_out[c] = jnp.concatenate([four[0][0:4], four[1]], axis=0)
            adjoint_out[c] = jnp.concatenate([four[2][0:4], four[3]], axis=0)

    give(un, uf_out, ua_out)
    give(b, vf_out, va_out)

    def first_share(value):
        nothing = jnp.zeros_like(value)
        parts = swap_rows((jnp.where(low4, value, 0.0), nothing, nothing, nothing))
        return [
            jnp.concatenate([parts[2 * kind][0:4], parts[2 * kind + 1]], axis=0)[:, 0:planes]
            for kind in range(2)
        ]

    own = first_share(unpack_half(send_e[...], 5))
    total = send_k[event]
    for kind in range(2):
        k_out[kind] = total[kind] + jnp.where(event == 0, own[kind], 0.0)

    def take_kernels():
        for offset in range(1, events):
            copies[offset - 1].wait_recv()
            k_out[...] = k_out[...] + recv_k[offset - 1]

    unless(lead, take_kernels)

    def meet_partner():
        copy_x.wait_recv()
        other = unpack_half(recv_x[...], 15).reshape(3, 5, 8, lanes)
        gy_two[0] = slope_rows(rows_of(other), 2 * lanes).reshape(3, 5, 8, 2 * lanes)
        copy_y.wait_recv()
        u_two[0:4] = unpack_half(recv_y[...], 60).reshape(4, 3, 5, 8, lanes)
        rows = slope_rows(rows_of(u_two[1:4]), 2 * lanes)
        gy_two[1:4] = rows.reshape(3, 3, 5, 8, 2 * lanes)

    def partner_kernels():
        meet_partner()
        other = unpack_half(recv_x[...], 15).reshape(3, 5, 8, lanes)
        add_plane(other)
        copy_pd.wait_recv()
        packed = recv_pd[...].reshape(3, 5, 8, lanes)
        grads_one = plane_grads(other, gy_two[0], packed)
        last, face = last_plane(other, *grads_one)
        for c in range(3):
            force = last[c] + turn(packed[c], 4)
            u_two[0, c] = u_two[0, c] - time_step * (im[0] * force)
        rows = slope_rows(rows_of(u_two[0]), 2 * lanes)
        gy_two[0] = rows.reshape(3, 5, 8, 2 * lanes)
        copy_w.wait_recv()
        u_two[4] = unpack_half(recv_w[...], 15).reshape(3, 5, 8, lanes)
        copy_z.wait_recv()
        kacc[0:4] = unpack_half(recv_z[...], 20).reshape(4, 5, 8, lanes)
        kinds(u_two, 1, gy_two, 4)
        weight = 0.1 * element_weight
        share = kinds_of(weight, *grads_one)
        first = middle_sum(kacc[0] + share)
        nodes = swap_rows((first, *[middle_sum(kacc[i]) for i in (1, 2, 3)]))
        for kind in range(2):
            whole = jnp.concatenate([nodes[2 * kind][0:4], nodes[2 * kind + 1]], axis=0)
            k_out[kind] = k_out[kind] + whole[:, 0:planes]
        copy_dd.wait_recv()
        coming = unpack_half(recv_dd[...], 15).reshape(3, 5, 8, lanes)
        slope = [fc[4, c] + ends * middle_sum(face[c]) + turn(coming[c], 4) for c in range(3)]
        grads_two = plane_grads(u_two[0], gy_two[0], slope)
        parts = first_share(middle_sum(kinds_of(weight, *grads_two)))
        for kind in range(2):
            k_out[kind] = k_out[kind] + parts[kind]

    only(lead, partner_kernels)

    takes_share = jnp.logical_and(event == 0, jnp.logical_not(lead)) if pair_up else event == 0

    @pl.when(takes_share)
    def _():
        extra = None
        for other in range(events - 1):
            pltpu.make_async_copy(recv_e.at[other], recv_e.at[other], sems_e.at[other]).wait()
            share = unpack_half(recv_e[other], 5)
            extra = share if extra is None else extra + share
        parts = first_share(extra)
        for kind in range(2):
            k_out[kind] = k_out[kind] + parts[kind]

    @pl.when(sends_share)
    def _():
        copy_e.wait_send()

    for copy in [copy_a, copy_b, copy_m, copy_p, copy_d, copy_q]:
        copy.wait_send()

    def close_copies():
        for copy in copies:
            copy.wait_send()

    def close_mate():
        for copy in (copy_x, copy_y, copy_w, copy_z):
            copy.wait_send()

    def close_giver():
        for copy in (copy_pd, copy_dd):
            copy.wait_send()

    unless(mate, close_copies)
    only(mate, close_mate)
    only(giver, close_giver)


def flush(*refs):
    sources, outs, sems = refs[:5], refs[5:10], refs[10]
    stores = [pltpu.make_async_copy(sources[n], outs[n], sems.at[n]) for n in range(5)]
    for store in stores:
        store.start()
    for store in stores:
        store.wait()


def run(regions, events, interpret, *arrays):
    lanes = arrays[0].shape[-1]
    fields = [jnp.transpose(array[0], (0, 2, 1, 3)) for array in arrays[:5]]
    models = [jnp.transpose(array, (1, 0, 2)) for array in arrays[5:]]
    tables = [jnp.asarray(table) for table in lane_tables(lanes)]
    operands = [*fields, *models, *tables]
    operands = [pltpu.with_memory_space_constraint(array, pltpu.HBM) for array in operands]
    planes = 8 // events
    state = jax.ShapeDtypeStruct((3, 9, 8, lanes), jnp.float32)
    f32 = jnp.float32
    vector = pltpu.VMEM((5, 3, 5, 8, lanes), f32)
    wide = pltpu.VMEM((5, 3, 5, 8, 2 * lanes), f32)
    scalar = pltpu.VMEM((5, 5, 8, lanes), f32)

    def packed(*lead):
        return pltpu.VMEM(lead + (8, lanes), f32)

    outs = pl.pallas_call(
        functools.partial(kernel, regions, events),
        out_shape=[state] * 4 + [jax.ShapeDtypeStruct((2, 9, planes, lanes), f32)],
        in_specs=[pl.BlockSpec(memory_space=pltpu.HBM)] * 12,
        out_specs=[pl.BlockSpec(memory_space=pltpu.VMEM)] * 5,
        scratch_shapes=[
            vector,
            vector,
            vector,
            vector,
            vector,
            scalar,
            scalar,
            scalar,
            wide,
            vector,
            wide,
            vector,
            vector,
            packed(3, 5),
            vector,
            scalar,
            scalar,
            scalar,
            scalar,
            scalar,
            scalar,
            packed(10),
            packed(10),
            packed(10),
            packed(10),
            packed(14),
            packed(14),
            packed(15),
            packed(15),
            packed(8),
            packed(8),
            packed(8),
            packed(8),
            packed(3),
            packed(max(events - 1, 1), 3),
            packed(8),
            packed(8),
            packed(30),
            packed(30),
            packed(8),
            packed(8),
            packed(10),
            packed(10),
            packed(15),
            packed(8),
            vector,
            wide,
            pltpu.SemaphoreType.DMA((2, 6)),
            pltpu.SemaphoreType.REGULAR,
            pltpu.VMEM((events, 2, 9, planes, lanes), f32),
            pltpu.VMEM((max(events - 1, 1), 2, 9, planes, lanes), f32),
            pltpu.SemaphoreType.DMA((2, 6)),
            pltpu.SemaphoreType.DMA((2, max(events - 1, 1))),
            pltpu.SemaphoreType.DMA((events,)),
            *[pltpu.VMEM(array.shape, array.dtype) for array in operands],
            pltpu.SemaphoreType.DMA((len(operands),)),
        ],
        compiler_params=pltpu.CompilerParams(
            collective_id=0, has_side_effects=True, vmem_limit_bytes=40 * 1024 * 1024
        ),
        name="adjoint_steps",
    )(*operands)
    shapes = [jax.ShapeDtypeStruct(out.shape, out.dtype) for out in outs]
    outs = pl.pallas_call(
        flush,
        out_shape=shapes,
        in_specs=[pl.BlockSpec(memory_space=pltpu.VMEM)] * 5,
        out_specs=[pl.BlockSpec(memory_space=pltpu.HBM)] * 5,
        scratch_shapes=[pltpu.SemaphoreType.DMA((5,))],
        compiler_params=pltpu.CompilerParams(vmem_limit_bytes=16 * 1024 * 1024),
        name="write_out",
    )(*outs)
    forward, forward_rate, adjoint, adjoint_rate = [
        jnp.transpose(out, (0, 2, 1, 3))[None] for out in outs[:4]
    ]
    return (forward, forward_rate, adjoint, adjoint_rate, jnp.transpose(outs[4], (0, 2, 1, 3)))


def solution(mesh):
    field = P("event", None, "region", None, None)
    model = P("region", None, None)
    regions, events = mesh.shape["region"], mesh.shape["event"]
    return jax.shard_map(
        functools.partial(run, regions, events, False),
        mesh=mesh,
        in_specs=(field,) * 5 + (model,) * 3,
        out_specs=(field,) * 4 + (P(None, ("region", "event"), None, None),),
        check_vma=False,
    )
```

```python
import functools
import math

import jax
import jax.numpy as jnp
import numpy as np
from jax import lax
from jax.experimental import pallas as pl
from jax.experimental.pallas import tpu as pltpu
from jax.sharding import PartitionSpec as P

STEPS = 2
time_step = 0.02
MESH = pl.DeviceIdType.MESH


def gll_numbers():
    points = np.array([-1.0, -math.sqrt(3.0 / 7.0), 0.0, math.sqrt(3.0 / 7.0), 1.0])
    weights = np.array([0.1, 49.0 / 90.0, 32.0 / 45.0, 49.0 / 90.0, 0.1])
    legendre = (35.0 * points**4 - 30.0 * points**2 + 3.0) / 8.0
    derivative = np.zeros((5, 5))
    for target in range(5):
        for column in range(5):
            if target != column:
                derivative[target, column] = legendre[target] / (
                    legendre[column] * (points[target] - points[column])
                )
    derivative[0, 0] = -5.0
    derivative[4, 4] = 5.0
    return (derivative, weights)


def lane_tables(lanes):
    numbers, _ = gll_numbers()
    table = np.zeros((lanes, 2 * lanes))
    for lane in range(lanes):
        start, local = lane - lane % 4, lane % 4
        for source in range(5):
            if local:
                table[(start + source) % lanes, lane] += numbers[local, source]
            else:
                right, left = (start + source) % lanes, (start - 4 + source) % lanes
                table[right, lane] += 0.5 * numbers[0, source]
                table[left, lane] += 0.5 * numbers[4, source]
                table[right, lanes + lane] += 0.5 * numbers[0, source]
                table[left, lanes + lane] -= 0.5 * numbers[4, source]
    high = table.astype(np.float32).astype(jnp.bfloat16)
    low = (table - high.astype(np.float64)).astype(np.float32).astype(jnp.bfloat16)
    return (
        np.concatenate([high, high], axis=0),
        low,
        np.concatenate([high.T, low.T], axis=1),
        np.ascontiguousarray(high.T),
    )


def combine(coefficients, pieces):
    total = None
    for number, piece in zip(coefficients, pieces):
        if number != 0.0:
            term = float(number) * piece
            total = term if total is None else total + term
    return total


def turn(value, shift):
    return pltpu.roll(value, shift % 8, value.ndim - 2)


def row_bit(shape, bit):
    return (lax.broadcasted_iota(jnp.int32, shape, len(shape) - 2) & bit) == 0


def swap_rows(four):
    shape = four[0].shape
    low_two, low_one = row_bit(shape, 2), row_bit(shape, 1)
    a0, a1, a2, a3 = four
    b0 = jnp.where(low_two, a0, turn(a2, 2))
    b2 = jnp.where(low_two, turn(a0, -2), a2)
    b1 = jnp.where(low_two, a1, turn(a3, 2))
    b3 = jnp.where(low_two, turn(a1, -2), a3)
    return (
        jnp.where(low_one, b0, turn(b1, 1)),
        jnp.where(low_one, turn(b0, -1), b1),
        jnp.where(low_one, b2, turn(b3, 1)),
        jnp.where(low_one, turn(b2, -1), b3),
    )


def middle_sum(blocks):
    first, last = blocks[..., 0, :, :], blocks[..., 4, :, :]
    low = row_bit(first.shape, 1)
    new_last = last + jnp.where(low, turn(first, -1), 0.0)
    new_first = first + jnp.where(low, 0.0, turn(last, 1))
    return jnp.concatenate(
        [new_first[..., None, :, :], blocks[..., 1:4, :, :], new_last[..., None, :, :]], axis=-3
    )


def pack_half(blocks, low):
    half = (blocks.shape[0] + 1) // 2
    first, second = blocks[:half], blocks[half:]
    if second.shape[0] < half:
        second = jnp.concatenate([second, first[-1:]], axis=0)
    keep = row_bit(first.shape, 4)
    other = turn(second, 4)
    return jnp.where(keep, first, other) if low else jnp.where(keep, other, first)


def unpack_half(packed, count):
    return jnp.concatenate([packed, turn(packed, 4)], axis=0)[:count]


def kernel(
    regions,
    events,
    uf_in,
    vf_in,
    ua_in,
    va_in,
    source_in,
    lam_in,
    mu_in,
    rho_in,
    slope_two_in,
    slope_low_in,
    back_two_in,
    back_high_in,
    uf_out,
    vf_out,
    ua_out,
    va_out,
    k_out,
    u,
    un,
    g,
    b,
    sm,
    im,
    muw,
    lamw,
    gy,
    sx,
    sy,
    f,
    fc,
    h,
    pre,
    kacc,
    imc,
    muc,
    lamc,
    px,
    mx,
    send_a,
    recv_a,
    send_b,
    recv_b,
    send_m,
    recv_m,
    send_p,
    recv_p,
    send_d,
    recv_d,
    send_q,
    recv_q,
    send_e,
    recv_e,
    send_x,
    recv_x,
    send_y,
    recv_y,
    send_w,
    recv_w,
    send_z,
    recv_z,
    recv_pd,
    recv_dd,
    u_two,
    gy_two,
    sems_y,
    open_sem,
    send_k,
    recv_k,
    sems,
    sems_k,
    sems_e,
    uf,
    vf,
    ua,
    va,
    source,
    lam,
    mu,
    rho,
    slope_two,
    slope_low,
    back_two,
    back_high,
    load_sems,
):
    numbers, weights = gll_numbers()
    lanes = u.shape[-1]
    region, event = lax.axis_index("region"), lax.axis_index("event")
    left, right = lax.rem(region + regions - 1, regions), lax.rem(region + 1, regions)
    planes = 8 // events
    corner = float(numbers[4, 4])
    pair_up = events == 2
    lead = jnp.logical_and(region == 0, event == 0)
    mate = jnp.logical_and(region == 0, event == 1)
    giver = jnp.logical_and(region == regions - 1, event == 1)
    keeper = jnp.logical_and(region == regions - 1, event == 0)

    def only(condition, action):
        if pair_up:
            pl.when(condition)(action)

    def unless(condition, action):
        if pair_up:
            pl.when(jnp.logical_not(condition))(action)
        else:
            action()

    barrier = pltpu.get_barrier_semaphore()
    def greet(side, other):
        pl.semaphore_signal(barrier, inc=1, device_id=(side, other), device_id_type=MESH)

    greet(left, event)
    unless(giver, lambda: greet(right, event))
    only(lead, lambda: greet(left, 1))
    for offset in range(1, events):
        partner = lax.rem(event + offset, events)
        unless(giver, functools.partial(greet, region, partner))

    loads = {}
    for number, (name, src, dst) in enumerate(
        (
            ("uf", uf_in, uf),
            ("ua", ua_in, ua),
            ("lam", lam_in, lam),
            ("mu", mu_in, mu),
            ("slope_two", slope_two_in, slope_two),
            ("slope_low", slope_low_in, slope_low),
            ("rho", rho_in, rho),
            ("back_two", back_two_in, back_two),
            ("back_high", back_high_in, back_high),
            ("vf", vf_in, vf),
            ("va", va_in, va),
            ("source", source_in, source),
        )
    ):
        loads[name] = pltpu.make_async_copy(src, dst, load_sems.at[number])
        if number < 7:
            loads[name].start()

    def ready(*names):
        for name in names:
            loads[name].wait()

    def remote(src, dst, number, target):
        return pltpu.make_async_remote_copy(
            src_ref=src,
            dst_ref=dst,
            send_sem=sems.at[0, number],
            recv_sem=sems.at[1, number],
            device_id=target,
            device_id_type=MESH,
        )

    def aside(src, dst, number, target):
        return pltpu.make_async_remote_copy(
            src_ref=src,
            dst_ref=dst,
            send_sem=sems_y.at[0, number],
            recv_sem=sems_y.at[1, number],
            device_id=target,
            device_id_type=MESH,
        )

    copy_x = aside(send_x, recv_x, 0, (region, 0))
    copy_y = aside(send_y, recv_y, 1, (region, 0))
    copy_z = aside(send_z, recv_z, 2, (region, 0))
    copy_w = aside(send_w, recv_w, 5, (region, 0))
    copy_pd = aside(send_p, recv_pd, 3, (right, 0))
    copy_dd = aside(send_d, recv_dd, 4, (right, 0))
    copy_a = remote(send_a, recv_a, 0, (left, event))
    copy_b = remote(send_b, recv_b, 1, (left, event))
    copy_m = remote(send_m, recv_m, 2, (right, event))
    copy_p = remote(send_p, recv_p, 3, (right, event))
    copy_d = remote(send_d, recv_d, 4, (right, event))
    copy_q = remote(send_q, recv_q, 5, (right, event))

    one = (5, 8, lanes)
    low4, low2, low1 = row_bit(one, 4), row_bit(one, 2), row_bit(one, 1)
    low4_all = row_bit((3,) + one, 4)
    lane_place = lax.broadcasted_iota(jnp.int32, one, 2) & 3
    lane_weight = jnp.where(
        lane_place == 0, 0.2, jnp.where(lane_place == 2, 32.0 / 45.0, 49.0 / 90.0)
    ).astype(jnp.float32)
    level = lax.broadcasted_iota(jnp.int32, one, 0)
    edge = (level == 0) | (level == 4)
    inner = jnp.where(level == 2, 32.0 / 45.0, 49.0 / 90.0)
    level_weight = jnp.where(edge, 0.1, inner).astype(jnp.float32)
    closed = ((level == 0) & low1) | ((level == 4) & jnp.logical_not(low1))
    node_weight = jnp.where(edge, jnp.where(closed, 0.1, 0.2), inner).astype(jnp.float32)
    element_weight = level_weight * lane_weight

    def take(first, second):
        return swap_rows((first[0:5], first[4:9], second[0:5], second[4:9]))

    def join(low, high):
        return jnp.where(low4_all, low, high)

    def rows_of(value):
        return value.reshape(-1, lanes)

    def split(values):
        high = values.astype(jnp.bfloat16)
        low = (values - high.astype(jnp.float32)).astype(jnp.bfloat16)
        return high, low

    def slope_rows(values, columns):
        high, low = split(values)
        return jnp.dot(
            jnp.concatenate([high, low], axis=1),
            slope_two[:, :columns],
            preferred_element_type=jnp.float32,
        ) + jnp.dot(high, slope_low[:, :columns], preferred_element_type=jnp.float32)

    def back_rows(values):
        deep = values.shape[1]
        high, low = split(values)
        first = jnp.dot(high, back_two[:deep], preferred_element_type=jnp.float32)
        total = first[:, :lanes] + first[:, lanes:]
        return total + jnp.dot(low, back_high[:deep], preferred_element_type=jnp.float32)

    def level_slopes(levels):
        return jnp.stack([combine(numbers[k], levels) for k in range(5)])

    def level_back(stress):
        levels = [stress[q] for q in range(5)]
        return jnp.stack([combine(numbers[:, k], levels) for k in range(5)])

    def slopes(src, begin, end):
        found = slope_rows(rows_of(src[begin:end]), 2 * lanes)
        gy[begin:end] = found.reshape(end - begin, 3, 5, 8, 2 * lanes)

    def product(value):
        return value * turn(value, -2)

    def kinds_of(weight, gx, gz, gm, gd):
        xz, xy, zy = gx[1] + gz[0], gx[2] + gm[0], gz[2] + gm[1]
        jump = product(gd[2])
        k1 = weight * (product(gx[0] + gz[1] + gm[2]) + jump)
        shear = product(gx[0]) + product(gz[1]) + product(gm[2]) + jump
        cross = product(xz) + product(xy) + product(zy) + product(gd[0]) + product(gd[1])
        k2 = weight * (2.0 * shear + cross)
        return jnp.where(low2, k1, turn(k2, 2))

    def store_stress(i, m, l, gx, gz, gm, gd):
        xz, xy, zy = gx[1] + gz[0], gx[2] + gm[0], gz[2] + gm[1]
        both = m + m
        press = l * (gx[0] + gz[1] + gm[2])
        s_xz, s_xy, s_zy = m * xz, m * xy, m * zy
        sx[i, 0] = both * gx[0] + press
        sx[i, 1] = s_xz
        sx[i, 2] = s_xy
        sy[i, 0, :, :, :lanes] = s_xy
        sy[i, 1, :, :, :lanes] = s_zy
        sy[i, 2, :, :, :lanes] = both * gm[2] + press
        sy[i, 0, :, :, lanes:] = m * gd[0]
        sy[i, 1, :, :, lanes:] = m * gd[1]
        sy[i, 2, :, :, lanes:] = (both + l) * gd[2]
        for c, stress in enumerate((s_xz, both * gz[1] + press, s_zy)):
            f[i, c] = level_back(stress)

    def grads(src, i, gy=gy):
        gx = [combine(numbers[i], [src[q, c] for q in range(5)]) for c in range(3)]
        gz = [level_slopes([src[i, c, q] for q in range(5)]) for c in range(3)]
        gm = [gy[i, c, :, :, :lanes] for c in range(3)]
        gd = [gy[i, c, :, :, lanes:] for c in range(3)]
        return gx, gz, gm, gd

    def stresses(src):
        for i in range(5):
            store_stress(i, muw[i], lamw[i], *grads(src, i))

    def kinds(src, step, gy=gy, last=5):
        for i in range(last):
            found = kinds_of(float(weights[i]) * element_weight, *grads(src, i, gy))
            kacc[i] = found if step == 0 else kacc[i] + found

    def gather_forces(*places):
        for i in places:
            total = back_rows(sy[i].reshape(120, 2 * lanes)).reshape(3, 5, 8, lanes)
            for c in range(3):
                value = f[i, c] + total[c] + combine(numbers[:, i], [sx[p, c] for p in range(5)])
                f[i, c] = middle_sum(value)

    def open_slope(src):
        return jnp.stack([combine(numbers[4, :4], [src[q, c] for q in range(4)]) for c in range(3)])

    def open_face(src, m, l, means):
        faces = []
        for p in range(4):
            gx = [combine(numbers[p, :4], [src[q, c] for q in range(4)]) for c in range(3)]
            gz = [level_slopes([src[p, c, q] for q in range(5)]) for c in range(2)]
            press = l[p] * (gx[0] + gz[1] + means(p, 2))
            faces.append(
                (
                    (m[p] + m[p]) * gx[0] + press,
                    m[p] * (gx[1] + gz[0]),
                    m[p] * (gx[2] + means(p, 0)),
                )
            )
        return jnp.stack(
            [middle_sum(combine(numbers[:4, 4], [faces[p][c] for p in range(4)])) for c in range(3)]
        )

    def face_means(src):
        rows = jnp.concatenate([rows_of(src[0:4, 0]), rows_of(src[0:4, 2])], axis=0)
        means = slope_rows(rows, lanes).reshape(2, 4, 5, 8, lanes)
        return lambda p, c: means[c // 2, p]

    def held_means(p, c):
        return gy[p, c, :, :, :lanes]

    def plane_grads(q, found, slope):
        gx = [slope[c] + corner * q[c] for c in range(3)]
        gz = [level_slopes([q[c, k] for k in range(5)]) for c in range(3)]
        gm = [found[c, :, :, :lanes] for c in range(3)]
        gd = [found[c, :, :, lanes:] for c in range(3)]
        return gx, gz, gm, gd

    def last_plane(q, gx, gz, gm, gd):
        m, l = muc[4], lamc[4]
        xz, xy, zy = gx[1] + gz[0], gx[2] + gm[0], gz[2] + gm[1]
        both = m + m
        press = l * (gx[0] + gz[1] + gm[2])
        s_xz, s_xy, s_zy = m * xz, m * xy, m * zy
        face = (both * gx[0] + press, s_xz, s_xy)
        mean = jnp.stack([s_xy, s_zy, both * gm[2] + press])
        half = jnp.stack([m * gd[0], m * gd[1], (both + l) * gd[2]])
        total = back_rows(
            jnp.concatenate([rows_of(mean), rows_of(half)], axis=1)
        ).reshape(3, 5, 8, lanes)
        inner_face = (px[4] * q[0], mx[4] * q[1], mx[4] * q[2])
        up = (s_xz, both * gz[1] + press, s_zy)
        result = [
            middle_sum(total[c] + inner_face[c] + corner * face[c] + level_back(up[c]))
            for c in range(3)
        ]
        return jnp.stack(result), face

    ready("uf", "ua")
    for comp in range(3):
        for place, value in enumerate(take(uf[comp], ua[comp])):
            u[place, comp] = value
    ready("lam", "mu", "rho")
    first_rows = row_bit((9, 8, lanes), 4)
    send_m[0:9] = jnp.where(first_rows, turn(lam[...], 4), mu[...])
    five = jnp.concatenate([rho[5:9], rho[8:9]], axis=0)
    send_m[9:14] = jnp.where(low4, turn(rho[0:5], 4), five)
    ready("slope_two", "slope_low")
    for name in ("back_two", "back_high", "vf", "va", "source"):
        loads[name].start()
    fewer = jnp.logical_or(mate, keeper)
    peers = jnp.where(fewer, events, jnp.where(giver, events + 2, events + 1))

    def enter():
        pl.semaphore_wait(barrier, peers if pair_up else events + 1)
        unless(giver, copy_m.start)

    def open_left():
        pl.semaphore_signal(open_sem, inc=1, device_id=(right, event), device_id_type=MESH)
        pl.semaphore_signal(open_sem, inc=1, device_id=(region, 0), device_id_type=MESH)

    unless(lead, enter)
    only(giver, open_left)
    slopes(u, 0, 4)
    lam_here, mu_here = take(lam[...], lam[...]), take(mu[...], mu[...])
    for place in range(4):
        weight = float(weights[place]) * element_weight
        muw[place] = mu_here[place] * weight
        lamw[place] = lam_here[place] * weight
    h[...] = open_slope(u)
    opened = open_face(u, muw, lamw, held_means)
    send_p[...] = pack_half(
        jnp.concatenate([opened.reshape(15, 8, lanes), h[...].reshape(15, 8, lanes)], axis=0), False
    )

    def give_twice():
        copy_pd.start()
        copy_m.start()

    only(giver, give_twice)
    unless(jnp.logical_or(lead, giver), copy_p.start)
    edge_pair = jnp.where(low2, mu_here[0], lam_here[0])
    send_a[...] = pack_half(
        jnp.concatenate([u[0].reshape(15, 8, lanes), edge_pair], axis=0), True
    )

    def share_first_plane():
        send_x[...] = pack_half(u[0].reshape(15, 8, lanes), True)
        copy_x.start()

    unless(region == 0, copy_a.start)
    only(mate, share_first_plane)

    u[4] = join(turn(u[0], 4), 0.0)
    wide_low = row_bit((3, 5, 8, 2 * lanes), 4)
    gy[4] = jnp.where(wide_low, turn(gy[0], 4), 0.0)
    muw[4] = jnp.where(low4, turn(mu_here[0], 4) * (0.1 * element_weight), 0.0)
    lamw[4] = jnp.where(low4, turn(lam_here[0], 4) * (0.1 * element_weight), 0.0)
    stresses(u)
    ready("back_two", "back_high")
    gather_forces(4, 0)

    rho_here = take(rho[...], rho[...])
    for place in range(4):
        weight = 0.2 if place == 0 else float(weights[place])
        im[place] = time_step / (rho_here[place] * (weight * (node_weight * lane_weight)))
    ready("vf", "va", "source")
    for comp in range(3):
        rates = take(vf[comp], va[comp])
        sources = take(jnp.zeros_like(source[comp]), source[comp])
        for place in range(4):
            pushed = sources[place] * im[place]
            sm[place, comp] = pushed
            b[place, comp] = rates[place] + pushed

    def advance(src, dst, place, force):
        for c in range(3):
            rate = b[place, c] - im[place] * force[c]
            b[place, c] = rate
            dst[place, c] = src[place, c] + time_step * rate

    advance(u, un, 0, f[0] + join(0.0, turn(f[4], 4)))
    send_b[...] = pack_half(
        jnp.concatenate([un[0].reshape(15, 8, lanes), time_step * im[0]], axis=0), True
    )
    unless(region == 0, copy_b.start)
    gather_forces(1, 2, 3)
    for place in (1, 2, 3):
        advance(u, un, place, f[place])

    def share_planes():
        send_y[...] = pack_half(un[0:4].reshape(60, 8, lanes), True)
        copy_y.start()

    only(mate, share_planes)
    send_d[...] = pack_half(open_slope(un).reshape(15, 8, lanes), False)

    def give_slope_twice():
        copy_dd.start()
        copy_p.start()

    only(giver, give_slope_twice)
    unless(lead, copy_d.start)
    send_q[...] = pack_half(
        open_face(un, muw, lamw, face_means(un)).reshape(15, 8, lanes), False
    )
    unless(lead, copy_q.start)

    def enter_late():
        pl.semaphore_wait(barrier, events + 1)
        for copy in (copy_a, copy_b, copy_m, copy_p, copy_d, copy_q):
            copy.start()

    copy_a.wait_recv()
    arrived = unpack_half(recv_a[...], 20)
    u[4] = join(u[4], turn(arrived[:15].reshape(3, 5, 8, lanes), 4))
    slopes(u, 4, 5)
    kinds(u, 0)
    pair = arrived[15:]
    mu_next, lam_next = jnp.where(low2, pair, turn(pair, 2)), jnp.where(low2, turn(pair, -2), pair)
    weight = 0.1 * element_weight
    muc[4] = jnp.where(low4, mu_here[0], turn(mu_next, 4)) * weight
    lamc[4] = jnp.where(low4, lam_here[0], turn(lam_next, 4)) * weight

    def share_first_element():
        far, m, l = u[4], muw, lamw
        factors = numbers[:4, 0] * numbers[:4, 4]
        m_face = combine(factors, [m[p] for p in range(4)])
        l_face = 2.0 * m_face + combine(factors, [l[p] for p in range(4)])
        number = float(numbers[0, 4])
        m_one, l_one = m[0] * number, l[0] * number
        rows = rows_of(jnp.stack([m_one * far[2], l_one * far[0]]))
        across = back_rows(rows).reshape(2, 5, 8, lanes)
        gx, gz, gm, _ = plane_grads(far, gy[4], h[...])
        m_last, l_last = muc[4], lamc[4]
        face = (
            (m_last + m_last) * gx[0] + l_last * (gx[0] + gz[1] + gm[2]),
            m_last * (gx[1] + gz[0]),
            m_last * (gx[2] + gm[0]),
        )
        inside = (
            l_face * far[0] + across[0] + level_back(m_one * far[1]),
            m_face * far[1] + level_back(l_one * far[0]),
            m_face * far[2] + across[1],
        )
        ends_here = []
        for c in range(3):
            force = middle_sum(inside[c] + float(numbers[4, 0]) * face[c])
            ends_here.append(turn(un[0, c] - time_step * (im[0] * force), 4))
        send_w[...] = pack_half(jnp.concatenate(ends_here, axis=0), True)
        copy_w.start()
        send_z[...] = pack_half(kacc[0:4].reshape(20, 8, lanes), True)
        copy_z.start()
        pl.semaphore_wait(open_sem, 1)
        copy_a.start()
        copy_b.start()

    only(mate, share_first_element)
    only(lead, enter_late)

    def meet_first_plane():
        copy_x.wait_recv()
        other = unpack_half(recv_x[...], 15).reshape(3, 5, 8, lanes)
        gy_two[0] = slope_rows(rows_of(other), 2 * lanes).reshape(3, 5, 8, 2 * lanes)

    only(lead, meet_first_plane)

    copy_m.wait_recv()
    both_models = recv_m[0:9]
    lam_mix = jnp.where(first_rows, both_models, lam[...])
    mu_mix = jnp.where(first_rows, turn(both_models, 4), mu[...])
    masses = recv_m[9:14]
    rho_mix = jnp.where(
        first_rows, jnp.concatenate([masses, turn(masses, 4)[0:4]], axis=0), rho[...]
    )
    lam_two, mu_two, rho_two = take(lam_mix, lam_mix), take(mu_mix, mu_mix), take(rho_mix, rho_mix)
    for place in range(4):
        weight = float(weights[place]) * element_weight
        muc[place] = mu_two[place] * weight
        lamc[place] = lam_two[place] * weight
        weight = 0.2 if place == 0 else float(weights[place])
        imc[place] = time_step / (rho_two[place] * (weight * (node_weight * lane_weight)))
    muw[4] = jnp.where(low4, muw[4], muc[4])
    lamw[4] = jnp.where(low4, lamw[4], lamc[4])
    for l in range(5):
        factors = numbers[:4, l] * numbers[:4, 4]
        mx[l] = combine(factors, [muc[p] for p in range(4)])
        px[l] = 2.0 * mx[l] + combine(factors, [lamc[p] for p in range(4)])
    ends = -time_step * combine(numbers[4, :4] ** 2, [imc[p] for p in range(4)])

    q = join(u[0], u[4])
    found = jnp.where(wide_low, gy[0], gy[4])

    def add_plane(q):
        shears = []
        for l in range(4):
            number = float(numbers[l, 4])
            shears.append(jnp.stack([muc[l] * q[2], lamc[l] * q[0]]) * number)
        around = back_rows(rows_of(jnp.stack(shears))).reshape(4, 2, 5, 8, lanes)
        for l in range(4):
            number = float(numbers[l, 4])
            up = level_back((number * muc[l]) * q[1])
            pre[l, 0] = middle_sum(px[l] * q[0] + around[l, 0] + up)
            pre[l, 1] = middle_sum(mx[l] * q[1] + level_back((number * lamc[l]) * q[0]))
            pre[l, 2] = middle_sum(mx[l] * q[2] + around[l, 1])
        for c in range(3):
            terms = [imc[l] * pre[l, c] for l in range(4)]
            fc[4, c] = -time_step * combine(numbers[4, :4], terms)

    def meet_planes():
        copy_y.wait_recv()
        u_two[0:4] = unpack_half(recv_y[...], 60).reshape(4, 3, 5, 8, lanes)
        rows = slope_rows(rows_of(u_two[1:4]), 2 * lanes)
        gy_two[1:4] = rows.reshape(3, 3, 5, 8, 2 * lanes)

    only(lead, meet_planes)
    add_plane(q)

    last, face = last_plane(q, *plane_grads(q, found, h[...]))
    for c in range(3):
        beyond = middle_sum(face[c])
        for place in range(4):
            change = imc[place] * (pre[place, c] + float(numbers[4, place]) * beyond)
            change = jnp.where(low4, 0.0, change)
            rate = b[place, c] - change
            b[place, c] = rate if place == 0 else rate + sm[place, c]
            un[place, c] = un[place, c] - time_step * change
    slopes(un, 1, 4)
    copy_b.wait_recv()
    later = unpack_half(recv_b[...], 20)
    for c in range(3):
        ahead = turn(later[5 * c : 5 * c + 5], 4) - turn(later[15:], 4) * (
            last[c] + f[4, c]
        )
        un[4, c] = jnp.where(low4, turn(un[0, c], 4), ahead)
    slopes(un, 4, 5)

    copy_p.wait_recv()
    packed = recv_p[...].reshape(3, 5, 8, lanes)
    first_grads = plane_grads(q, found, packed)
    last, face = last_plane(q, *first_grads)
    for c in range(3):
        force = last[c] + turn(packed[c], 4)
        change = jnp.where(low4, im[0] * force, 0.0)
        rate = b[0, c] - change
        b[0, c] = rate + sm[0, c]
        un[0, c] = un[0, c] - time_step * change
    slopes(un, 0, 1)
    kinds(un, 1)
    first_plane = middle_sum(kacc[0] + jnp.where(low4, 0.0, turn(kacc[4], 4)))
    nodes = swap_rows((first_plane, *[middle_sum(kacc[i]) for i in (1, 2, 3)]))
    for kind in range(2):
        whole = jnp.concatenate([nodes[2 * kind][0:4], nodes[2 * kind + 1]], axis=0)
        for owner in range(events):
            send_k[owner, kind] = whole[:, planes * owner : planes * owner + planes]
    copies = []
    for offset in range(1, events):
        partner = lax.rem(event + offset, events)
        copy = pltpu.make_async_remote_copy(
            src_ref=send_k.at[partner],
            dst_ref=recv_k.at[offset - 1],
            send_sem=sems_k.at[0, offset - 1],
            recv_sem=sems_k.at[1, offset - 1],
            device_id=(region, partner),
            device_id_type=MESH,
        )
        only(keeper, lambda: pl.semaphore_wait(open_sem, 1))
        unless(mate, copy.start)
        copies.append(copy)

    edge_kinds = kinds_of(0.1 * element_weight, *first_grads)
    copy_d.wait_recv()
    coming = unpack_half(recv_d[...], 15).reshape(3, 5, 8, lanes)
    beyond = [middle_sum(face[c]) for c in range(3)]
    slope = [fc[4, c] + ends * beyond[c] + turn(coming[c], 4) for c in range(3)]
    second_grads = plane_grads(un[0], gy[0], slope)
    edge_kinds = middle_sum(edge_kinds + kinds_of(0.1 * element_weight, *second_grads))
    send_e[...] = pack_half(edge_kinds, True)
    slot = lax.max(event - 1, 0)
    copy_e = pltpu.make_async_remote_copy(
        src_ref=send_e,
        dst_ref=recv_e.at[slot],
        send_sem=sems_e.at[events - 1],
        recv_sem=sems_e.at[slot],
        device_id=(region, 0),
        device_id_type=MESH,
    )

    sends_share = jnp.logical_and(event > 0, jnp.logical_not(mate)) if pair_up else event > 0

    @pl.when(sends_share)
    def _():
        copy_e.start()

    for c in range(3):
        for l in range(4):
            change = pre[l, c] + float(numbers[4, l]) * beyond[c]
            g[l, c] = -time_step * (imc[l] * change)
    force = open_face(g, muc, lamc, face_means(g))
    last, _ = last_plane(un[0], *second_grads)
    copy_q.wait_recv()
    coming = unpack_half(recv_q[...], 15).reshape(3, 5, 8, lanes)
    fc[0] = last + force + turn(coming, 4)
    stresses(un)
    gather_forces(4, 0, 1, 2, 3)
    advance(un, un, 0, f[0] + join(fc[0], turn(f[4], 4)))
    for place in (1, 2, 3):
        advance(un, un, place, f[place])

    def give(state, forward_out, adjoint_out):
        for c in range(3):
            four = swap_rows((state[0, c], state[1, c], state[2, c], state[3, c]))
            forward_out[c] = jnp.concatenate([four[0][0:4], four[1]], axis=0)
            adjoint_out[c] = jnp.concatenate([four[2][0:4], four[3]], axis=0)

    give(un, uf_out, ua_out)
    give(b, vf_out, va_out)

    def first_share(value):
        nothing = jnp.zeros_like(value)
        parts = swap_rows((jnp.where(low4, value, 0.0), nothing, nothing, nothing))
        return [
            jnp.concatenate([parts[2 * kind][0:4], parts[2 * kind + 1]], axis=0)[:, 0:planes]
            for kind in range(2)
        ]

    own = first_share(unpack_half(send_e[...], 5))
    total = send_k[event]
    for kind in range(2):
        k_out[kind] = total[kind] + jnp.where(event == 0, own[kind], 0.0)

    def take_kernels():
        for offset in range(1, events):
            copies[offset - 1].wait_recv()
            k_out[...] = k_out[...] + recv_k[offset - 1]

    unless(lead, take_kernels)

    def partner_kernels():
        other = unpack_half(recv_x[...], 15).reshape(3, 5, 8, lanes)
        add_plane(other)
        copy_pd.wait_recv()
        packed = recv_pd[...].reshape(3, 5, 8, lanes)
        grads_one = plane_grads(other, gy_two[0], packed)
        last, face = last_plane(other, *grads_one)
        for c in range(3):
            force = last[c] + turn(packed[c], 4)
            u_two[0, c] = u_two[0, c] - time_step * (im[0] * force)
        rows = slope_rows(rows_of(u_two[0]), 2 * lanes)
        gy_two[0] = rows.reshape(3, 5, 8, 2 * lanes)
        copy_w.wait_recv()
        u_two[4] = unpack_half(recv_w[...], 15).reshape(3, 5, 8, lanes)
        copy_z.wait_recv()
        kacc[0:4] = unpack_half(recv_z[...], 20).reshape(4, 5, 8, lanes)
        kinds(u_two, 1, gy_two, 4)
        weight = 0.1 * element_weight
        share = kinds_of(weight, *grads_one)
        first = middle_sum(kacc[0] + share)
        nodes = swap_rows((first, *[middle_sum(kacc[i]) for i in (1, 2, 3)]))
        for kind in range(2):
            whole = jnp.concatenate([nodes[2 * kind][0:4], nodes[2 * kind + 1]], axis=0)
            k_out[kind] = k_out[kind] + whole[:, 0:planes]
        copy_dd.wait_recv()
        coming = unpack_half(recv_dd[...], 15).reshape(3, 5, 8, lanes)
        slope = [fc[4, c] + ends * middle_sum(face[c]) + turn(coming[c], 4) for c in range(3)]
        grads_two = plane_grads(u_two[0], gy_two[0], slope)
        parts = first_share(middle_sum(kinds_of(weight, *grads_two)))
        for kind in range(2):
            k_out[kind] = k_out[kind] + parts[kind]

    only(lead, partner_kernels)

    takes_share = jnp.logical_and(event == 0, jnp.logical_not(lead)) if pair_up else event == 0

    @pl.when(takes_share)
    def _():
        extra = None
        for other in range(events - 1):
            pltpu.make_async_copy(recv_e.at[other], recv_e.at[other], sems_e.at[other]).wait()
            share = unpack_half(recv_e[other], 5)
            extra = share if extra is None else extra + share
        parts = first_share(extra)
        for kind in range(2):
            k_out[kind] = k_out[kind] + parts[kind]

    @pl.when(sends_share)
    def _():
        copy_e.wait_send()

    for copy in [copy_a, copy_b, copy_m, copy_p, copy_d, copy_q]:
        copy.wait_send()

    def close_copies():
        for copy in copies:
            copy.wait_send()

    def close_mate():
        for copy in (copy_x, copy_y, copy_w, copy_z):
            copy.wait_send()

    def close_giver():
        for copy in (copy_pd, copy_dd):
            copy.wait_send()

    unless(mate, close_copies)
    only(mate, close_mate)
    only(giver, close_giver)


def flush(*refs):
    sources, outs, sems = refs[:5], refs[5:10], refs[10]
    stores = [pltpu.make_async_copy(sources[n], outs[n], sems.at[n]) for n in range(5)]
    for store in stores:
        store.start()
    for store in stores:
        store.wait()


def run(regions, events, interpret, *arrays):
    lanes = arrays[0].shape[-1]
    fields = [jnp.transpose(array[0], (0, 2, 1, 3)) for array in arrays[:5]]
    models = [jnp.transpose(array, (1, 0, 2)) for array in arrays[5:]]
    tables = [jnp.asarray(table) for table in lane_tables(lanes)]
    operands = [*fields, *models, *tables]
    operands = [pltpu.with_memory_space_constraint(array, pltpu.HBM) for array in operands]
    planes = 8 // events
    state = jax.ShapeDtypeStruct((3, 9, 8, lanes), jnp.float32)
    f32 = jnp.float32
    vector = pltpu.VMEM((5, 3, 5, 8, lanes), f32)
    wide = pltpu.VMEM((5, 3, 5, 8, 2 * lanes), f32)
    scalar = pltpu.VMEM((5, 5, 8, lanes), f32)

    def packed(*lead):
        return pltpu.VMEM(lead + (8, lanes), f32)

    outs = pl.pallas_call(
        functools.partial(kernel, regions, events),
        out_shape=[state] * 4 + [jax.ShapeDtypeStruct((2, 9, planes, lanes), f32)],
        in_specs=[pl.BlockSpec(memory_space=pltpu.HBM)] * 12,
        out_specs=[pl.BlockSpec(memory_space=pltpu.VMEM)] * 5,
        scratch_shapes=[
            vector,
            vector,
            vector,
            vector,
            vector,
            scalar,
            scalar,
            scalar,
            wide,
            vector,
            wide,
            vector,
            vector,
            packed(3, 5),
            vector,
            scalar,
            scalar,
            scalar,
            scalar,
            scalar,
            scalar,
            packed(10),
            packed(10),
            packed(10),
            packed(10),
            packed(14),
            packed(14),
            packed(15),
            packed(15),
            packed(8),
            packed(8),
            packed(8),
            packed(8),
            packed(3),
            packed(max(events - 1, 1), 3),
            packed(8),
            packed(8),
            packed(30),
            packed(30),
            packed(8),
            packed(8),
            packed(10),
            packed(10),
            packed(15),
            packed(8),
            vector,
            wide,
            pltpu.SemaphoreType.DMA((2, 6)),
            pltpu.SemaphoreType.REGULAR,
            pltpu.VMEM((events, 2, 9, planes, lanes), f32),
            pltpu.VMEM((max(events - 1, 1), 2, 9, planes, lanes), f32),
            pltpu.SemaphoreType.DMA((2, 6)),
            pltpu.SemaphoreType.DMA((2, max(events - 1, 1))),
            pltpu.SemaphoreType.DMA((events,)),
            *[pltpu.VMEM(array.shape, array.dtype) for array in operands],
            pltpu.SemaphoreType.DMA((len(operands),)),
        ],
        compiler_params=pltpu.CompilerParams(
            collective_id=0, has_side_effects=True, vmem_limit_bytes=40 * 1024 * 1024
        ),
        name="adjoint_steps",
    )(*operands)
    shapes = [jax.ShapeDtypeStruct(out.shape, out.dtype) for out in outs]
    outs = pl.pallas_call(
        flush,
        out_shape=shapes,
        in_specs=[pl.BlockSpec(memory_space=pltpu.VMEM)] * 5,
        out_specs=[pl.BlockSpec(memory_space=pltpu.HBM)] * 5,
        scratch_shapes=[pltpu.SemaphoreType.DMA((5,))],
        compiler_params=pltpu.CompilerParams(vmem_limit_bytes=16 * 1024 * 1024),
        name="write_out",
    )(*outs)
    forward, forward_rate, adjoint, adjoint_rate = [
        jnp.transpose(out, (0, 2, 1, 3))[None] for out in outs[:4]
    ]
    return (forward, forward_rate, adjoint, adjoint_rate, jnp.transpose(outs[4], (0, 2, 1, 3)))


def solution(mesh):
    field = P("event", None, "region", None, None)
    model = P("region", None, None)
    regions, events = mesh.shape["region"], mesh.shape["event"]
    return jax.shard_map(
        functools.partial(run, regions, events, False),
        mesh=mesh,
        in_specs=(field,) * 5 + (model,) * 3,
        out_specs=(field,) * 4 + (P(None, ("region", "event"), None, None),),
        check_vma=False,
    )
```

```python
import functools
import math

import jax
import jax.numpy as jnp
import numpy as np
from jax import lax
from jax.experimental import pallas as pl
from jax.experimental.pallas import tpu as pltpu
from jax.sharding import PartitionSpec as P

STEPS = 2
time_step = 0.02
MESH = pl.DeviceIdType.MESH


def gll_numbers():
    points = np.array([-1.0, -math.sqrt(3.0 / 7.0), 0.0, math.sqrt(3.0 / 7.0), 1.0])
    weights = np.array([0.1, 49.0 / 90.0, 32.0 / 45.0, 49.0 / 90.0, 0.1])
    legendre = (35.0 * points**4 - 30.0 * points**2 + 3.0) / 8.0
    derivative = np.zeros((5, 5))
    for target in range(5):
        for column in range(5):
            if target != column:
                derivative[target, column] = legendre[target] / (
                    legendre[column] * (points[target] - points[column])
                )
    derivative[0, 0] = -5.0
    derivative[4, 4] = 5.0
    return (derivative, weights)


def lane_tables(lanes):
    numbers, _ = gll_numbers()
    table = np.zeros((lanes, 2 * lanes))
    for lane in range(lanes):
        start, local = lane - lane % 4, lane % 4
        for source in range(5):
            if local:
                table[(start + source) % lanes, lane] += numbers[local, source]
            else:
                right, left = (start + source) % lanes, (start - 4 + source) % lanes
                table[right, lane] += 0.5 * numbers[0, source]
                table[left, lane] += 0.5 * numbers[4, source]
                table[right, lanes + lane] += 0.5 * numbers[0, source]
                table[left, lanes + lane] -= 0.5 * numbers[4, source]
    high = table.astype(np.float32).astype(jnp.bfloat16)
    low = (table - high.astype(np.float64)).astype(np.float32).astype(jnp.bfloat16)
    return (
        np.concatenate([high, high], axis=0),
        low,
        np.concatenate([high.T, low.T], axis=1),
    )


def combine(coefficients, pieces):
    total = None
    for number, piece in zip(coefficients, pieces):
        if number != 0.0:
            term = float(number) * piece
            total = term if total is None else total + term
    return total


def turn(value, shift):
    return pltpu.roll(value, shift % 8, value.ndim - 2)


def row_bit(shape, bit):
    return (lax.broadcasted_iota(jnp.int32, shape, len(shape) - 2) & bit) == 0


def swap_rows(four):
    shape = four[0].shape
    low_two, low_one = row_bit(shape, 2), row_bit(shape, 1)
    a0, a1, a2, a3 = four
    b0 = jnp.where(low_two, a0, turn(a2, 2))
    b2 = jnp.where(low_two, turn(a0, -2), a2)
    b1 = jnp.where(low_two, a1, turn(a3, 2))
    b3 = jnp.where(low_two, turn(a1, -2), a3)
    return (
        jnp.where(low_one, b0, turn(b1, 1)),
        jnp.where(low_one, turn(b0, -1), b1),
        jnp.where(low_one, b2, turn(b3, 1)),
        jnp.where(low_one, turn(b2, -1), b3),
    )


def middle_sum(blocks):
    first, last = blocks[..., 0, :, :], blocks[..., 4, :, :]
    low = row_bit(first.shape, 1)
    new_last = last + jnp.where(low, turn(first, -1), 0.0)
    new_first = first + jnp.where(low, 0.0, turn(last, 1))
    return jnp.concatenate(
        [new_first[..., None, :, :], blocks[..., 1:4, :, :], new_last[..., None, :, :]], axis=-3
    )


def pack_half(blocks, low):
    half = (blocks.shape[0] + 1) // 2
    first, second = blocks[:half], blocks[half:]
    if second.shape[0] < half:
        second = jnp.concatenate([second, first[-1:]], axis=0)
    keep = row_bit(first.shape, 4)
    other = turn(second, 4)
    return jnp.where(keep, first, other) if low else jnp.where(keep, other, first)


def unpack_half(packed, count):
    return jnp.concatenate([packed, turn(packed, 4)], axis=0)[:count]


def kernel(
    regions,
    events,
    uf_in,
    vf_in,
    ua_in,
    va_in,
    source_in,
    lam_in,
    mu_in,
    rho_in,
    slope_two_in,
    slope_low_in,
    back_two_in,
    uf_out,
    vf_out,
    ua_out,
    va_out,
    k_out,
    u,
    un,
    g,
    b,
    sm,
    im,
    muw,
    lamw,
    gy,
    sx,
    sy,
    f,
    fc,
    h,
    pre,
    kacc,
    imc,
    muc,
    lamc,
    px,
    mx,
    send_a,
    recv_a,
    send_b,
    recv_b,
    send_m,
    recv_m,
    send_p,
    recv_p,
    send_d,
    recv_d,
    send_q,
    recv_q,
    send_e,
    recv_e,
    send_x,
    recv_x,
    send_y,
    recv_y,
    send_w,
    recv_w,
    send_z,
    recv_z,
    recv_pd,
    recv_dd,
    u_two,
    gy_two,
    sems_y,
    open_sem,
    send_k,
    recv_k,
    sems,
    sems_k,
    sems_e,
    uf,
    vf,
    ua,
    va,
    source,
    lam,
    mu,
    rho,
    slope_two,
    slope_low,
    back_two,
    load_sems,
):
    numbers, weights = gll_numbers()
    lanes = u.shape[-1]
    region, event = lax.axis_index("region"), lax.axis_index("event")
    left, right = lax.rem(region + regions - 1, regions), lax.rem(region + 1, regions)
    planes = 8 // events
    corner = float(numbers[4, 4])
    pair_up = events == 2
    lead = jnp.logical_and(region == 0, event == 0)
    mate = jnp.logical_and(region == 0, event == 1)
    giver = jnp.logical_and(region == regions - 1, event == 1)
    keeper = jnp.logical_and(region == regions - 1, event == 0)

    def only(condition, action):
        if pair_up:
            pl.when(condition)(action)

    def unless(condition, action):
        if pair_up:
            pl.when(jnp.logical_not(condition))(action)
        else:
            action()

    barrier = pltpu.get_barrier_semaphore()
    def greet(side, other):
        pl.semaphore_signal(barrier, inc=1, device_id=(side, other), device_id_type=MESH)

    greet(left, event)
    unless(giver, lambda: greet(right, event))
    only(lead, lambda: greet(left, 1))
    for offset in range(1, events):
        partner = lax.rem(event + offset, events)
        unless(giver, functools.partial(greet, region, partner))

    loads = {}
    for number, (name, src, dst) in enumerate(
        (
            ("uf", uf_in, uf),
            ("ua", ua_in, ua),
            ("lam", lam_in, lam),
            ("mu", mu_in, mu),
            ("slope_two", slope_two_in, slope_two),
            ("slope_low", slope_low_in, slope_low),
            ("rho", rho_in, rho),
            ("back_two", back_two_in, back_two),
            ("vf", vf_in, vf),
            ("va", va_in, va),
            ("source", source_in, source),
        )
    ):
        loads[name] = pltpu.make_async_copy(src, dst, load_sems.at[number])
        if number < 7:
            loads[name].start()

    def ready(*names):
        for name in names:
            loads[name].wait()

    def remote(src, dst, number, target):
        return pltpu.make_async_remote_copy(
            src_ref=src,
            dst_ref=dst,
            send_sem=sems.at[0, number],
            recv_sem=sems.at[1, number],
            device_id=target,
            device_id_type=MESH,
        )

    def aside(src, dst, number, target):
        return pltpu.make_async_remote_copy(
            src_ref=src,
            dst_ref=dst,
            send_sem=sems_y.at[0, number],
            recv_sem=sems_y.at[1, number],
            device_id=target,
            device_id_type=MESH,
        )

    copy_x = aside(send_x, recv_x, 0, (region, 0))
    copy_y = aside(send_y, recv_y, 1, (region, 0))
    copy_z = aside(send_z, recv_z, 2, (region, 0))
    copy_w = aside(send_w, recv_w, 5, (region, 0))
    copy_pd = aside(send_p, recv_pd, 3, (right, 0))
    copy_dd = aside(send_d, recv_dd, 4, (right, 0))
    copy_a = remote(send_a, recv_a, 0, (left, event))
    copy_b = remote(send_b, recv_b, 1, (left, event))
    copy_m = remote(send_m, recv_m, 2, (right, event))
    copy_p = remote(send_p, recv_p, 3, (right, event))
    copy_d = remote(send_d, recv_d, 4, (right, event))
    copy_q = remote(send_q, recv_q, 5, (right, event))

    one = (5, 8, lanes)
    low4, low2, low1 = row_bit(one, 4), row_bit(one, 2), row_bit(one, 1)
    low4_all = row_bit((3,) + one, 4)
    lane_place = lax.broadcasted_iota(jnp.int32, one, 2) & 3
    lane_weight = jnp.where(
        lane_place == 0, 0.2, jnp.where(lane_place == 2, 32.0 / 45.0, 49.0 / 90.0)
    ).astype(jnp.float32)
    level = lax.broadcasted_iota(jnp.int32, one, 0)
    edge = (level == 0) | (level == 4)
    inner = jnp.where(level == 2, 32.0 / 45.0, 49.0 / 90.0)
    level_weight = jnp.where(edge, 0.1, inner).astype(jnp.float32)
    closed = ((level == 0) & low1) | ((level == 4) & jnp.logical_not(low1))
    node_weight = jnp.where(edge, jnp.where(closed, 0.1, 0.2), inner).astype(jnp.float32)
    element_weight = level_weight * lane_weight

    def take(first, second):
        return swap_rows((first[0:5], first[4:9], second[0:5], second[4:9]))

    def join(low, high):
        return jnp.where(low4_all, low, high)

    def rows_of(value):
        return value.reshape(-1, lanes)

    def split(values):
        high = values.astype(jnp.bfloat16)
        low = (values - high.astype(jnp.float32)).astype(jnp.bfloat16)
        return high, low

    def slope_rows(values, columns):
        high, low = split(values)
        return jnp.dot(
            jnp.concatenate([high, low], axis=1),
            slope_two[:, :columns],
            preferred_element_type=jnp.float32,
        ) + jnp.dot(high, slope_low[:, :columns], preferred_element_type=jnp.float32)

    def back_rows(values):
        deep = values.shape[1]
        high, low = split(values)
        first = jnp.dot(high, back_two[:deep], preferred_element_type=jnp.float32)
        total = first[:, :lanes] + first[:, lanes:]
        return total + jnp.dot(low, back_two[:deep, :lanes], preferred_element_type=jnp.float32)

    def level_slopes(levels):
        return jnp.stack([combine(numbers[k], levels) for k in range(5)])

    def level_back(stress):
        levels = [stress[q] for q in range(5)]
        return jnp.stack([combine(numbers[:, k], levels) for k in range(5)])

    def slopes(src, begin, end):
        found = slope_rows(rows_of(src[begin:end]), 2 * lanes)
        gy[begin:end] = found.reshape(end - begin, 3, 5, 8, 2 * lanes)

    def product(value):
        return value * turn(value, -2)

    def kinds_of(weight, gx, gz, gm, gd):
        xz, xy, zy = gx[1] + gz[0], gx[2] + gm[0], gz[2] + gm[1]
        jump = product(gd[2])
        k1 = weight * (product(gx[0] + gz[1] + gm[2]) + jump)
        shear = product(gx[0]) + product(gz[1]) + product(gm[2]) + jump
        cross = product(xz) + product(xy) + product(zy) + product(gd[0]) + product(gd[1])
        k2 = weight * (2.0 * shear + cross)
        return jnp.where(low2, k1, turn(k2, 2))

    def store_stress(i, m, l, gx, gz, gm, gd):
        xz, xy, zy = gx[1] + gz[0], gx[2] + gm[0], gz[2] + gm[1]
        both = m + m
        press = l * (gx[0] + gz[1] + gm[2])
        s_xz, s_xy, s_zy = m * xz, m * xy, m * zy
        sx[i, 0] = both * gx[0] + press
        sx[i, 1] = s_xz
        sx[i, 2] = s_xy
        sy[i, 0, :, :, :lanes] = s_xy
        sy[i, 1, :, :, :lanes] = s_zy
        sy[i, 2, :, :, :lanes] = both * gm[2] + press
        sy[i, 0, :, :, lanes:] = m * gd[0]
        sy[i, 1, :, :, lanes:] = m * gd[1]
        sy[i, 2, :, :, lanes:] = (both + l) * gd[2]
        for c, stress in enumerate((s_xz, both * gz[1] + press, s_zy)):
            f[i, c] = level_back(stress)

    def grads(src, i, gy=gy):
        gx = [combine(numbers[i], [src[q, c] for q in range(5)]) for c in range(3)]
        gz = [level_slopes([src[i, c, q] for q in range(5)]) for c in range(3)]
        gm = [gy[i, c, :, :, :lanes] for c in range(3)]
        gd = [gy[i, c, :, :, lanes:] for c in range(3)]
        return gx, gz, gm, gd

    def stresses(src):
        for i in range(5):
            store_stress(i, muw[i], lamw[i], *grads(src, i))

    def kinds(src, step, gy=gy, last=5):
        for i in range(last):
            found = kinds_of(float(weights[i]) * element_weight, *grads(src, i, gy))
            kacc[i] = found if step == 0 else kacc[i] + found

    def gather_forces(*places):
        for i in places:
            total = back_rows(sy[i].reshape(120, 2 * lanes)).reshape(3, 5, 8, lanes)
            for c in range(3):
                value = f[i, c] + total[c] + combine(numbers[:, i], [sx[p, c] for p in range(5)])
                f[i, c] = middle_sum(value)

    def open_slope(src):
        return jnp.stack([combine(numbers[4, :4], [src[q, c] for q in range(4)]) for c in range(3)])

    def open_face(src, m, l, means):
        faces = []
        for p in range(4):
            gx = [combine(numbers[p, :4], [src[q, c] for q in range(4)]) for c in range(3)]
            gz = [level_slopes([src[p, c, q] for q in range(5)]) for c in range(2)]
            press = l[p] * (gx[0] + gz[1] + means(p, 2))
            faces.append(
                (
                    (m[p] + m[p]) * gx[0] + press,
                    m[p] * (gx[1] + gz[0]),
                    m[p] * (gx[2] + means(p, 0)),
                )
            )
        return jnp.stack(
            [middle_sum(combine(numbers[:4, 4], [faces[p][c] for p in range(4)])) for c in range(3)]
        )

    def face_means(src):
        rows = jnp.concatenate([rows_of(src[0:4, 0]), rows_of(src[0:4, 2])], axis=0)
        means = slope_rows(rows, lanes).reshape(2, 4, 5, 8, lanes)
        return lambda p, c: means[c // 2, p]

    def held_means(p, c):
        return gy[p, c, :, :, :lanes]

    def plane_grads(q, found, slope):
        gx = [slope[c] + corner * q[c] for c in range(3)]
        gz = [level_slopes([q[c, k] for k in range(5)]) for c in range(3)]
        gm = [found[c, :, :, :lanes] for c in range(3)]
        gd = [found[c, :, :, lanes:] for c in range(3)]
        return gx, gz, gm, gd

    def last_plane(q, gx, gz, gm, gd):
        m, l = muc[4], lamc[4]
        xz, xy, zy = gx[1] + gz[0], gx[2] + gm[0], gz[2] + gm[1]
        both = m + m
        press = l * (gx[0] + gz[1] + gm[2])
        s_xz, s_xy, s_zy = m * xz, m * xy, m * zy
        face = (both * gx[0] + press, s_xz, s_xy)
        mean = jnp.stack([s_xy, s_zy, both * gm[2] + press])
        half = jnp.stack([m * gd[0], m * gd[1], (both + l) * gd[2]])
        total = back_rows(
            jnp.concatenate([rows_of(mean), rows_of(half)], axis=1)
        ).reshape(3, 5, 8, lanes)
        inner_face = (px[4] * q[0], mx[4] * q[1], mx[4] * q[2])
        up = (s_xz, both * gz[1] + press, s_zy)
        result = [
            middle_sum(total[c] + inner_face[c] + corner * face[c] + level_back(up[c]))
            for c in range(3)
        ]
        return jnp.stack(result), face

    ready("uf", "ua")
    for comp in range(3):
        for place, value in enumerate(take(uf[comp], ua[comp])):
            u[place, comp] = value
    ready("lam", "mu", "rho")
    first_rows = row_bit((9, 8, lanes), 4)
    send_m[0:9] = jnp.where(first_rows, turn(lam[...], 4), mu[...])
    five = jnp.concatenate([rho[5:9], rho[8:9]], axis=0)
    send_m[9:14] = jnp.where(low4, turn(rho[0:5], 4), five)
    ready("slope_two", "slope_low")
    for name in ("back_two", "vf", "va", "source"):
        loads[name].start()
    fewer = jnp.logical_or(mate, keeper)
    peers = jnp.where(fewer, events, jnp.where(giver, events + 2, events + 1))

    def enter():
        pl.semaphore_wait(barrier, peers if pair_up else events + 1)
        unless(giver, copy_m.start)

    def open_left():
        pl.semaphore_signal(open_sem, inc=1, device_id=(right, event), device_id_type=MESH)
        pl.semaphore_signal(open_sem, inc=1, device_id=(region, 0), device_id_type=MESH)

    unless(lead, enter)
    only(giver, open_left)
    slopes(u, 0, 4)
    lam_here, mu_here = take(lam[...], lam[...]), take(mu[...], mu[...])
    for place in range(4):
        weight = float(weights[place]) * element_weight
        muw[place] = mu_here[place] * weight
        lamw[place] = lam_here[place] * weight
    h[...] = open_slope(u)
    opened = open_face(u, muw, lamw, held_means)
    send_p[...] = pack_half(
        jnp.concatenate([opened.reshape(15, 8, lanes), h[...].reshape(15, 8, lanes)], axis=0), False
    )

    def give_twice():
        copy_pd.start()
        copy_m.start()

    only(giver, give_twice)
    unless(jnp.logical_or(lead, giver), copy_p.start)
    edge_pair = jnp.where(low2, mu_here[0], lam_here[0])
    send_a[...] = pack_half(
        jnp.concatenate([u[0].reshape(15, 8, lanes), edge_pair], axis=0), True
    )

    def share_first_plane():
        send_x[...] = pack_half(u[0].reshape(15, 8, lanes), True)
        copy_x.start()

    unless(region == 0, copy_a.start)
    only(mate, share_first_plane)

    u[4] = join(turn(u[0], 4), 0.0)
    wide_low = row_bit((3, 5, 8, 2 * lanes), 4)
    gy[4] = jnp.where(wide_low, turn(gy[0], 4), 0.0)
    muw[4] = jnp.where(low4, turn(mu_here[0], 4) * (0.1 * element_weight), 0.0)
    lamw[4] = jnp.where(low4, turn(lam_here[0], 4) * (0.1 * element_weight), 0.0)
    stresses(u)
    ready("back_two")
    gather_forces(4, 0)

    rho_here = take(rho[...], rho[...])
    for place in range(4):
        weight = 0.2 if place == 0 else float(weights[place])
        im[place] = time_step / (rho_here[place] * (weight * (node_weight * lane_weight)))
    ready("vf", "va", "source")
    for comp in range(3):
        rates = take(vf[comp], va[comp])
        sources = take(jnp.zeros_like(source[comp]), source[comp])
        for place in range(4):
            pushed = sources[place] * im[place]
            sm[place, comp] = pushed
            b[place, comp] = rates[place] + pushed

    def advance(src, dst, place, force):
        for c in range(3):
            rate = b[place, c] - im[place] * force[c]
            b[place, c] = rate
            dst[place, c] = src[place, c] + time_step * rate

    advance(u, un, 0, f[0] + join(0.0, turn(f[4], 4)))
    send_b[...] = pack_half(
        jnp.concatenate([un[0].reshape(15, 8, lanes), time_step * im[0]], axis=0), True
    )
    unless(region == 0, copy_b.start)
    gather_forces(1, 2, 3)
    for place in (1, 2, 3):
        advance(u, un, place, f[place])

    def share_planes():
        send_y[...] = pack_half(un[0:4].reshape(60, 8, lanes), True)
        copy_y.start()

    only(mate, share_planes)
    send_d[...] = pack_half(open_slope(un).reshape(15, 8, lanes), False)

    def give_slope_twice():
        copy_dd.start()
        copy_p.start()

    only(giver, give_slope_twice)
    unless(lead, copy_d.start)
    send_q[...] = pack_half(
        open_face(un, muw, lamw, face_means(un)).reshape(15, 8, lanes), False
    )
    unless(lead, copy_q.start)

    def enter_late():
        pl.semaphore_wait(barrier, events + 1)
        for copy in (copy_a, copy_b, copy_m, copy_p, copy_d, copy_q):
            copy.start()

    copy_a.wait_recv()
    arrived = unpack_half(recv_a[...], 20)
    u[4] = join(u[4], turn(arrived[:15].reshape(3, 5, 8, lanes), 4))
    slopes(u, 4, 5)
    kinds(u, 0)
    pair = arrived[15:]
    mu_next, lam_next = jnp.where(low2, pair, turn(pair, 2)), jnp.where(low2, turn(pair, -2), pair)
    weight = 0.1 * element_weight
    muc[4] = jnp.where(low4, mu_here[0], turn(mu_next, 4)) * weight
    lamc[4] = jnp.where(low4, lam_here[0], turn(lam_next, 4)) * weight

    def share_first_element():
        far, m, l = u[4], muw, lamw
        factors = numbers[:4, 0] * numbers[:4, 4]
        m_face = combine(factors, [m[p] for p in range(4)])
        l_face = 2.0 * m_face + combine(factors, [l[p] for p in range(4)])
        number = float(numbers[0, 4])
        m_one, l_one = m[0] * number, l[0] * number
        rows = rows_of(jnp.stack([m_one * far[2], l_one * far[0]]))
        across = back_rows(rows).reshape(2, 5, 8, lanes)
        gx, gz, gm, _ = plane_grads(far, gy[4], h[...])
        m_last, l_last = muc[4], lamc[4]
        face = (
            (m_last + m_last) * gx[0] + l_last * (gx[0] + gz[1] + gm[2]),
            m_last * (gx[1] + gz[0]),
            m_last * (gx[2] + gm[0]),
        )
        inside = (
            l_face * far[0] + across[0] + level_back(m_one * far[1]),
            m_face * far[1] + level_back(l_one * far[0]),
            m_face * far[2] + across[1],
        )
        ends_here = []
        for c in range(3):
            force = middle_sum(inside[c] + float(numbers[4, 0]) * face[c])
            ends_here.append(turn(un[0, c] - time_step * (im[0] * force), 4))
        send_w[...] = pack_half(jnp.concatenate(ends_here, axis=0), True)
        copy_w.start()
        send_z[...] = pack_half(kacc[0:4].reshape(20, 8, lanes), True)
        copy_z.start()
        pl.semaphore_wait(open_sem, 1)
        copy_a.start()
        copy_b.start()

    only(mate, share_first_element)
    only(lead, enter_late)

    def meet_first_plane():
        copy_x.wait_recv()
        other = unpack_half(recv_x[...], 15).reshape(3, 5, 8, lanes)
        gy_two[0] = slope_rows(rows_of(other), 2 * lanes).reshape(3, 5, 8, 2 * lanes)

    only(lead, meet_first_plane)

    copy_m.wait_recv()
    both_models = recv_m[0:9]
    lam_mix = jnp.where(first_rows, both_models, lam[...])
    mu_mix = jnp.where(first_rows, turn(both_models, 4), mu[...])
    masses = recv_m[9:14]
    rho_mix = jnp.where(
        first_rows, jnp.concatenate([masses, turn(masses, 4)[0:4]], axis=0), rho[...]
    )
    lam_two, mu_two, rho_two = take(lam_mix, lam_mix), take(mu_mix, mu_mix), take(rho_mix, rho_mix)
    for place in range(4):
        weight = float(weights[place]) * element_weight
        muc[place] = mu_two[place] * weight
        lamc[place] = lam_two[place] * weight
        weight = 0.2 if place == 0 else float(weights[place])
        imc[place] = time_step / (rho_two[place] * (weight * (node_weight * lane_weight)))
    muw[4] = jnp.where(low4, muw[4], muc[4])
    lamw[4] = jnp.where(low4, lamw[4], lamc[4])
    for l in range(5):
        factors = numbers[:4, l] * numbers[:4, 4]
        mx[l] = combine(factors, [muc[p] for p in range(4)])
        px[l] = 2.0 * mx[l] + combine(factors, [lamc[p] for p in range(4)])
    ends = -time_step * combine(numbers[4, :4] ** 2, [imc[p] for p in range(4)])

    q = join(u[0], u[4])
    found = jnp.where(wide_low, gy[0], gy[4])

    def add_plane(q):
        shears = []
        for l in range(4):
            number = float(numbers[l, 4])
            shears.append(jnp.stack([muc[l] * q[2], lamc[l] * q[0]]) * number)
        around = back_rows(rows_of(jnp.stack(shears))).reshape(4, 2, 5, 8, lanes)
        for l in range(4):
            number = float(numbers[l, 4])
            up = level_back((number * muc[l]) * q[1])
            pre[l, 0] = middle_sum(px[l] * q[0] + around[l, 0] + up)
            pre[l, 1] = middle_sum(mx[l] * q[1] + level_back((number * lamc[l]) * q[0]))
            pre[l, 2] = middle_sum(mx[l] * q[2] + around[l, 1])
        for c in range(3):
            terms = [imc[l] * pre[l, c] for l in range(4)]
            fc[4, c] = -time_step * combine(numbers[4, :4], terms)

    def meet_planes():
        copy_y.wait_recv()
        u_two[0:4] = unpack_half(recv_y[...], 60).reshape(4, 3, 5, 8, lanes)
        rows = slope_rows(rows_of(u_two[1:4]), 2 * lanes)
        gy_two[1:4] = rows.reshape(3, 3, 5, 8, 2 * lanes)

    only(lead, meet_planes)
    add_plane(q)

    last, face = last_plane(q, *plane_grads(q, found, h[...]))
    for c in range(3):
        beyond = middle_sum(face[c])
        for place in range(4):
            change = imc[place] * (pre[place, c] + float(numbers[4, place]) * beyond)
            change = jnp.where(low4, 0.0, change)
            rate = b[place, c] - change
            b[place, c] = rate if place == 0 else rate + sm[place, c]
            un[place, c] = un[place, c] - time_step * change
    slopes(un, 1, 4)
    copy_b.wait_recv()
    later = unpack_half(recv_b[...], 20)
    for c in range(3):
        ahead = turn(later[5 * c : 5 * c + 5], 4) - turn(later[15:], 4) * (
            last[c] + f[4, c]
        )
        un[4, c] = jnp.where(low4, turn(un[0, c], 4), ahead)
    slopes(un, 4, 5)

    copy_p.wait_recv()
    packed = recv_p[...].reshape(3, 5, 8, lanes)
    first_grads = plane_grads(q, found, packed)
    last, face = last_plane(q, *first_grads)
    for c in range(3):
        force = last[c] + turn(packed[c], 4)
        change = jnp.where(low4, im[0] * force, 0.0)
        rate = b[0, c] - change
        b[0, c] = rate + sm[0, c]
        un[0, c] = un[0, c] - time_step * change
    slopes(un, 0, 1)
    kinds(un, 1)
    first_plane = middle_sum(kacc[0] + jnp.where(low4, 0.0, turn(kacc[4], 4)))
    nodes = swap_rows((first_plane, *[middle_sum(kacc[i]) for i in (1, 2, 3)]))
    for kind in range(2):
        whole = jnp.concatenate([nodes[2 * kind][0:4], nodes[2 * kind + 1]], axis=0)
        for owner in range(events):
            send_k[owner, kind] = whole[:, planes * owner : planes * owner + planes]
    copies = []
    for offset in range(1, events):
        partner = lax.rem(event + offset, events)
        copy = pltpu.make_async_remote_copy(
            src_ref=send_k.at[partner],
            dst_ref=recv_k.at[offset - 1],
            send_sem=sems_k.at[0, offset - 1],
            recv_sem=sems_k.at[1, offset - 1],
            device_id=(region, partner),
            device_id_type=MESH,
        )
        only(keeper, lambda: pl.semaphore_wait(open_sem, 1))
        unless(mate, copy.start)
        copies.append(copy)

    edge_kinds = kinds_of(0.1 * element_weight, *first_grads)
    copy_d.wait_recv()
    coming = unpack_half(recv_d[...], 15).reshape(3, 5, 8, lanes)
    beyond = [middle_sum(face[c]) for c in range(3)]
    slope = [fc[4, c] + ends * beyond[c] + turn(coming[c], 4) for c in range(3)]
    second_grads = plane_grads(un[0], gy[0], slope)
    edge_kinds = middle_sum(edge_kinds + kinds_of(0.1 * element_weight, *second_grads))
    send_e[...] = pack_half(edge_kinds, True)
    slot = lax.max(event - 1, 0)
    copy_e = pltpu.make_async_remote_copy(
        src_ref=send_e,
        dst_ref=recv_e.at[slot],
        send_sem=sems_e.at[events - 1],
        recv_sem=sems_e.at[slot],
        device_id=(region, 0),
        device_id_type=MESH,
    )

    sends_share = jnp.logical_and(event > 0, jnp.logical_not(mate)) if pair_up else event > 0

    @pl.when(sends_share)
    def _():
        copy_e.start()

    for c in range(3):
        for l in range(4):
            change = pre[l, c] + float(numbers[4, l]) * beyond[c]
            g[l, c] = -time_step * (imc[l] * change)
    force = open_face(g, muc, lamc, face_means(g))
    last, _ = last_plane(un[0], *second_grads)
    copy_q.wait_recv()
    coming = unpack_half(recv_q[...], 15).reshape(3, 5, 8, lanes)
    fc[0] = last + force + turn(coming, 4)
    stresses(un)
    gather_forces(4, 0, 1, 2, 3)
    advance(un, un, 0, f[0] + join(fc[0], turn(f[4], 4)))
    for place in (1, 2, 3):
        advance(un, un, place, f[place])

    def give(state, forward_out, adjoint_out):
        for c in range(3):
            four = swap_rows((state[0, c], state[1, c], state[2, c], state[3, c]))
            forward_out[c] = jnp.concatenate([four[0][0:4], four[1]], axis=0)
            adjoint_out[c] = jnp.concatenate([four[2][0:4], four[3]], axis=0)

    give(un, uf_out, ua_out)
    give(b, vf_out, va_out)

    def first_share(value):
        nothing = jnp.zeros_like(value)
        parts = swap_rows((jnp.where(low4, value, 0.0), nothing, nothing, nothing))
        return [
            jnp.concatenate([parts[2 * kind][0:4], parts[2 * kind + 1]], axis=0)[:, 0:planes]
            for kind in range(2)
        ]

    own = first_share(unpack_half(send_e[...], 5))
    total = send_k[event]
    for kind in range(2):
        k_out[kind] = total[kind] + jnp.where(event == 0, own[kind], 0.0)

    def take_kernels():
        for offset in range(1, events):
            copies[offset - 1].wait_recv()
            k_out[...] = k_out[...] + recv_k[offset - 1]

    unless(lead, take_kernels)

    def partner_kernels():
        other = unpack_half(recv_x[...], 15).reshape(3, 5, 8, lanes)
        add_plane(other)
        copy_pd.wait_recv()
        packed = recv_pd[...].reshape(3, 5, 8, lanes)
        grads_one = plane_grads(other, gy_two[0], packed)
        last, face = last_plane(other, *grads_one)
        for c in range(3):
            force = last[c] + turn(packed[c], 4)
            u_two[0, c] = u_two[0, c] - time_step * (im[0] * force)
        rows = slope_rows(rows_of(u_two[0]), 2 * lanes)
        gy_two[0] = rows.reshape(3, 5, 8, 2 * lanes)
        copy_w.wait_recv()
        u_two[4] = unpack_half(recv_w[...], 15).reshape(3, 5, 8, lanes)
        copy_z.wait_recv()
        kacc[0:4] = unpack_half(recv_z[...], 20).reshape(4, 5, 8, lanes)
        kinds(u_two, 1, gy_two, 4)
        weight = 0.1 * element_weight
        share = kinds_of(weight, *grads_one)
        first = middle_sum(kacc[0] + share)
        nodes = swap_rows((first, *[middle_sum(kacc[i]) for i in (1, 2, 3)]))
        for kind in range(2):
            whole = jnp.concatenate([nodes[2 * kind][0:4], nodes[2 * kind + 1]], axis=0)
            k_out[kind] = k_out[kind] + whole[:, 0:planes]
        copy_dd.wait_recv()
        coming = unpack_half(recv_dd[...], 15).reshape(3, 5, 8, lanes)
        slope = [fc[4, c] + ends * middle_sum(face[c]) + turn(coming[c], 4) for c in range(3)]
        grads_two = plane_grads(u_two[0], gy_two[0], slope)
        parts = first_share(middle_sum(kinds_of(weight, *grads_two)))
        for kind in range(2):
            k_out[kind] = k_out[kind] + parts[kind]

    only(lead, partner_kernels)

    takes_share = jnp.logical_and(event == 0, jnp.logical_not(lead)) if pair_up else event == 0

    @pl.when(takes_share)
    def _():
        extra = None
        for other in range(events - 1):
            pltpu.make_async_copy(recv_e.at[other], recv_e.at[other], sems_e.at[other]).wait()
            share = unpack_half(recv_e[other], 5)
            extra = share if extra is None else extra + share
        parts = first_share(extra)
        for kind in range(2):
            k_out[kind] = k_out[kind] + parts[kind]

    @pl.when(sends_share)
    def _():
        copy_e.wait_send()

    for copy in [copy_a, copy_b, copy_m, copy_p, copy_d, copy_q]:
        copy.wait_send()

    def close_copies():
        for copy in copies:
            copy.wait_send()

    def close_mate():
        for copy in (copy_x, copy_y, copy_w, copy_z):
            copy.wait_send()

    def close_giver():
        for copy in (copy_pd, copy_dd):
            copy.wait_send()

    unless(mate, close_copies)
    only(mate, close_mate)
    only(giver, close_giver)


def flush(*refs):
    sources, outs, sems = refs[:5], refs[5:10], refs[10]
    stores = [pltpu.make_async_copy(sources[n], outs[n], sems.at[n]) for n in range(5)]
    for store in stores:
        store.start()
    for store in stores:
        store.wait()


def run(regions, events, interpret, *arrays):
    lanes = arrays[0].shape[-1]
    fields = [jnp.transpose(array[0], (0, 2, 1, 3)) for array in arrays[:5]]
    models = [jnp.transpose(array, (1, 0, 2)) for array in arrays[5:]]
    tables = [jnp.asarray(table) for table in lane_tables(lanes)]
    operands = [*fields, *models, *tables]
    operands = [pltpu.with_memory_space_constraint(array, pltpu.HBM) for array in operands]
    planes = 8 // events
    state = jax.ShapeDtypeStruct((3, 9, 8, lanes), jnp.float32)
    f32 = jnp.float32
    vector = pltpu.VMEM((5, 3, 5, 8, lanes), f32)
    wide = pltpu.VMEM((5, 3, 5, 8, 2 * lanes), f32)
    scalar = pltpu.VMEM((5, 5, 8, lanes), f32)

    def packed(*lead):
        return pltpu.VMEM(lead + (8, lanes), f32)

    outs = pl.pallas_call(
        functools.partial(kernel, regions, events),
        out_shape=[state] * 4 + [jax.ShapeDtypeStruct((2, 9, planes, lanes), f32)],
        in_specs=[pl.BlockSpec(memory_space=pltpu.HBM)] * 11,
        out_specs=[pl.BlockSpec(memory_space=pltpu.VMEM)] * 5,
        scratch_shapes=[
            vector,
            vector,
            vector,
            vector,
            vector,
            scalar,
            scalar,
            scalar,
            wide,
            vector,
            wide,
            vector,
            vector,
            packed(3, 5),
            vector,
            scalar,
            scalar,
            scalar,
            scalar,
            scalar,
            scalar,
            packed(10),
            packed(10),
            packed(10),
            packed(10),
            packed(14),
            packed(14),
            packed(15),
            packed(15),
            packed(8),
            packed(8),
            packed(8),
            packed(8),
            packed(3),
            packed(max(events - 1, 1), 3),
            packed(8),
            packed(8),
            packed(30),
            packed(30),
            packed(8),
            packed(8),
            packed(10),
            packed(10),
            packed(15),
            packed(8),
            vector,
            wide,
            pltpu.SemaphoreType.DMA((2, 6)),
            pltpu.SemaphoreType.REGULAR,
            pltpu.VMEM((events, 2, 9, planes, lanes), f32),
            pltpu.VMEM((max(events - 1, 1), 2, 9, planes, lanes), f32),
            pltpu.SemaphoreType.DMA((2, 6)),
            pltpu.SemaphoreType.DMA((2, max(events - 1, 1))),
            pltpu.SemaphoreType.DMA((events,)),
            *[pltpu.VMEM(array.shape, array.dtype) for array in operands],
            pltpu.SemaphoreType.DMA((len(operands),)),
        ],
        compiler_params=pltpu.CompilerParams(
            collective_id=0, has_side_effects=True, vmem_limit_bytes=40 * 1024 * 1024
        ),
        name="adjoint_steps",
    )(*operands)
    shapes = [jax.ShapeDtypeStruct(out.shape, out.dtype) for out in outs]
    outs = pl.pallas_call(
        flush,
        out_shape=shapes,
        in_specs=[pl.BlockSpec(memory_space=pltpu.VMEM)] * 5,
        out_specs=[pl.BlockSpec(memory_space=pltpu.HBM)] * 5,
        scratch_shapes=[pltpu.SemaphoreType.DMA((5,))],
        compiler_params=pltpu.CompilerParams(vmem_limit_bytes=16 * 1024 * 1024),
        name="write_out",
    )(*outs)
    forward, forward_rate, adjoint, adjoint_rate = [
        jnp.transpose(out, (0, 2, 1, 3))[None] for out in outs[:4]
    ]
    return (forward, forward_rate, adjoint, adjoint_rate, jnp.transpose(outs[4], (0, 2, 1, 3)))


def solution(mesh):
    field = P("event", None, "region", None, None)
    model = P("region", None, None)
    regions, events = mesh.shape["region"], mesh.shape["event"]
    return jax.shard_map(
        functools.partial(run, regions, events, False),
        mesh=mesh,
        in_specs=(field,) * 5 + (model,) * 3,
        out_specs=(field,) * 4 + (P(None, ("region", "event"), None, None),),
        check_vma=False,
    )
```
